512 devices in a mesh: prow: 16 (over y, core), pcol: 32 (over z, x).
Axes of the slice: x: 4, y: 8, z: 8, core: 2. Of those that a mesh axis runs over, the one named last changes fastest.
Arguments:
- right_side: float32 [6, 512, 2048], P(None, 'pcol', 'prow'), may hold values from -6 to 6
- coupling: float32 [2048, 2048], P('prow', 'pcol'), may hold values from -0.125 to 0.125
- row_bases: float32 [2048, 512], P('prow'), may hold values from -1 to 1, as said below
- row_values: float32 [4, 512], replicated, may hold values from 0.5 to 4
- column_bases: float32 [6, 512, 512], P(None, 'pcol'), may hold values from -1 to 1, as said below
- column_values: float32 [6, 512], replicated, may hold values from 0.5 to 4
- column_coupling: float32 [6, 512, 3072], P(None, 'pcol'), may hold values from -0.109375 to 0.109375
Outputs:
- solution: float32 [6, 512, 2048], P(None, 'pcol', 'prow')
The draws below stay inside these ranges and needn't reach their ends.
Inputs may be any that keep to these rules, and one draw needn't show every extreme that they name: Each 512 x 512 block of row_bases is an orthogonal matrix. Each column_bases[j] is an orthogonal matrix.
All inputs are finite; a program needn't handle non-finite values.
Results may differ from the reference program's by a relative error of at most 0.00014.
Values sent between devices are 32-bit elements; how exact they have to be, the bound alone decides.
A program may use at most 64 MiB of HBM per device.

```python
import math
import jax
import jax.numpy as jnp
from jax import lax

BS = 512
RB = 4
CB = 6
ROWS = 2048
COLS = 3072


def orthogonal_stack(key, count, order):
    normal_entries = jax.random.normal(key, (count, order, order), jnp.float32)
    skew_part = (normal_entries - jnp.swapaxes(normal_entries, 1, 2)) * (0.7 / math.sqrt(order)) / 16.0
    identity = jnp.broadcast_to(jnp.eye(order, dtype=jnp.float32), (count, order, order))
    series_term = identity
    series_total = identity
    for power in range(1, 11):
        series_term = jnp.einsum('nab,nbc->nac', series_term, skew_part, precision=lax.Precision.HIGHEST) / power
        series_total = series_total + series_term
    for square_step in range(4):
        series_total = jnp.einsum('nab,nbc->nac', series_total, series_total, precision=lax.Precision.HIGHEST)
    return series_total


def draw_row_bases(key, part):
    return orthogonal_stack(jax.random.fold_in(key, 11), RB, BS).reshape(ROWS, BS)


def draw_column_bases(key, part):
    return orthogonal_stack(jax.random.fold_in(key, 23), CB, BS)


def block_scale(stream_key, extent, shards, least, top_value):
    def one(axis_at, shards_of):
        draws = jax.random.uniform(jax.random.fold_in(jax.random.fold_in(stream_key, 6), axis_at), (shards_of,), jnp.float32, least / len(shards), top_value / len(shards))
        return jnp.repeat(jnp.exp(draws), extent[axis_at] // shards_of).reshape((-1,) + (1,) * (len(extent) - axis_at - 1))

    level = one(*shards[0])
    for cut in shards[1:]:
        level = level * one(*cut)
    return level


def noise(rng, shape, spread, reach, pieces=(), kind=jnp.bfloat16):
    level = block_scale(rng, shape, pieces, -0.22, 0.18) if pieces else 1.0
    values = jax.random.normal(rng, shape, jnp.float32) * spread * level
    return jnp.minimum(jnp.maximum(values, -reach), reach).astype(kind)


def setup_inputs(seed: int = 0) -> dict:
    seeds = jax.random.split(jax.random.key(seed), 8)
    right_side = noise(seeds[0], (CB, BS, ROWS), 1.0, 6.0, ((1, 32), (2, 16)), jnp.float32)
    coupling = noise(seeds[1], (ROWS, ROWS), ROWS ** -0.5, 0.125, ((0, 16), (1, 32)), jnp.float32)
    row_bases = draw_row_bases(jax.random.fold_in(seeds[7], 71), 0)
    row_values = jnp.clip(jnp.exp(jax.random.uniform(seeds[3], (RB, BS), jnp.float32, math.log(0.5), math.log(4.0))), 0.5, 4.0)
    column_bases = draw_column_bases(jax.random.fold_in(seeds[7], 71), 0)
    column_values = jnp.clip(jnp.exp(jax.random.uniform(seeds[5], (CB, BS), jnp.float32, math.log(0.5), math.log(4.0))), 0.5, 4.0)
    column_coupling = noise(seeds[6], (CB, BS, COLS), COLS ** -0.5, 0.109375, ((1, 32),), jnp.float32)
    return {"right_side": right_side, "coupling": coupling, "row_bases": row_bases, "row_values": row_values, "column_bases": column_bases, "column_values": column_values, "column_coupling": column_coupling}


HIGHEST = lax.Precision.HIGHEST


def product(left, right):
    return jnp.dot(left, right, precision=HIGHEST, preferred_element_type=jnp.float32)


def reference(right_side, coupling, row_bases, row_values, column_bases, column_values, column_coupling):
    rhs_full = right_side.reshape(COLS, ROWS).T
    b_full = column_coupling.reshape(COLS, COLS).T
    answer = jnp.zeros((ROWS, COLS), jnp.float32)
    for block_column in range(CB):
        for block_row in reversed(range(RB)):
            row_start = block_row * BS
            row_end = row_start + BS
            col_start = block_column * BS
            col_end = col_start + BS
            residual = rhs_full[row_start:row_end, col_start:col_end]
            residual = residual - product(coupling[row_start:row_end, row_end:], answer[row_end:, col_start:col_end])
            residual = residual - product(answer[row_start:row_end, :col_start], b_full[:col_start, col_start:col_end])
            left_basis = row_bases[row_start:row_end]
            right_basis = column_bases[block_column]
            sums = row_values[block_row][:, None] + column_values[block_column][None, :]
            eigen_mix = product(product(left_basis.T, residual), right_basis) / sums
            solved = product(product(left_basis, eigen_mix), right_basis.T)
            answer = answer.at[row_start:row_end, col_start:col_end].set(solved)
    return answer.T.reshape(CB, BS, ROWS)
```

```python
import functools

import jax
import jax.numpy as jnp
from jax import lax
from jax.experimental import pallas as pl
from jax.experimental.pallas import tpu as pltpu
from jax.sharding import PartitionSpec as P

RB = 4
CB = 6
HIGHEST = lax.Precision.HIGHEST
MESH = pl.DeviceIdType.MESH
F32 = jnp.float32
BF16 = jnp.bfloat16


def halves(value):
    high = value.astype(BF16)
    low = (value - high.astype(F32)).astype(BF16)
    return high, low


def dot_of(left, right, dims):
    return lax.dot_general(left, right, (dims, ((), ())), preferred_element_type=F32)


def dot_split(left, right, dims):
    (left_high, left_low), (right_high, right_low) = left, right
    small = dot_of(left_low, right_high, dims) + dot_of(left_high, right_low, dims)
    return dot_of(left_high, right_high, dims) + small


def waves(
    np_, nq, cw, at, lhs, den, bases, out, yown, wown, yrow, ycol, wbuf, pend, acc, sems
):
    ns = nq // RB
    fw, ew = cw.shape[1], cw.shape[2]
    bs = fw * np_
    q = lax.axis_index("prow")
    p = lax.axis_index("pcol")
    i = q // ns
    s = q % ns
    row_send, row_recv, col_send, col_recv, w_send, w_recv = (sems.at[n] for n in range(6))

    barrier = pltpu.get_barrier_semaphore()

    @pl.loop(1, np_)
    def _(d):
        pl.semaphore_signal(barrier, inc=1, device_id=(q, (p + d) % np_), device_id_type=MESH)

    @pl.loop(1, nq)
    def _(d):
        pl.semaphore_signal(barrier, inc=1, device_id=((q + d) % nq, p), device_id_type=MESH)

    pl.semaphore_wait(barrier, np_ + nq - 2)

    pend[...] = cw[...]
    own_rows = pl.ds(pl.multiple_of(p * fw, fw), fw)
    own_lanes = pl.ds(pl.multiple_of(s * ew, ew), ew)

    for j in range(CB):
        acc[...] = pend[j]
        for k in range(1, RB):

            @pl.when(k > i)
            def _(k=k):
                pltpu.make_async_copy(
                    ycol.at[k - 1, j], ycol.at[k - 1, j], col_recv.at[(k - 1) * CB + j]
                ).wait()
                term = dot_split(
                    halves(ycol[k - 1, j]), halves(at[(k - 1) * bs : k * bs]), ((1,), (0,))
                )
                acc[...] -= term

        yown[j] = acc[...] / den[j]
        yrow[j, own_rows, :] = yown[j]

        @pl.loop(1, np_)
        def _(d):
            pltpu.make_async_remote_copy(
                src_ref=yown.at[j],
                dst_ref=yrow.at[j, own_rows],
                send_sem=row_send.at[j],
                recv_sem=row_recv.at[j],
                device_id=(q, (p + d) % np_),
                device_id_type=MESH,
            ).start()

        for k in range(1, RB):

            @pl.when(i == k)
            def _(k=k):
                @pl.loop(0, k * ns)
                def _(target):
                    pltpu.make_async_remote_copy(
                        src_ref=yown.at[j],
                        dst_ref=ycol.at[k - 1, j, :, own_lanes],
                        send_sem=col_send.at[j],
                        recv_sem=col_recv.at[(k - 1) * CB + j],
                        device_id=(target, p),
                        device_id_type=MESH,
                    ).start()

        arrived = yrow.at[j, pl.ds(0, bs - fw)]
        pltpu.make_async_copy(arrived, arrived, row_recv.at[j]).wait()
        rows = (CB - j) * fw
        both = dot_split(halves(lhs[j, :rows]), halves(yrow[j]), ((1,), (0,)))
        wown[j] = both[:fw]
        for later in range(j + 1, CB):
            at_row = (later - j) * fw
            pend[later] -= both[at_row : at_row + fw]
        wbuf[j, :, own_lanes] = wown[j]

        @pl.loop(1, ns)
        def _(d):
            pltpu.make_async_remote_copy(
                src_ref=wown.at[j],
                dst_ref=wbuf.at[j, :, own_lanes],
                send_sem=w_send.at[j],
                recv_sem=w_recv.at[j],
                device_id=(i * ns + (s + d) % ns, p),
                device_id_type=MESH,
            ).start()

    bases_split = halves(bases[...])
    for j in range(CB):
        part = wbuf.at[j, :, pl.ds(0, (ns - 1) * ew)]
        pltpu.make_async_copy(part, part, w_recv.at[j]).wait()
        out[j] = dot_split(halves(wbuf[j]), bases_split, ((1,), (1,)))

    for j in range(CB):
        arrived = yrow.at[j, pl.ds(0, bs - fw)]
        pltpu.make_async_copy(arrived, arrived, row_send.at[j]).wait()
        part = wbuf.at[j, :, pl.ds(0, (ns - 1) * ew)]
        pltpu.make_async_copy(part, part, w_send.at[j]).wait()
        for k in range(1, RB):

            @pl.when(i == k)
            def _(k=k):
                sent = yrow.at[j, pl.ds(0, fw * k * ns)]
                pltpu.make_async_copy(sent, sent, col_send.at[j]).wait()


def run_waves(np_, nq, cw, at, lhs, den, bases):
    fw, ew = cw.shape[1], cw.shape[2]
    bs = fw * np_
    vmem = pl.BlockSpec(memory_space=pltpu.VMEM)
    return pl.pallas_call(
        functools.partial(waves, np_, nq),
        out_shape=jax.ShapeDtypeStruct((CB, fw, ew), F32),
        in_specs=[vmem] * 5,
        out_specs=vmem,
        scratch_shapes=[
            pltpu.VMEM((CB, fw, ew), F32),
            pltpu.VMEM((CB, fw, ew), F32),
            pltpu.VMEM((CB, bs, ew), F32),
            pltpu.VMEM((RB - 1, CB, fw, bs), F32),
            pltpu.VMEM((CB, fw, bs), F32),
            pltpu.VMEM((CB, fw, ew), F32),
            pltpu.VMEM((fw, ew), F32),
            pltpu.SemaphoreType.DMA((6, (RB - 1) * CB)),
        ],
        compiler_params=pltpu.CompilerParams(collective_id=0, has_side_effects=True),
    )(cw, at, lhs, den, bases)


def take(array, index):
    return lax.dynamic_index_in_dim(array, index, 0, keepdims=False)


def product(spec, left, right):
    return jnp.einsum(spec, left, right, precision=HIGHEST, preferred_element_type=F32)


def shards(np_, nq, right_side, coupling, row_bases, row_values, column_bases, column_values, column_coupling):
    ns = nq // RB
    fw, ew = right_side.shape[1], right_side.shape[2]
    bs = row_bases.shape[1]
    q = lax.axis_index("prow")
    p = lax.axis_index("pcol")
    i, s = q // ns, q % ns
    groups = [[g * ns + m for m in range(ns)] for g in range(RB)]
    cw_width = coupling.shape[1]
    nw = bs // cw_width
    blocks = [[g * nw + m for m in range(nw)] for g in range(np_ // nw)]

    half = product("jbr,re->jbe", right_side, row_bases)
    half = lax.psum_scatter(half, "prow", scatter_dimension=2, axis_index_groups=groups, tiled=True)
    full = product("jbf,jbe->jfe", column_bases, half)
    cw = lax.psum_scatter(full, "pcol", scatter_dimension=1, tiled=True)

    inner = product("rc,re->ce", coupling, row_bases)
    inner = lax.psum_scatter(inner, "prow", scatter_dimension=1, axis_index_groups=groups, tiled=True)
    per_row = ew // cw_width
    piece = lax.dynamic_slice_in_dim(row_bases, (p % per_row) * cw_width, cw_width, 0)
    piece = lax.psum(jnp.where(q == p // per_row, piece, 0.0), "prow")
    outer = product("ce,cg->eg", piece, inner)
    outer = lax.psum_scatter(outer, "pcol", scatter_dimension=0, axis_index_groups=blocks, tiled=True)
    at = lax.all_gather(outer, "pcol", axis=0, tiled=True)[bs:]

    pairs = [(l, j) for j in range(1, CB) for l in range(j)]
    of_l = jnp.array([l for l, j in pairs] + [0], jnp.int32)
    of_j = jnp.array([j for l, j in pairs] + [0], jnp.int32)
    l_at, j_at = of_l[q], of_j[q]
    basis = lax.all_gather(take(column_bases, l_at), "pcol", axis=0, tiled=True)
    mine = lax.dynamic_slice_in_dim(take(column_coupling, j_at), l_at * bs, bs, 1)
    mixed = product("bt,tf->bf", mine, basis)
    mixed = product("bg,bf->gf", take(column_bases, j_at), mixed)
    mixed = lax.psum_scatter(mixed, "pcol", scatter_dimension=0, tiled=True)
    mixed = lax.all_gather(mixed, "prow", axis=0)
    lhs = []
    for l in range(CB):
        rows = [column_bases[l]] + [mixed[pairs.index((l, j))] for j in range(l + 1, CB)]
        rows += [jnp.zeros((l * fw, bs), F32)] if l else []
        lhs.append(jnp.concatenate(rows, 0))
    lhs = jnp.stack(lhs)

    own_values = lax.dynamic_slice(row_values, (i, s * ew), (1, ew))
    own_shifts = lax.dynamic_slice_in_dim(column_values, p * fw, fw, 1)
    den = own_shifts[:, :, None] + own_values[:, None, :]
    return run_waves(np_, nq, cw, at, lhs, den, row_bases)


def solution(mesh):
    placed = (
        P(None, "pcol", "prow"),
        P("prow", "pcol"),
        P("prow", None),
        P(),
        P(None, "pcol", None),
        P(),
        P(None, "pcol", None),
    )
    body = functools.partial(shards, mesh.shape["pcol"], mesh.shape["prow"])
    return jax.shard_map(
        body, mesh=mesh, in_specs=placed, out_specs=P(None, "pcol", "prow"), check_vma=False
    )
```

```python
import functools

import jax
import jax.numpy as jnp
from jax import lax
from jax.experimental import pallas as pl
from jax.experimental.pallas import tpu as pltpu
from jax.sharding import PartitionSpec as P

RB = 4
CB = 6
PAIRS = CB * (CB - 1) // 2
MESH = pl.DeviceIdType.MESH
F32 = jnp.float32
BF16 = jnp.bfloat16
ROW_BY_COL = ((1,), (0,))
COL_BY_COL = ((0,), (0,))
ROW_BY_ROW = ((1,), (1,))


def halves(value):
    high = value.astype(BF16)
    low = (value - high.astype(F32)).astype(BF16)
    return high, low


def dot_of(left, right, dims):
    return lax.dot_general(left, right, (dims, ((), ())), preferred_element_type=F32)


def dot_split(left, right, dims):
    (left_high, left_low), (right_high, right_low) = left, right
    small = dot_of(left_low, right_high, dims) + dot_of(left_high, right_low, dims)
    return dot_of(left_high, right_high, dims) + small


def dot3(left, right, dims=ROW_BY_COL):
    return dot_split(halves(left), halves(right), dims)


def kernel(np_, nq, *refs):
    (rhs, coupling, bases, den, colbases, colcoup, out, *rest) = refs
    (upart, urecv, vpart, crecv, hpart, hrecv, pk, gpart, grecv, apiece, at) = rest[:11]
    (bx, qx, ql, tpart, trecv, tpiece, lhs) = rest[11:18]
    (yown, wown, yrow, ycol, wbuf, pend, acc, sems) = rest[18:]
    fw, ew = rhs.shape[1], rhs.shape[2]
    cww = coupling.shape[1]
    bs = fw * np_
    ns = nq // RB
    nx = bs // ew
    nz = np_ // nx
    zw = bs // nz
    nw = bs // cww
    per_row = ew // cww
    q = lax.axis_index("prow")
    p = lax.axis_index("pcol")
    i, s = q // ns, q % ns
    z, x = p // nx, p % nx
    k_own, w_own = p // nw, p % nw
    j_own = 1
    for first in range(2, CB):
        j_own = j_own + (q >= first * (first - 1) // 2).astype(jnp.int32)
    l_own = q - j_own * (j_own - 1) // 2
    has_pair = q < PAIRS
    has_coupling = k_own > i

    used = [0]

    def new_sem(count=1):
        at_sem = used[0]
        used[0] += count
        return [sems.at[at_sem + n] for n in range(count)]

    row_send, row_recv, col_send = new_sem(CB), new_sem(CB), new_sem(CB)
    col_recv = [new_sem(CB) for _ in range(RB - 1)]
    w_send, w_recv = new_sem(CB), new_sem(CB)
    c1_send, c1_recv, c2_send, c2_recv = new_sem(2), new_sem(2), new_sem(CB), new_sem(CB)
    (a1_send, a1_recv, a2_send, a2_recv, a3_send, a3_recv, a4_send) = new_sem(7)
    a4_recv = new_sem(RB - 1)
    (b1_send, b1_recv, q1_send, q1_recv, l1_send, l1_recv) = new_sem(6)
    (b2_send, b2_recv, b3_send) = new_sem(3)
    b3_recv = new_sem(CB - 1)

    def send(src, dst, send_sem, recv_sem, q_to, p_to):
        pltpu.make_async_remote_copy(
            src_ref=src,
            dst_ref=dst,
            send_sem=send_sem,
            recv_sem=recv_sem,
            device_id=(q_to, p_to),
            device_id_type=MESH,
        ).start()

    def keep(src, dst, recv_sem):
        pltpu.make_async_copy(src, dst, recv_sem).start()

    def wait(ref, sem):
        pltpu.make_async_copy(ref, ref, sem).wait()

    def rows_of(n, size):
        return pl.ds(pl.multiple_of(n * size, size), size)

    barrier = pltpu.get_barrier_semaphore()

    @pl.loop(1, np_)
    def _(d):
        pl.semaphore_signal(barrier, inc=1, device_id=(q, (p + d) % np_), device_id_type=MESH)

    @pl.loop(0, nq * nx)
    def _(t):
        q_to = t // nx

        @pl.when(q_to != q)
        def _():
            pl.semaphore_signal(
                barrier, inc=1, device_id=(q_to, z * nx + t % nx), device_id_type=MESH
            )

    bases_split = halves(bases[...])
    stacked = rhs[...].reshape(CB * fw, ew)
    first = dot_split(halves(stacked), bases_split, ROW_BY_COL)
    inner = dot_split(halves(coupling[...]), bases_split, COL_BY_COL)
    for n in range(ns):
        upart[n] = first[:, n * ew : (n + 1) * ew]
        hpart[n] = inner[:, n * ew : (n + 1) * ew]
    for l in range(CB):
        lhs[l, :fw] = colbases[l]

    pl.semaphore_wait(barrier, np_ - 1 + (nq - 1) * nx)

    chunks = (pl.ds(0, fw), pl.ds(fw, (CB - 1) * fw))

    def send_c1(c):
        @pl.loop(0, ns)
        def _(t):
            src, dst = upart.at[t, chunks[c]], urecv.at[s, chunks[c]]

            @pl.when(t == s)
            def _():
                keep(src, dst, c1_recv[c])

            @pl.when(t != s)
            def _():
                send(src, dst, c1_send[c], c1_recv[c], i * ns + t, p)

    send_c1(0)

    @pl.when(has_pair)
    def _():
        @pl.loop(0, np_)
        def _(t):
            src = colbases.at[l_own, :, rows_of(t % nx, ew)]
            dst = ql.at[rows_of(p, fw)]

            @pl.when(t == p)
            def _():
                keep(src, dst, l1_recv)

            @pl.when(t != p)
            def _():
                send(src, dst, l1_send, l1_recv, q, t)

        @pl.loop(0, nx)
        def _(t):
            src_b = colcoup.at[j_own, :, rows_of(l_own, bs)]
            src_q = colbases.at[j_own]
            dst_b, dst_q = bx.at[rows_of(x, fw)], qx.at[rows_of(x, fw)]

            @pl.when(t == x)
            def _():
                keep(src_b, dst_b, b1_recv)
                keep(src_q, dst_q, q1_recv)

            @pl.when(t != x)
            def _():
                send(src_b, dst_b, b1_send, b1_recv, q, z * nx + t)
                send(src_q, dst_q, q1_send, q1_recv, q, z * nx + t)

    @pl.when(has_coupling)
    def _():
        @pl.loop(0, ns)
        def _(t):
            @pl.when(t == s)
            def _():
                keep(hpart.at[t], hrecv.at[s], a1_recv)

            @pl.when(t != s)
            def _():
                send(hpart.at[t], hrecv.at[s], a1_send, a1_recv, i * ns + t, p)

    @pl.when(q == p // per_row)
    def _():
        @pl.loop(0, i * ns)
        def _(t):
            send(
                bases.at[rows_of(p % per_row, cww)],
                pk,
                a2_send,
                a2_recv,
                i * ns - 1 - t,
                p,
            )

    send_c1(1)

    def send_c2(j):
        @pl.loop(0, np_)
        def _(t):
            src, dst = vpart.at[j, rows_of(t, fw)], crecv.at[j, p]

            @pl.when(t == p)
            def _():
                keep(src, dst, c2_recv[j])

            @pl.when(t != p)
            def _():
                send(src, dst, c2_send[j], c2_recv[j], q, t)

    wait(urecv.at[:, chunks[0]], c1_recv[0])
    vpart[0] = dot3(colbases[0], jnp.sum(urecv[:, :fw], axis=0), COL_BY_COL)
    send_c2(0)

    @pl.when(has_pair)
    def _():
        wait(ql, l1_recv)
        wait(bx, b1_recv)
        wait(qx, q1_recv)
        mixed = dot3(bx[...], ql[...])
        tpart[...] = dot3(qx[...], mixed, COL_BY_COL)

        @pl.loop(0, nz)
        def _(t):
            src, dst = tpart.at[rows_of(t, zw)], trecv.at[z]

            @pl.when(t == z)
            def _():
                keep(src, dst, b2_recv)

            @pl.when(t != z)
            def _():
                send(src, dst, b2_send, b2_recv, q, t * nx + x)

    @pl.when(has_coupling)
    def _():
        wait(hrecv, a1_recv)
        wait(pk, a2_recv)
        gpart[...] = dot3(pk[...], jnp.sum(hrecv[...], axis=0), COL_BY_COL)

        @pl.loop(0, nw)
        def _(t):
            src, dst = gpart.at[rows_of(t, cww)], grecv.at[w_own]

            @pl.when(t == w_own)
            def _():
                keep(src, dst, a3_recv)

            @pl.when(t != w_own)
            def _():
                send(src, dst, a3_send, a3_recv, q, k_own * nw + t)

    wait(urecv.at[:, chunks[1]], c1_recv[1])
    for j in range(1, CB):
        left = jnp.sum(urecv[:, j * fw : (j + 1) * fw], axis=0)
        vpart[j] = dot3(colbases[j], left, COL_BY_COL)
    send_c2(1)

    own_rows = rows_of(p, fw)
    own_lanes = rows_of(s, ew)

    def sum_up(j):
        wait(crecv.at[j], c2_recv[j])
        pend[j] += jnp.sum(crecv[j], axis=0)

    def finish(j):
        yown[j] = acc[...] / den[j]
        yrow[j, own_rows, :] = yown[j]

        @pl.loop(1, np_)
        def _(d):
            send(
                yown.at[j],
                yrow.at[j, own_rows],
                row_send[j],
                row_recv[j],
                q,
                (p + d) % np_,
            )

        for k in range(1, RB):

            @pl.when(i == k)
            def _(k=k):
                @pl.loop(0, k * ns)
                def _(t):
                    send(
                        yown.at[j],
                        ycol.at[k - 1, j, :, own_lanes],
                        col_send[j],
                        col_recv[k - 1][j],
                        k * ns - 1 - t,
                        p,
                    )

    def left_terms(j):
        for k in range(1, RB):

            @pl.when(k > i)
            def _(k=k):
                if j == 0:
                    wait(at.at[k * bs : (k + 1) * bs], a4_recv[k - 1])
                wait(ycol.at[k - 1, j], col_recv[k - 1][j])
                acc[...] -= dot3(ycol[k - 1, j], at[k * bs : (k + 1) * bs])

    pend[...] = jnp.zeros_like(pend)
    sum_up(0)
    acc[...] = pend[0]

    @pl.when(i == RB - 1)
    def _():
        finish(0)

    @pl.when(has_pair)
    def _():
        wait(trecv, b2_recv)
        tpiece[...] = jnp.sum(trecv[...], axis=0)

        for l in range(CB - 1):

            @pl.when(l_own == l)
            def _(l=l):
                @pl.loop(0, nq * nx)
                def _(t):
                    q_to, x_to = t // nx, t % nx
                    src = tpiece.at[rows_of(x_to, fw)]
                    dst = lhs.at[l, rows_of(j_own - l, fw), rows_of(x, ew)]
                    here = jnp.logical_and(q_to == q, x_to == x)

                    @pl.when(here)
                    def _():
                        keep(src, dst, b3_recv[l])

                    @pl.when(jnp.logical_not(here))
                    def _():
                        send(src, dst, b3_send, b3_recv[l], q_to, z * nx + x_to)

    @pl.when(has_coupling)
    def _():
        wait(grecv, a3_recv)
        apiece[...] = jnp.sum(grecv[...], axis=0)
        for k in range(1, RB):

            @pl.when(k_own == k)
            def _(k=k):
                @pl.loop(0, np_)
                def _(t):
                    dst = at.at[rows_of(p, cww)]

                    @pl.when(t == p)
                    def _():
                        keep(apiece, dst, a4_recv[k - 1])

                    @pl.when(t != p)
                    def _():
                        send(apiece, dst, a4_send, a4_recv[k - 1], q, t)

    for j in range(CB):
        if j == 0:

            @pl.when(i < RB - 1)
            def _():
                left_terms(0)
                finish(0)

        else:
            sum_up(j)
            acc[...] = pend[j]
            left_terms(j)
            finish(j)
        if j + 2 < CB:
            send_c2(j + 2)

        wait(yrow.at[j, pl.ds(0, bs - fw)], row_recv[j])
        if j < CB - 1:
            wait(lhs.at[j, fw : (CB - j) * fw], b3_recv[j])
        both = dot3(lhs[j, : (CB - j) * fw], yrow[j])
        wown[j] = both[:fw]
        for later in range(j + 1, CB):
            at_row = (later - j) * fw
            pend[later] -= both[at_row : at_row + fw]
        wbuf[j, :, own_lanes] = wown[j]

        @pl.loop(1, ns)
        def _(d):
            send(
                wown.at[j],
                wbuf.at[j, :, own_lanes],
                w_send[j],
                w_recv[j],
                i * ns + (s + d) % ns,
                p,
            )

    for j in range(CB):
        wait(wbuf.at[j, :, pl.ds(0, (ns - 1) * ew)], w_recv[j])
        out[j] = dot_split(halves(wbuf[j]), halves(bases[...]), ROW_BY_ROW)

    for c in range(2):
        wait(urecv.at[pl.ds(0, ns - 1), chunks[c]], c1_send[c])
    for j in range(CB):
        wait(crecv.at[j, pl.ds(0, np_ - 1)], c2_send[j])
        wait(yrow.at[j, pl.ds(0, bs - fw)], row_send[j])
        wait(wbuf.at[j, :, pl.ds(0, (ns - 1) * ew)], w_send[j])
        for k in range(1, RB):

            @pl.when(i == k)
            def _(k=k):
                wait(yrow.at[j, pl.ds(0, fw * k * ns)], col_send[j])

    @pl.when(has_coupling)
    def _():
        wait(hrecv.at[pl.ds(0, ns - 1)], a1_send)
        wait(grecv.at[pl.ds(0, nw - 1)], a3_send)
        wait(at.at[pl.ds(0, (np_ - 1) * cww)], a4_send)

    for k in range(1, RB):

        @pl.when(jnp.logical_and(i == k, q == p // per_row))
        def _(k=k):
            wait(yrow.at[pl.ds(0, k * ns * cww // ew)], a2_send)

    @pl.when(has_pair)
    def _():
        wait(bx.at[pl.ds(0, (nx - 1) * fw)], b1_send)
        wait(qx.at[pl.ds(0, (nx - 1) * fw)], q1_send)
        wait(ql.at[pl.ds(0, bs - fw)], l1_send)
        wait(trecv.at[pl.ds(0, nz - 1)], b2_send)
        wait(at.at[pl.ds(0, (nq * nx - 1) * fw)], b3_send)


def shards(np_, nq, right_side, coupling, row_bases, row_values, column_bases, column_values, column_coupling):
    ns = nq // RB
    fw, ew = right_side.shape[1], right_side.shape[2]
    cww = coupling.shape[1]
    bs = row_bases.shape[1]
    nx = bs // ew
    nz = np_ // nx
    zw = bs // nz
    nw = bs // cww
    q = lax.axis_index("prow")
    p = lax.axis_index("pcol")
    i, s = q // ns, q % ns
    own_values = lax.dynamic_slice(row_values, (i, s * ew), (1, ew))
    own_shifts = lax.dynamic_slice_in_dim(column_values, p * fw, fw, 1)
    den = own_shifts[:, :, None] + own_values[:, None, :]
    vmem = pl.BlockSpec(memory_space=pltpu.VMEM)
    scratch = (
        (ns, CB * fw, ew),
        (ns, CB * fw, ew),
        (CB, bs, ew),
        (CB, np_, fw, ew),
        (ns, cww, ew),
        (ns, cww, ew),
        (cww, bs),
        (bs, ew),
        (nw, cww, ew),
        (cww, ew),
        (RB * bs, ew),
        (nx * fw, bs),
        (nx * fw, bs),
        (bs, ew),
        (bs, ew),
        (nz, zw, ew),
        (zw, ew),
        (CB, CB * fw, bs),
        (CB, fw, ew),
        (CB, fw, ew),
        (CB, bs, ew),
        (RB - 1, CB, fw, bs),
        (CB, fw, bs),
        (CB, fw, ew),
        (fw, ew),
    )
    return pl.pallas_call(
        functools.partial(kernel, np_, nq),
        out_shape=jax.ShapeDtypeStruct((CB, fw, ew), F32),
        in_specs=[vmem] * 6,
        out_specs=vmem,
        scratch_shapes=[pltpu.VMEM(shape, F32) for shape in scratch]
        + [pltpu.SemaphoreType.DMA((96,))],
        compiler_params=pltpu.CompilerParams(collective_id=0, has_side_effects=True),
    )(right_side, coupling, row_bases, den, column_bases, column_coupling)


def solution(mesh):
    placed = (
        P(None, "pcol", "prow"),
        P("prow", "pcol"),
        P("prow", None),
        P(),
        P(None, "pcol", None),
        P(),
        P(None, "pcol", None),
    )
    body = functools.partial(shards, mesh.shape["pcol"], mesh.shape["prow"])
    return jax.shard_map(
        body, mesh=mesh, in_specs=placed, out_specs=P(None, "pcol", "prow"), check_vma=False
    )
```

```python
import functools

import jax
import jax.numpy as jnp
from jax import lax
from jax.experimental import pallas as pl
from jax.experimental.pallas import tpu as pltpu
from jax.sharding import PartitionSpec as P

RB = 4
CB = 6
PAIRS = CB * (CB - 1) // 2
MESH = pl.DeviceIdType.MESH
F32 = jnp.float32
BF16 = jnp.bfloat16
ROW_BY_COL = ((1,), (0,))
COL_BY_COL = ((0,), (0,))
ROW_BY_ROW = ((1,), (1,))


def halves(value):
    high = value.astype(BF16)
    low = (value - high.astype(F32)).astype(BF16)
    return high, low


def dot_of(left, right, dims):
    return lax.dot_general(left, right, (dims, ((), ())), preferred_element_type=F32)


def dot_split(left, right, dims):
    (left_high, left_low), (right_high, right_low) = left, right
    small = dot_of(left_low, right_high, dims) + dot_of(left_high, right_low, dims)
    return dot_of(left_high, right_high, dims) + small


def dot3(left, right, dims=ROW_BY_COL):
    return dot_split(halves(left), halves(right), dims)


def kernel(np_, nq, *refs):
    (rhs, coupling, bases, row_values, colbases, col_values, colcoup, out, *rest) = refs
    (upart, urecv, ux, uown, qside, vpart, crecv) = rest[:7]
    (hpart, hrecv, pk, gpart, grecv, apiece, at) = rest[7:14]
    (bx, qx, ql, tpart, trecv, tpiece, lhs) = rest[14:21]
    (yown, wown, yrow, ycol, wbuf, pend, den, acc, sems) = rest[21:]
    fw, ew = rhs.shape[1], rhs.shape[2]
    cww = coupling.shape[0]
    bs = fw * np_
    ns = nq // RB
    nx = bs // ew
    nz = np_ // nx
    nw = bs // cww
    per_row = ew // cww
    q = lax.axis_index("prow")
    p = lax.axis_index("pcol")
    i, s = q // ns, q % ns
    z, x = p // nx, p % nx
    k_own, w_own = p // nw, p % nw
    pair = nq - 1 - q
    j_own = 1
    for first in range(2, CB):
        j_own = j_own + (pair >= first * (first - 1) // 2).astype(jnp.int32)
    l_own = pair - j_own * (j_own - 1) // 2
    has_pair = pair < PAIRS
    has_coupling = k_own > i

    used = [0]

    def new_sem(count=1):
        at_sem = used[0]
        used[0] += count
        return [sems.at[at_sem + n] for n in range(count)]

    row_send, row_recv, col_send = new_sem(CB), new_sem(CB), new_sem(CB)
    col_recv = [new_sem(CB) for _ in range(RB - 1)]
    w_send, w_recv = new_sem(CB), new_sem(CB)
    c1_send, c1_recv, c2_send, c2_recv = new_sem(2), new_sem(2), new_sem(2), new_sem(2)
    c3_send, c3_recv, q2_send, q2_recv = new_sem(2), new_sem(2), new_sem(2), new_sem(2)
    a1_send, a1_recv, a2_send, a2_recv, a2_pass, a3_send = new_sem(6)
    a3_recv, a4_send, a4_recv = new_sem(RB - 1), new_sem(RB - 1), new_sem(RB - 1)
    b1_send, b1_recv, q1_send, q1_recv, l1_send, l1_recv = new_sem(6)
    b2_send, b2_recv, b3_send = new_sem(3)
    b3_recv = new_sem(CB - 1)

    def send(src, dst, send_sem, recv_sem, q_to, p_to):
        pltpu.make_async_remote_copy(
            src_ref=src,
            dst_ref=dst,
            send_sem=send_sem,
            recv_sem=recv_sem,
            device_id=(q_to, p_to),
            device_id_type=MESH,
        ).start()

    def send_or_keep(here, src, dst, send_sem, recv_sem, q_to, p_to):
        @pl.when(here)
        def _():
            pltpu.make_async_copy(src, dst, recv_sem).start()

        @pl.when(jnp.logical_not(here))
        def _():
            send(src, dst, send_sem, recv_sem, q_to, p_to)

    def wait(ref, sem, name="w"):
        pltpu.make_async_copy(ref, ref, sem).wait()

    def rows_of(n, size):
        return pl.ds(pl.multiple_of(n * size, size), size)

    def far_first(d):
        return (p + (d + np_ // 2 - 1) % (np_ - 1) + 1) % np_

    barrier = pltpu.get_barrier_semaphore()

    @pl.loop(0, np_ - 1)
    def _(d):
        pl.semaphore_signal(barrier, inc=1, device_id=(q, far_first(d)), device_id_type=MESH)

    @pl.loop(1, nq)
    def _(d):
        for x_to in range(nx):
            pl.semaphore_signal(
                barrier, inc=1, device_id=((q + d) % nq, z * nx + x_to), device_id_type=MESH
            )

    bases_split = halves(bases[...])
    stacked = rhs[...].reshape(CB * fw, ew)
    first = dot_split(halves(stacked), bases_split, ROW_BY_COL)
    inner = dot_split(halves(coupling[...]), bases_split, ROW_BY_COL)
    for n in range(ns):
        upart[n] = first[:, n * ew : (n + 1) * ew]
        hpart[n] = inner[:, n * ew : (n + 1) * ew]
    for l in range(CB):
        lhs[l, :fw] = colbases[l]
    own_lanes = rows_of(s, ew)
    values = row_values[:, own_lanes]
    own_value = lax.broadcasted_iota(jnp.int32, values.shape, 0) == i
    eigen = jnp.sum(jnp.where(own_value, values, 0.0), axis=0, keepdims=True)
    lanes = lax.broadcasted_iota(jnp.int32, (fw, ew), 1)
    chosen = lanes == z * fw + lax.broadcasted_iota(jnp.int32, (fw, ew), 0)
    for j in range(CB):
        shifts = col_values[pl.ds(j, 1), rows_of(x, ew)]
        shift = jnp.sum(jnp.where(chosen, shifts, 0.0), axis=1, keepdims=True)
        den[j] = shift + eigen

    pl.semaphore_wait(barrier, np_ - 1 + (nq - 1) * nx)

    chunks = (pl.ds(0, fw), pl.ds(fw, (CB - 1) * fw))
    blocks = (pl.ds(0, 1), pl.ds(1, CB - 1))

    def send_c1(c):
        @pl.loop(0, ns)
        def _(t):
            src, dst = upart.at[t, chunks[c]], urecv.at[s, chunks[c]]
            send_or_keep(t == s, src, dst, c1_send[c], c1_recv[c], i * ns + t, p)

    def send_q2(c):
        @pl.loop(0, nx)
        def _(t):
            src, dst = colbases.at[blocks[c], :, rows_of(t, ew)], qside.at[blocks[c], x]
            send_or_keep(t == x, src, dst, q2_send[c], q2_recv[c], q, z * nx + t)

    def send_c2(c):
        wait(urecv.at[:, chunks[c]], c1_recv[c], "c1_%d" % c)
        count = (1, CB - 1)[c]
        summed = jnp.sum(urecv[:, chunks[c]], axis=0)
        uown[blocks[c]] = summed.reshape(count, fw, ew)

        @pl.loop(0, nx)
        def _(t):
            src, dst = uown.at[blocks[c]], ux.at[blocks[c], x]
            send_or_keep(t == x, src, dst, c2_send[c], c2_recv[c], q, z * nx + t)

    def send_c3(c):
        wait(ux.at[blocks[c]], c2_recv[c], "c2_%d" % c)
        wait(qside.at[blocks[c]], q2_recv[c], "q2_%d" % c)
        for j in ((0,), tuple(range(1, CB)))[c]:
            left = qside[j].reshape(nx * fw, ew)
            right = ux[j].reshape(nx * fw, ew)
            vpart[j] = dot3(left, right, COL_BY_COL).reshape(nz, fw, ew)

        @pl.loop(0, nz)
        def _(t):
            src, dst = vpart.at[blocks[c], t], crecv.at[blocks[c], z]
            send_or_keep(t == z, src, dst, c3_send[c], c3_recv[c], q, t * nx + x)

    send_c1(0)
    send_q2(0)

    @pl.when(has_pair)
    def _():
        @pl.loop(0, nx)
        def _(t):
            src_b = colcoup.at[j_own, :, rows_of(l_own, bs)]
            src_q = colbases.at[j_own]
            dst_b, dst_q = bx.at[rows_of(x, fw)], qx.at[rows_of(x, fw)]
            send_or_keep(t == x, src_b, dst_b, b1_send, b1_recv, q, z * nx + t)
            send_or_keep(t == x, src_q, dst_q, q1_send, q1_recv, q, z * nx + t)

        dst = ql.at[rows_of(p, fw)]
        own = colbases.at[l_own, :, rows_of(x, ew)]
        pltpu.make_async_copy(own, dst, l1_recv).start()

        @pl.loop(0, np_ - 1)
        def _(d):
            to = far_first(d)
            src = colbases.at[l_own, :, rows_of(to % nx, ew)]
            send(src, dst, l1_send, l1_recv, q, to)

    core = q % 2
    partner = q + 1 - 2 * core
    piece = bases.at[rows_of(p % per_row, cww)]
    holder = p // per_row

    @pl.when(has_coupling)
    def _():
        @pl.loop(0, ns)
        def _(t):
            send_or_keep(t == s, hpart.at[t], hrecv.at[s], a1_send, a1_recv, i * ns + t, p)

    @pl.when(q == holder)
    def _():
        @pl.loop(0, i * ns // 2)
        def _(t):
            send(piece, pk, a2_send, a2_recv, i * ns - 2 - 2 * t + core, p)

    send_c2(0)

    @pl.when(has_coupling)
    def _():
        wait(hrecv, a1_recv, "a1")
        wait(pk, a2_recv, "a2")

        @pl.when(core == holder % 2)
        def _():
            send(pk, pk, a2_pass, a2_recv, partner, p)

        gpart[...] = dot3(pk[...], jnp.sum(hrecv[...], axis=0), COL_BY_COL)
        for k in range(1, RB):

            @pl.when(k_own == k)
            def _(k=k):
                dst = grecv.at[k - 1, w_own]
                pltpu.make_async_copy(gpart.at[rows_of(p, fw)], dst, a3_recv[k - 1]).start()

                @pl.loop(0, np_ - 1)
                def _(d):
                    to = far_first(d)
                    send(gpart.at[rows_of(to, fw)], dst, a3_send, a3_recv[k - 1], q, to)

    @pl.when(has_pair)
    def _():
        wait(bx, b1_recv, "bx")
        wait(qx, q1_recv, "qx")
        wait(ql, l1_recv, "ql")
        mixed = dot3(bx[...], ql[...])
        tpart[...] = dot3(qx[...], mixed, COL_BY_COL).reshape(nx, nz, fw, ew)

        @pl.loop(0, nz)
        def _(t):
            src, dst = tpart.at[:, t], trecv.at[z]
            send_or_keep(t == z, src, dst, b2_send, b2_recv, q, t * nx + x)

    send_c3(0)

    for k in range(RB - 1, 0, -1):

        @pl.when(k > i)
        def _(k=k):
            wait(grecv.at[k - 1], a3_recv[k - 1], "a3_%d" % k)
            apiece[k - 1] = jnp.sum(grecv[k - 1], axis=0)
            dst = at.at[k, rows_of(p, fw)]
            pltpu.make_async_copy(apiece.at[k - 1], dst, a4_recv[k - 1]).start()

            @pl.loop(0, np_ - 1)
            def _(d):
                send(apiece.at[k - 1], dst, a4_send[k - 1], a4_recv[k - 1], q, far_first(d))

    own_rows = rows_of(x * nz + z, fw)

    def finish(j):
        yown[j] = acc[...] / den[j]
        for k in range(1, RB):

            @pl.when(i == k)
            def _(k=k):
                @pl.loop(0, k * ns)
                def _(t):
                    send(
                        yown.at[j],
                        ycol.at[k - 1, j, :, own_lanes],
                        col_send[j],
                        col_recv[k - 1][j],
                        k * ns - 1 - t,
                        p,
                    )

        @pl.loop(0, np_ - 1)
        def _(d):
            dst = yrow.at[j, own_rows]
            send(yown.at[j], dst, row_send[j], row_recv[j], q, far_first(d))

        yrow[j, own_rows, :] = yown[j]

    def left_terms(j):
        for k in range(RB - 1, 0, -1):

            @pl.when(k > i)
            def _(k=k):
                if j == 0:
                    wait(at.at[k], a4_recv[k - 1], "a4_%d" % k)
                wait(ycol.at[k - 1, j], col_recv[k - 1][j], "col_%d_%d" % (k, j))
                acc[...] -= dot3(ycol[k - 1, j], at[k])

    def last_product(j):
        wait(wbuf.at[j, :, pl.ds(0, (ns - 1) * ew)], w_recv[j], "wx_%d" % j)
        out[j] = dot3(wbuf[j], bases[...], ROW_BY_ROW)

    wait(crecv.at[blocks[0]], c3_recv[0], "c3_0")
    acc[...] = jnp.sum(crecv[0], axis=0)

    @pl.when(i == RB - 1)
    def _():
        finish(0)

    @pl.when(has_pair)
    def _():
        wait(trecv, b2_recv, "b2")
        tpiece[...] = jnp.sum(trecv[...], axis=0)

        for l in range(CB - 1):

            @pl.when(l_own == l)
            def _(l=l):
                @pl.loop(0, nq * nx)
                def _(t):
                    q_to, x_to = nq - 1 - t // nx, t % nx
                    dst = lhs.at[l, rows_of(j_own - l, fw), rows_of(x, ew)]
                    here = jnp.logical_and(q_to == q, x_to == x)
                    to = z * nx + x_to
                    send_or_keep(here, tpiece.at[x_to], dst, b3_send, b3_recv[l], q_to, to)

    send_c1(1)
    send_q2(1)

    @pl.when(i < RB - 1)
    def _():
        left_terms(0)
        finish(0)

    send_c2(1)
    send_c3(1)
    wait(crecv.at[blocks[1]], c3_recv[1], "c3_1")
    for j in range(1, CB):
        pend[j] = jnp.sum(crecv[j], axis=0)

    for j in range(CB):
        if j > 0:
            acc[...] = pend[j]
            left_terms(j)
            finish(j)
            last_product(j - 1)

        wait(yrow.at[j, pl.ds(0, bs - fw)], row_recv[j], "row_%d" % j)
        if j < CB - 1:
            wait(lhs.at[j, fw : (CB - j) * fw], b3_recv[j], "b3_%d" % j)
        both = dot3(lhs[j, : (CB - j) * fw], yrow[j])
        wown[j] = both[:fw]
        for later in range(j + 1, CB):
            at_row = (later - j) * fw
            pend[later] -= both[at_row : at_row + fw]
        wbuf[j, :, own_lanes] = wown[j]

        @pl.loop(1, ns)
        def _(d):
            send(
                wown.at[j],
                wbuf.at[j, :, own_lanes],
                w_send[j],
                w_recv[j],
                i * ns + (s + d) % ns,
                p,
            )

    last_product(CB - 1)

    for c in range(2):
        wait(urecv.at[pl.ds(0, ns - 1), chunks[c]], c1_send[c])
        wait(ux.at[blocks[c], pl.ds(0, nx - 1)], c2_send[c])
        wait(qside.at[blocks[c], pl.ds(0, nx - 1)], q2_send[c])
        wait(crecv.at[blocks[c], pl.ds(0, nz - 1)], c3_send[c])
    for j in range(CB):
        wait(yrow.at[j, pl.ds(0, bs - fw)], row_send[j])
        wait(wbuf.at[j, :, pl.ds(0, (ns - 1) * ew)], w_send[j])
        for k in range(1, RB):

            @pl.when(i == k)
            def _(k=k):
                wait(yrow.at[j, pl.ds(0, fw * k * ns)], col_send[j])

    for k in range(1, RB):

        @pl.when(k > i)
        def _(k=k):
            wait(at.at[k, pl.ds(0, bs - fw)], a4_send[k - 1])

        @pl.when(jnp.logical_and(i == k, q == holder))
        def _(k=k):
            wait(yrow.at[pl.ds(0, k * ns * cww // (2 * ew))], a2_send)

    @pl.when(has_coupling)
    def _():
        wait(hrecv.at[pl.ds(0, ns - 1)], a1_send)
        wait(gpart.at[pl.ds(0, bs - fw)], a3_send)

        @pl.when(core == holder % 2)
        def _():
            wait(pk, a2_pass)

    @pl.when(has_pair)
    def _():
        wait(bx.at[pl.ds(0, (nx - 1) * fw)], b1_send)
        wait(qx.at[pl.ds(0, (nx - 1) * fw)], q1_send)
        wait(ql.at[pl.ds(0, bs - fw)], l1_send)
        wait(trecv.at[pl.ds(0, nz - 1)], b2_send)
        wait(yrow.at[pl.ds(0, 2), pl.ds(0, (nq * nx - 1) * fw // 2)], b3_send)


def shards(np_, nq, right_side, coupling, row_bases, row_values, column_bases, column_values, column_coupling):
    ns = nq // RB
    fw, ew = right_side.shape[1], right_side.shape[2]
    cww = coupling.shape[1]
    bs = row_bases.shape[1]
    nx = bs // ew
    nz = np_ // nx
    nw = bs // cww
    vmem = pl.BlockSpec(memory_space=pltpu.VMEM)
    scratch = (
        (ns, CB * fw, ew),
        (ns, CB * fw, ew),
        (CB, nx, fw, ew),
        (CB, fw, ew),
        (CB, nx, fw, ew),
        (CB, nz, fw, ew),
        (CB, nz, fw, ew),
        (ns, cww, ew),
        (ns, cww, ew),
        (cww, bs),
        (bs, ew),
        (RB - 1, nw, fw, ew),
        (RB - 1, fw, ew),
        (RB, bs, ew),
        (nx * fw, bs),
        (nx * fw, bs),
        (bs, ew),
        (nx, nz, fw, ew),
        (nz, nx, fw, ew),
        (nx, fw, ew),
        (CB, CB * fw, bs),
        (CB, fw, ew),
        (CB, fw, ew),
        (CB, bs, ew),
        (RB - 1, CB, fw, bs),
        (CB, fw, bs),
        (CB, fw, ew),
        (CB, fw, ew),
        (fw, ew),
    )
    return pl.pallas_call(
        functools.partial(kernel, np_, nq),
        out_shape=jax.ShapeDtypeStruct((CB, fw, ew), F32),
        in_specs=[vmem] * 7,
        out_specs=vmem,
        scratch_shapes=[pltpu.VMEM(shape, F32) for shape in scratch]
        + [pltpu.SemaphoreType.DMA((96,))],
        compiler_params=pltpu.CompilerParams(collective_id=0, has_side_effects=True),
    )(
        right_side,
        coupling.T,
        row_bases,
        row_values,
        column_bases,
        column_values,
        column_coupling,
    )


def solution(mesh):
    placed = (
        P(None, "pcol", "prow"),
        P("prow", "pcol"),
        P("prow", None),
        P(),
        P(None, "pcol", None),
        P(),
        P(None, "pcol", None),
    )
    body = functools.partial(shards, mesh.shape["pcol"], mesh.shape["prow"])
    return jax.shard_map(
        body, mesh=mesh, in_specs=placed, out_specs=P(None, "pcol", "prow"), check_vma=False
    )
```

```python
import functools

import jax
import jax.numpy as jnp
from jax import lax
from jax.experimental import pallas as pl
from jax.experimental.pallas import tpu as pltpu
from jax.sharding import PartitionSpec as P

RB = 4
CB = 6
PAIRS = CB * (CB - 1) // 2
MESH = pl.DeviceIdType.MESH
F32 = jnp.float32
BF16 = jnp.bfloat16
ROW_BY_COL = ((1,), (0,))
COL_BY_COL = ((0,), (0,))
ROW_BY_ROW = ((1,), (1,))


def halves(value):
    high = value.astype(BF16)
    low = (value - high.astype(F32)).astype(BF16)
    return high, low


def dot_of(left, right, dims):
    return lax.dot_general(left, right, (dims, ((), ())), preferred_element_type=F32)


def dot_split(left, right, dims):
    (left_high, left_low), (right_high, right_low) = left, right
    small = dot_of(left_low, right_high, dims) + dot_of(left_high, right_low, dims)
    return dot_of(left_high, right_high, dims) + small


def dot3(left, right, dims=ROW_BY_COL):
    return dot_split(halves(left), halves(right), dims)


def kernel(np_, nq, *refs):
    (rhs, coupling, bases, row_values, colbases, col_values, colcoup, out, *rest) = refs
    (upart, urecv, ux, uown, qside, vpart, crecv) = rest[:7]
    (hpart, hrecv, pk, gpart, grecv, apiece, at) = rest[7:14]
    (bx, qx, ql, tpart, trecv, tpiece, lhs) = rest[14:21]
    (yown, wown, yrow, ycol, wbuf, pend, den, acc, sems) = rest[21:]
    fw, ew = rhs.shape[1], rhs.shape[2]
    cww = coupling.shape[0]
    bs = fw * np_
    ns = nq // RB
    nx = bs // ew
    nz = np_ // nx
    nw = bs // cww
    per_row = ew // cww
    q = lax.axis_index("prow")
    p = lax.axis_index("pcol")
    i, s = q // ns, q % ns
    z, x = p // nx, p % nx
    k_own, w_own = p // nw, p % nw
    pair = nq - 1 - q
    j_own = 1
    for first in range(2, CB):
        j_own = j_own + (pair >= first * (first - 1) // 2).astype(jnp.int32)
    l_own = pair - j_own * (j_own - 1) // 2
    has_pair = pair < PAIRS
    has_coupling = k_own > i

    used = [0]

    def new_sem(count=1):
        at_sem = used[0]
        used[0] += count
        return [sems.at[at_sem + n] for n in range(count)]

    row_send, row_recv, col_send = new_sem(CB), new_sem(CB), new_sem(CB)
    col_recv = [new_sem(CB) for _ in range(RB - 1)]
    w_send, w_recv = new_sem(CB), new_sem(CB)
    c1_send, c1_recv, c2_send, c2_recv = new_sem(2), new_sem(2), new_sem(2), new_sem(2)
    c3_send, c3_recv, q2_send, q2_recv = new_sem(2), new_sem(2), new_sem(2), new_sem(2)
    a1_send, a1_recv, a2_send, a2_recv, a2_pass, a3_send = new_sem(6)
    a3_recv, a4_send, a4_recv = new_sem(RB - 1), new_sem(RB - 1), new_sem(RB - 1)
    b1_send, b1_recv, q1_send, q1_recv, l1_send, l1_recv = new_sem(6)
    b2_send, b2_recv, b3_send = new_sem(3)
    b3_pass = new_sem(PAIRS)
    b3_base = used[0]
    b3_recv = new_sem(PAIRS)

    def send(src, dst, send_sem, recv_sem, q_to, p_to):
        pltpu.make_async_remote_copy(
            src_ref=src,
            dst_ref=dst,
            send_sem=send_sem,
            recv_sem=recv_sem,
            device_id=(q_to, p_to),
            device_id_type=MESH,
        ).start()

    def send_or_keep(here, src, dst, send_sem, recv_sem, q_to, p_to):
        @pl.when(here)
        def _():
            pltpu.make_async_copy(src, dst, recv_sem).start()

        @pl.when(jnp.logical_not(here))
        def _():
            send(src, dst, send_sem, recv_sem, q_to, p_to)

    def wait(ref, sem, name="w"):
        pltpu.make_async_copy(ref, ref, sem).wait()

    def rows_of(n, size):
        return pl.ds(pl.multiple_of(n * size, size), size)

    def far_first(d):
        return (p + (d + np_ // 2 - 1) % (np_ - 1) + 1) % np_

    barrier = pltpu.get_barrier_semaphore()

    @pl.loop(0, np_ - 1)
    def _(d):
        pl.semaphore_signal(barrier, inc=1, device_id=(q, far_first(d)), device_id_type=MESH)

    @pl.loop(1, nq)
    def _(d):
        for x_to in range(nx):
            pl.semaphore_signal(
                barrier, inc=1, device_id=((q + d) % nq, z * nx + x_to), device_id_type=MESH
            )

    bases_split = halves(bases[...])
    stacked = rhs[...].reshape(CB * fw, ew)
    first = dot_split(halves(stacked), bases_split, ROW_BY_COL)
    inner = dot_split(halves(coupling[...]), bases_split, ROW_BY_COL)
    for n in range(ns):
        upart[n] = first[:, n * ew : (n + 1) * ew]
        hpart[n] = inner[:, n * ew : (n + 1) * ew]
    own_lanes = rows_of(s, ew)
    values = row_values[:, own_lanes]
    own_value = lax.broadcasted_iota(jnp.int32, values.shape, 0) == i
    eigen = jnp.sum(jnp.where(own_value, values, 0.0), axis=0, keepdims=True)
    lanes = lax.broadcasted_iota(jnp.int32, (fw, ew), 1)
    chosen = lanes == z * fw + lax.broadcasted_iota(jnp.int32, (fw, ew), 0)
    for j in range(CB):
        shifts = col_values[pl.ds(j, 1), rows_of(x, ew)]
        shift = jnp.sum(jnp.where(chosen, shifts, 0.0), axis=1, keepdims=True)
        den[j] = shift + eigen

    pl.semaphore_wait(barrier, np_ - 1 + (nq - 1) * nx)

    chunks = (pl.ds(0, fw), pl.ds(fw, (CB - 1) * fw))
    blocks = (pl.ds(0, 1), pl.ds(1, CB - 1))

    def send_c1(c):
        @pl.loop(0, ns)
        def _(t):
            src, dst = upart.at[t, chunks[c]], urecv.at[s, chunks[c]]
            send_or_keep(t == s, src, dst, c1_send[c], c1_recv[c], i * ns + t, p)

    def send_q2(c):
        @pl.loop(0, nx)
        def _(t):
            src, dst = colbases.at[blocks[c], :, rows_of(t, ew)], qside.at[blocks[c], x]
            send_or_keep(t == x, src, dst, q2_send[c], q2_recv[c], q, z * nx + t)

    def send_c2(c):
        wait(urecv.at[:, chunks[c]], c1_recv[c], "c1_%d" % c)
        count = (1, CB - 1)[c]
        summed = jnp.sum(urecv[:, chunks[c]], axis=0)
        uown[blocks[c]] = summed.reshape(count, fw, ew)

        @pl.loop(0, nx)
        def _(t):
            src, dst = uown.at[blocks[c]], ux.at[blocks[c], x]
            send_or_keep(t == x, src, dst, c2_send[c], c2_recv[c], q, z * nx + t)

    def send_c3(c):
        wait(ux.at[blocks[c]], c2_recv[c], "c2_%d" % c)
        wait(qside.at[blocks[c]], q2_recv[c], "q2_%d" % c)
        for j in ((0,), tuple(range(1, CB)))[c]:
            left = qside[j].reshape(nx * fw, ew)
            right = ux[j].reshape(nx * fw, ew)
            vpart[j] = dot3(left, right, COL_BY_COL).reshape(nz, fw, ew)

        @pl.loop(0, nz)
        def _(t):
            src, dst = vpart.at[blocks[c], t], crecv.at[blocks[c], z]
            send_or_keep(t == z, src, dst, c3_send[c], c3_recv[c], q, t * nx + x)

    core = q % 2
    partner = q + 1 - 2 * core
    piece = bases.at[rows_of(p % per_row, cww)]
    holder = p // per_row
    top = i == RB - 1
    early_pair = jnp.logical_and(has_pair, top)
    late_pair = jnp.logical_and(has_pair, i < RB - 1)

    def send_b1():
        @pl.loop(0, nx)
        def _(t):
            src_b = colcoup.at[j_own, :, rows_of(l_own, bs)]
            src_q = colbases.at[j_own]
            dst_b, dst_q = bx.at[rows_of(x, fw)], qx.at[rows_of(x, fw)]
            send_or_keep(t == x, src_b, dst_b, b1_send, b1_recv, q, z * nx + t)
            send_or_keep(t == x, src_q, dst_q, q1_send, q1_recv, q, z * nx + t)

        dst = ql.at[rows_of(p, fw)]
        own = colbases.at[l_own, :, rows_of(x, ew)]
        pltpu.make_async_copy(own, dst, l1_recv).start()

        @pl.loop(0, np_ - 1)
        def _(d):
            to = far_first(d)
            src = colbases.at[l_own, :, rows_of(to % nx, ew)]
            send(src, dst, l1_send, l1_recv, q, to)

    def send_b2():
        wait(bx, b1_recv, "bx")
        wait(qx, q1_recv, "qx")
        wait(ql, l1_recv, "ql")
        mixed = dot3(bx[...], ql[...])
        tpart[...] = dot3(qx[...], mixed, COL_BY_COL).reshape(nx, nz, fw, ew)

        @pl.loop(0, nz)
        def _(t):
            src, dst = tpart.at[:, t], trecv.at[z]
            send_or_keep(t == z, src, dst, b2_send, b2_recv, q, t * nx + x)

    @pl.when(q == holder)
    def _():
        @pl.loop(0, i * ns // 2)
        def _(t):
            send(piece, pk, a2_send, a2_recv, i * ns - 2 - 2 * t + core, p)

    @pl.when(has_coupling)
    def _():
        @pl.loop(0, ns)
        def _(t):
            send_or_keep(t == s, hpart.at[t], hrecv.at[s], a1_send, a1_recv, i * ns + t, p)

    send_c1(0)
    send_q2(0)
    pl.when(early_pair)(send_b1)
    send_c1(1)
    send_q2(1)

    @pl.when(has_coupling)
    def _():
        wait(hrecv, a1_recv, "a1")
        wait(pk, a2_recv, "a2")

        @pl.when(core == holder % 2)
        def _():
            send(pk, pk, a2_pass, a2_recv, partner, p)

        gpart[...] = dot3(pk[...], jnp.sum(hrecv[...], axis=0), COL_BY_COL)
        for k in range(1, RB):

            @pl.when(k_own == k)
            def _(k=k):
                dst = grecv.at[k - 1, w_own]
                pltpu.make_async_copy(gpart.at[rows_of(p, fw)], dst, a3_recv[k - 1]).start()

                @pl.loop(0, np_ - 1)
                def _(d):
                    to = far_first(d)
                    send(gpart.at[rows_of(to, fw)], dst, a3_send, a3_recv[k - 1], q, to)

    send_c2(0)

    @pl.when(top)
    def _():
        send_c3(0)

    pl.when(late_pair)(send_b1)
    pl.when(early_pair)(send_b2)
    send_c2(1)

    for k in range(RB - 1, 0, -1):

        @pl.when(k > i)
        def _(k=k):
            wait(grecv.at[k - 1], a3_recv[k - 1], "a3_%d" % k)
            apiece[k - 1] = jnp.sum(grecv[k - 1], axis=0)
            dst = at.at[k, rows_of(p, fw)]
            pltpu.make_async_copy(apiece.at[k - 1], dst, a4_recv[k - 1]).start()

            @pl.loop(0, np_ - 1)
            def _(d):
                send(apiece.at[k - 1], dst, a4_send[k - 1], a4_recv[k - 1], q, far_first(d))

    @pl.when(jnp.logical_not(top))
    def _():
        send_c3(0)

    send_c3(1)
    pl.when(late_pair)(send_b2)

    own_rows = rows_of(x * nz + z, fw)

    def finish(j):
        yown[j] = acc[...] / den[j]
        for k in range(1, RB):

            @pl.when(i == k)
            def _(k=k):
                @pl.loop(0, k * ns)
                def _(t):
                    send(
                        yown.at[j],
                        ycol.at[k - 1, j, :, own_lanes],
                        col_send[j],
                        col_recv[k - 1][j],
                        k * ns - 1 - t,
                        p,
                    )

        @pl.loop(0, np_ - 1)
        def _(d):
            dst = yrow.at[j, own_rows]
            send(yown.at[j], dst, row_send[j], row_recv[j], q, far_first(d))

        yrow[j, own_rows, :] = yown[j]

    def left_term(j, k, total):
        if j == 0:
            wait(at.at[k], a4_recv[k - 1], "a4_%d" % k)
        wait(ycol.at[k - 1, j], col_recv[k - 1][j], "col_%d_%d" % (k, j))
        total[...] -= dot3(ycol[k - 1, j], at[k])

    def older_left_terms(j, total):
        for k in range(RB - 1, 1, -1):
            pl.when(k > i + 1)(functools.partial(left_term, j, k, total))

    def newest_left_term(j, total):
        for k in range(1, RB):
            pl.when(k == i + 1)(functools.partial(left_term, j, k, total))

    def last_product(j):
        wait(wbuf.at[j, :, pl.ds(0, (ns - 1) * ew)], w_recv[j], "wx_%d" % j)
        out[j] = dot3(wbuf[j], bases[...], ROW_BY_ROW)

    def exchange(j):
        wown[j] = dot3(colbases[j], yrow[j])
        wbuf[j, :, own_lanes] = wown[j]

        @pl.loop(1, ns)
        def _(d):
            send(
                wown.at[j],
                wbuf.at[j, :, own_lanes],
                w_send[j],
                w_recv[j],
                i * ns + (s + d) % ns,
                p,
            )

    def pair_at(l, j):
        return j * (j - 1) // 2 + l

    def pass_pairs(j):
        for l in range(j):
            n = pair_at(l, j)
            wait(lhs.at[n], b3_recv[n], "b3_%d" % n)

            @pl.when(core == (nq - 1 - n) % 2)
            def _(n=n):
                send(lhs.at[n], lhs.at[n], b3_pass[n], b3_recv[n], partner, p)

    wait(crecv.at[blocks[0]], c3_recv[0], "c3_0")
    acc[...] = jnp.sum(crecv[0], axis=0)
    older_left_terms(0, acc)
    newest_left_term(0, acc)
    finish(0)

    @pl.when(has_pair)
    def _():
        wait(trecv, b2_recv, "b2")
        tpiece[...] = jnp.sum(trecv[...], axis=0)
        dst = lhs.at[pair, :, rows_of(x, ew)]
        recv_sem = sems.at[b3_base + pair]

        @pl.loop(0, nq // 2 * nx)
        def _(t):
            q_to, x_to = nq - 2 - t // nx * 2 + core, t % nx
            here = jnp.logical_and(q_to == q, x_to == x)
            to = z * nx + x_to
            send_or_keep(here, tpiece.at[x_to], dst, b3_send, recv_sem, q_to, to)

    wait(crecv.at[blocks[1]], c3_recv[1], "c3_1")
    for j in range(1, CB):
        pend[j] = jnp.sum(crecv[j], axis=0)

    for j in range(CB):
        if j == 0:
            pass_pairs(1)
        else:
            exchange(j - 1)
        if j + 2 < CB:
            pass_pairs(j + 2)
        if j + 1 < CB:
            for l in range(j):
                pend[j + 1] -= dot3(lhs[pair_at(l, j + 1)], yrow[l])
            older_left_terms(j + 1, pend.at[j + 1])
        if j > 1:
            last_product(j - 2)

        wait(yrow.at[j, pl.ds(0, bs - fw)], row_recv[j], "row_%d" % j)
        if j + 1 < CB:
            acc[...] = pend[j + 1] - dot3(lhs[pair_at(j, j + 1)], yrow[j])
            newest_left_term(j + 1, acc)
            finish(j + 1)

    exchange(CB - 1)
    last_product(CB - 2)
    last_product(CB - 1)

    for n in range(PAIRS):

        @pl.when(core == (nq - 1 - n) % 2)
        def _(n=n):
            wait(lhs.at[n], b3_pass[n])

    for c in range(2):
        wait(urecv.at[pl.ds(0, ns - 1), chunks[c]], c1_send[c])
        wait(ux.at[blocks[c], pl.ds(0, nx - 1)], c2_send[c])
        wait(qside.at[blocks[c], pl.ds(0, nx - 1)], q2_send[c])
        wait(crecv.at[blocks[c], pl.ds(0, nz - 1)], c3_send[c])
    for j in range(CB):
        wait(yrow.at[j, pl.ds(0, bs - fw)], row_send[j])
        wait(wbuf.at[j, :, pl.ds(0, (ns - 1) * ew)], w_send[j])
        for k in range(1, RB):

            @pl.when(i == k)
            def _(k=k):
                wait(yrow.at[j, pl.ds(0, fw * k * ns)], col_send[j])

    for k in range(1, RB):

        @pl.when(k > i)
        def _(k=k):
            wait(at.at[k, pl.ds(0, bs - fw)], a4_send[k - 1])

        @pl.when(jnp.logical_and(i == k, q == holder))
        def _(k=k):
            wait(yrow.at[pl.ds(0, k * ns * cww // (2 * ew))], a2_send)

    @pl.when(has_coupling)
    def _():
        wait(hrecv.at[pl.ds(0, ns - 1)], a1_send)
        wait(gpart.at[pl.ds(0, bs - fw)], a3_send)

        @pl.when(core == holder % 2)
        def _():
            wait(pk, a2_pass)

    @pl.when(has_pair)
    def _():
        wait(bx.at[pl.ds(0, (nx - 1) * fw)], b1_send)
        wait(qx.at[pl.ds(0, (nx - 1) * fw)], q1_send)
        wait(ql.at[pl.ds(0, bs - fw)], l1_send)
        wait(trecv.at[pl.ds(0, nz - 1)], b2_send)
        wait(yrow.at[0, pl.ds(0, (nq // 2 * nx - 1) * fw)], b3_send)


def shards(np_, nq, right_side, coupling, row_bases, row_values, column_bases, column_values, column_coupling):
    ns = nq // RB
    fw, ew = right_side.shape[1], right_side.shape[2]
    cww = coupling.shape[1]
    bs = row_bases.shape[1]
    nx = bs // ew
    nz = np_ // nx
    nw = bs // cww
    vmem = pl.BlockSpec(memory_space=pltpu.VMEM)
    scratch = (
        (ns, CB * fw, ew),
        (ns, CB * fw, ew),
        (CB, nx, fw, ew),
        (CB, fw, ew),
        (CB, nx, fw, ew),
        (CB, nz, fw, ew),
        (CB, nz, fw, ew),
        (ns, cww, ew),
        (ns, cww, ew),
        (cww, bs),
        (bs, ew),
        (RB - 1, nw, fw, ew),
        (RB - 1, fw, ew),
        (RB, bs, ew),
        (nx * fw, bs),
        (nx * fw, bs),
        (bs, ew),
        (nx, nz, fw, ew),
        (nz, nx, fw, ew),
        (nx, fw, ew),
        (PAIRS, fw, bs),
        (CB, fw, ew),
        (CB, fw, ew),
        (CB, bs, ew),
        (RB - 1, CB, fw, bs),
        (CB, fw, bs),
        (CB, fw, ew),
        (CB, fw, ew),
        (fw, ew),
    )
    return pl.pallas_call(
        functools.partial(kernel, np_, nq),
        out_shape=jax.ShapeDtypeStruct((CB, fw, ew), F32),
        in_specs=[vmem] * 7,
        out_specs=vmem,
        scratch_shapes=[pltpu.VMEM(shape, F32) for shape in scratch]
        + [pltpu.SemaphoreType.DMA((128,))],
        compiler_params=pltpu.CompilerParams(collective_id=0, has_side_effects=True),
    )(
        right_side,
        coupling.T,
        row_bases,
        row_values,
        column_bases,
        column_values,
        column_coupling,
    )


def solution(mesh):
    placed = (
        P(None, "pcol", "prow"),
        P("prow", "pcol"),
        P("prow", None),
        P(),
        P(None, "pcol", None),
        P(),
        P(None, "pcol", None),
    )
    body = functools.partial(shards, mesh.shape["pcol"], mesh.shape["prow"])
    return jax.shard_map(
        body, mesh=mesh, in_specs=placed, out_specs=P(None, "pcol", "prow"), check_vma=False
    )
```

```python
import functools

import jax
import jax.numpy as jnp
from jax import lax
from jax.experimental import pallas as pl
from jax.experimental.pallas import tpu as pltpu
from jax.sharding import PartitionSpec as P

RB = 4
CB = 6
PAIRS = CB * (CB - 1) // 2
MESH = pl.DeviceIdType.MESH
F32 = jnp.float32
BF16 = jnp.bfloat16
ROW_BY_COL = ((1,), (0,))
COL_BY_COL = ((0,), (0,))
ROW_BY_ROW = ((1,), (1,))


def halves(value):
    high = value.astype(BF16)
    low = (value - high.astype(F32)).astype(BF16)
    return high, low


def dot_of(left, right, dims):
    return lax.dot_general(left, right, (dims, ((), ())), preferred_element_type=F32)


def dot_split(left, right, dims):
    (left_high, left_low), (right_high, right_low) = left, right
    small = dot_of(left_low, right_high, dims) + dot_of(left_high, right_low, dims)
    return dot_of(left_high, right_high, dims) + small


def dot3(left, right, dims=ROW_BY_COL):
    return dot_split(halves(left), halves(right), dims)


def kernel(np_, nq, *refs):
    (rhs, coupling, bases, row_values, colbases, col_values, colcoup, out, *rest) = refs
    (upart, urecv, ux, uown, qside, vpart, crecv) = rest[:7]
    (hpart, hrecv, pk, gpart, grecv, apiece, at) = rest[7:14]
    (bx, qx, ql, tpart, trecv, tpiece, lhs) = rest[14:21]
    (yown, yx, xpart, brecv, wpart, wrecv, wown, wbuf) = rest[21:29]
    (ycol, pend, psum, den, acc, sems) = rest[29:]
    fw, ew = rhs.shape[1], rhs.shape[2]
    cww = coupling.shape[0]
    bs = fw * np_
    ns = nq // RB
    nx = bs // ew
    nz = np_ // nx
    nw = bs // cww
    per_row = ew // cww
    q = lax.axis_index("prow")
    p = lax.axis_index("pcol")
    i, s = q // ns, q % ns
    z, x = p // nx, p % nx
    core = q % 2
    partner = q + 1 - 2 * core
    k_own, w_own = p // nw, p % nw
    has_coupling = k_own > i
    top = i == RB - 1
    holder = p // per_row
    late_pair = jnp.logical_and(q > ns, q < nq - ns)

    used = [0]

    def new_sem(count=1):
        at_sem = used[0]
        used[0] += count
        return [sems.at[at_sem + n] for n in range(count)]

    z_send, z_recv, x_send, x_recv = new_sem(CB), new_sem(CB), new_sem(CB), new_sem(CB)
    v_send, v_recv = new_sem(CB), new_sem(CB)
    w_send, w_recv, col_send = new_sem(CB), new_sem(CB), new_sem(CB)
    col_recv = [new_sem(CB) for _ in range(RB - 1)]
    c1_send, c1_recv, c2_send, c2_recv = new_sem(2), new_sem(2), new_sem(2), new_sem(2)
    c3_send, c3_recv, q2_send, q2_recv = new_sem(2), new_sem(2), new_sem(2), new_sem(2)
    a1_send, a1_recv, a2_send, a2_recv, a2_pass, a3_send = new_sem(6)
    a3_recv, a4_send, a4_recv = new_sem(RB - 1), new_sem(RB - 1), new_sem(RB - 1)
    b1_send, b1_recv, q1_send, q1_recv = new_sem(2), new_sem(2), new_sem(2), new_sem(2)
    l1_send, l1_recv, b2_send, b2_recv = new_sem(2), new_sem(2), new_sem(2), new_sem(2)
    b3_send = new_sem(2)
    b3_pass = new_sem(PAIRS)
    b3_base = used[0]
    b3_recv = new_sem(PAIRS)

    def send(src, dst, send_sem, recv_sem, q_to, p_to):
        pltpu.make_async_remote_copy(
            src_ref=src,
            dst_ref=dst,
            send_sem=send_sem,
            recv_sem=recv_sem,
            device_id=(q_to, p_to),
            device_id_type=MESH,
        ).start()

    def keep(src, dst, recv_sem):
        pltpu.make_async_copy(src, dst, recv_sem).start()

    def send_or_keep(here, src, dst, send_sem, recv_sem, q_to, p_to):
        @pl.when(here)
        def _():
            keep(src, dst, recv_sem)

        @pl.when(jnp.logical_not(here))
        def _():
            send(src, dst, send_sem, recv_sem, q_to, p_to)

    def wait(ref, sem, name="w"):
        pltpu.make_async_copy(ref, ref, sem).wait()

    def rows_of(n, size):
        return pl.ds(pl.multiple_of(n * size, size), size)

    def to_columns(body):
        for start, stop in ((np_ // 2, np_), (1, np_ // 2)):

            @pl.loop(start, stop)
            def _(d):
                body(lax.rem(p + d, np_))

    def pair_of(n):
        j_own = 1
        for first in range(2, CB):
            j_own = j_own + (n >= first * (first - 1) // 2).astype(jnp.int32)
        return n - j_own * (j_own - 1) // 2, j_own

    own_pair = (nq - 1 - q, nq + ns - 1 - q)

    barrier = pltpu.get_barrier_semaphore()

    def greet(to):
        pl.semaphore_signal(barrier, inc=1, device_id=(q, to), device_id_type=MESH)

    to_columns(greet)

    @pl.loop(1, nq)
    def _(d):
        pl.semaphore_signal(
            barrier, inc=1, device_id=(lax.rem(q + d, nq), p), device_id_type=MESH
        )

    bases_split = halves(bases[...])
    inner = dot_split(halves(coupling[...]), bases_split, ROW_BY_COL)
    stacked = rhs[...].reshape(CB * fw, ew)
    first = dot_split(halves(stacked), bases_split, ROW_BY_COL)
    for n in range(ns):
        upart[n] = first[:, n * ew : (n + 1) * ew]
        hpart[n] = inner[:, n * ew : (n + 1) * ew]
    own_lanes = rows_of(s, ew)
    values = row_values[:, own_lanes]
    own_value = lax.broadcasted_iota(jnp.int32, values.shape, 0) == i
    eigen = jnp.sum(jnp.where(own_value, values, 0.0), axis=0, keepdims=True)
    lanes = lax.broadcasted_iota(jnp.int32, (fw, ew), 1)
    chosen = lanes == z * fw + lax.broadcasted_iota(jnp.int32, (fw, ew), 0)
    for j in range(CB):
        shifts = col_values[pl.ds(j, 1), rows_of(x, ew)]
        shift = jnp.sum(jnp.where(chosen, shifts, 0.0), axis=1, keepdims=True)
        den[j] = shift + eigen

    pl.semaphore_wait(barrier, np_ + nq - 2)

    chunks = (pl.ds(0, fw), pl.ds(fw, (CB - 1) * fw))
    blocks = (pl.ds(0, 1), pl.ds(1, CB - 1))

    def send_c1(c):
        @pl.loop(0, ns)
        def _(t):
            src, dst = upart.at[t, chunks[c]], urecv.at[s, chunks[c]]
            send_or_keep(t == s, src, dst, c1_send[c], c1_recv[c], i * ns + t, p)

    def send_q2(c):
        @pl.loop(0, nx)
        def _(t):
            src, dst = colbases.at[blocks[c], :, rows_of(t, ew)], qside.at[blocks[c], x]
            send_or_keep(t == x, src, dst, q2_send[c], q2_recv[c], q, z * nx + t)

    def send_c2(c):
        wait(urecv.at[:, chunks[c]], c1_recv[c], "c1_%d" % c)
        count = (1, CB - 1)[c]
        summed = jnp.sum(urecv[:, chunks[c]], axis=0)
        uown[blocks[c]] = summed.reshape(count, fw, ew)

        @pl.loop(0, nx)
        def _(t):
            src, dst = uown.at[blocks[c]], ux.at[blocks[c], x]
            send_or_keep(t == x, src, dst, c2_send[c], c2_recv[c], q, z * nx + t)

    def send_c3(c):
        wait(ux.at[blocks[c]], c2_recv[c], "c2_%d" % c)
        wait(qside.at[blocks[c]], q2_recv[c], "q2_%d" % c)
        for j in ((0,), tuple(range(1, CB)))[c]:
            left = qside[j].reshape(nx * fw, ew)
            right = ux[j].reshape(nx * fw, ew)
            vpart[j] = dot3(left, right, COL_BY_COL).reshape(nz, fw, ew)

        @pl.loop(0, nz)
        def _(t):
            src, dst = vpart.at[blocks[c], t], crecv.at[blocks[c], z]
            send_or_keep(t == z, src, dst, c3_send[c], c3_recv[c], q, t * nx + x)

    def send_b1(r, n):
        l_own, j_own = pair_of(n)

        @pl.loop(0, nx)
        def _(t):
            src_b = colcoup.at[j_own, :, rows_of(l_own, bs)]
            src_q = colbases.at[j_own]
            dst_b, dst_q = bx.at[r, rows_of(x, fw)], qx.at[r, rows_of(x, fw)]
            to = z * nx + t
            send_or_keep(t == x, src_b, dst_b, b1_send[r], b1_recv[r], q, to)
            send_or_keep(t == x, src_q, dst_q, q1_send[r], q1_recv[r], q, to)

        dst = ql.at[r, rows_of(p, fw)]
        keep(colbases.at[l_own, :, rows_of(x, ew)], dst, l1_recv[r])

        def one(to):
            src = colbases.at[l_own, :, rows_of(lax.rem(to, nx), ew)]
            send(src, dst, l1_send[r], l1_recv[r], q, to)

        to_columns(one)

    def send_b2(r):
        wait(bx.at[r], b1_recv[r], "bx%d" % r)
        wait(qx.at[r], q1_recv[r], "qx%d" % r)
        wait(ql.at[r], l1_recv[r], "ql%d" % r)
        mixed = dot3(bx[r], ql[r])
        tpart[r] = dot3(qx[r], mixed, COL_BY_COL).reshape(nx, nz, fw, ew)

        @pl.loop(0, nz)
        def _(t):
            src, dst = tpart.at[r, :, t], trecv.at[r, z]
            send_or_keep(t == z, src, dst, b2_send[r], b2_recv[r], q, t * nx + x)

    def send_b3(r, n):
        wait(trecv.at[r], b2_recv[r], "b2%d" % r)
        tpiece[r] = jnp.sum(trecv[r], axis=0)
        dst, recv_sem = lhs.at[n], sems.at[b3_base + n]

        @pl.loop(0, nq // 2)
        def _(t):
            q_to = nq - 2 - 2 * t + core
            send_or_keep(q_to == q, tpiece.at[r], dst, b3_send[r], recv_sem, q_to, p)

    @pl.when(q == holder)
    def _():
        @pl.loop(0, i * ns // 2)
        def _(t):
            src = bases.at[rows_of(lax.rem(p, per_row), cww)]
            send(src, pk, a2_send, a2_recv, i * ns - 2 - 2 * t + core, p)

    @pl.when(has_coupling)
    def _():
        @pl.loop(0, ns)
        def _(t):
            send_or_keep(t == s, hpart.at[t], hrecv.at[s], a1_send, a1_recv, i * ns + t, p)

    send_c1(0)
    send_q2(0)

    @pl.when(top)
    def _():
        send_b1(0, own_pair[0])

    send_c1(1)
    send_q2(1)

    @pl.when(has_coupling)
    def _():
        wait(hrecv, a1_recv, "a1")
        wait(pk, a2_recv, "a2")

        @pl.when(core == holder % 2)
        def _():
            send(pk, pk, a2_pass, a2_recv, partner, p)

        gpart[...] = dot3(pk[...], jnp.sum(hrecv[...], axis=0), COL_BY_COL)
        for k in range(1, RB):

            @pl.when(k_own == k)
            def _(k=k):
                dst = grecv.at[k - 1, w_own]
                keep(gpart.at[rows_of(p, fw)], dst, a3_recv[k - 1])

                def one(to):
                    send(gpart.at[rows_of(to, fw)], dst, a3_send, a3_recv[k - 1], q, to)

                to_columns(one)

    send_c2(0)
    send_c3(0)

    @pl.when(top)
    def _():
        send_b2(0)
        send_b1(1, own_pair[1])

    send_c2(1)

    for k in range(RB - 1, 0, -1):

        @pl.when(k > i)
        def _(k=k):
            wait(grecv.at[k - 1], a3_recv[k - 1], "a3_%d" % k)
            apiece[k - 1] = jnp.sum(grecv[k - 1], axis=0)
            dst = at.at[k, rows_of(p, fw)]
            keep(apiece.at[k - 1], dst, a4_recv[k - 1])

            def one(to):
                send(apiece.at[k - 1], dst, a4_send[k - 1], a4_recv[k - 1], q, to)

            to_columns(one)

    send_c3(1)

    @pl.when(late_pair)
    def _():
        send_b1(0, own_pair[1])

    def finish(j):
        yown[j] = acc[...] / den[j]
        for d in (4, 3, 5, 2, 6, 1, 7):
            if d < nz:
                to = lax.rem(z + d, nz) * nx + x
                send(yown.at[j], yx.at[j, z], z_send[j], z_recv[j], q, to)
        for k in range(1, RB):

            @pl.when(i == k)
            def _(k=k):
                @pl.loop(0, k * ns)
                def _(t):
                    send(
                        yown.at[j],
                        ycol.at[k - 1, j, :, own_lanes],
                        col_send[j],
                        col_recv[k - 1][j],
                        k * ns - 1 - t,
                        p,
                    )

        yx[j, z] = yown[j]

    def left_term(j, k, total):
        if j == 0:
            wait(at.at[k], a4_recv[k - 1], "a4_%d" % k)
        wait(ycol.at[k - 1, j], col_recv[k - 1][j], "col_%d_%d" % (k, j))
        total[...] -= dot3(ycol[k - 1, j], at[k])

    def older_left_terms(j, total):
        for k in range(RB - 1, 1, -1):
            pl.when(k > i + 1)(functools.partial(left_term, j, k, total))

    def newest_left_term(j, total):
        for k in range(1, RB):
            pl.when(k == i + 1)(functools.partial(left_term, j, k, total))

    def scatter_x(part, arrived, send_sem, recv_sem):
        for d in (2, 1, 3):
            if d < nx:
                to = lax.rem(x + d, nx)
                send(part.at[to], arrived.at[x], send_sem, recv_sem, q, z * nx + to)

    def whole_of(ref, j):
        return ref[j].reshape(nz * fw, ew)

    def start_last(j):
        wpart[j] = dot3(qside[j].reshape(nx * fw, ew), whole_of(yx, j)).reshape(nx, fw, ew)
        scatter_x(wpart.at[j], wrecv.at[j], v_send[j], v_recv[j])
        wrecv[j, x] = wpart[j, x]

    def exchange(j):
        wait(wrecv.at[j, pl.ds(0, nx - 1)], v_recv[j], "v_%d" % j)
        wown[j] = jnp.sum(wrecv[j], axis=0)

        @pl.loop(1, ns)
        def _(d):
            send(
                wown.at[j],
                wbuf.at[j, :, own_lanes],
                w_send[j],
                w_recv[j],
                i * ns + lax.rem(s + d, ns),
                p,
            )

        wbuf[j, :, own_lanes] = wown[j]

    def last_product(j):
        wait(wbuf.at[j, :, pl.ds(0, (ns - 1) * ew)], w_recv[j], "wx_%d" % j)
        out[j] = dot3(wbuf[j], bases[...], ROW_BY_ROW)

    def pair_at(l, j):
        return j * (j - 1) // 2 + l

    def pass_pairs(j):
        for l in range(j):
            n = pair_at(l, j)

            @pl.when(core == (nq - 1 - n) % 2)
            def _(n=n):
                wait(lhs.at[n], b3_recv[n], "b3_%d" % n)
                send(lhs.at[n], lhs.at[n], b3_pass[n], b3_recv[n], partner, p)

        for l in range(j):
            n = pair_at(l, j)

            @pl.when(core != (nq - 1 - n) % 2)
            def _(n=n):
                wait(lhs.at[n], b3_recv[n], "b3_%d" % n)

    def right_term(l, j):
        return dot3(lhs[pair_at(l, j)].reshape(nx * fw, ew), whole_of(yx, l))

    wait(crecv.at[blocks[0]], c3_recv[0], "c3_0")
    acc[...] = jnp.sum(crecv[0], axis=0)
    older_left_terms(0, acc)
    newest_left_term(0, acc)
    finish(0)

    @pl.when(top)
    def _():
        send_b3(0, own_pair[0])
        send_b2(1)

    wait(crecv.at[blocks[1]], c3_recv[1], "c3_1")
    for j in range(1, CB):
        pend[j] = jnp.sum(crecv[j], axis=0)

    for j in range(CB):
        last = j + 1 == CB
        if not last:
            pass_pairs(j + 1)
            psum[...] = jnp.zeros_like(psum)
            for l in range(j):
                psum[...] += right_term(l, j + 1)
            older_left_terms(j + 1, pend.at[j + 1])
        if j >= 1:
            start_last(j - 1)
        if j >= 2:
            exchange(j - 2)
        if j >= 3:
            last_product(j - 3)
        if j == 0:
            pl.when(late_pair)(functools.partial(send_b2, 0))
        if j == 1:
            pl.when(top)(functools.partial(send_b3, 1, own_pair[1]))
        if j == 2:
            pl.when(late_pair)(functools.partial(send_b3, 0, own_pair[1]))

        wait(yx.at[j, pl.ds(0, nz - 1)], z_recv[j], "z_%d" % j)
        if not last:
            xpart[j + 1] = (psum[...] + right_term(j, j + 1)).reshape(nx, fw, ew)
            scatter_x(xpart.at[j + 1], brecv.at[j + 1], x_send[j + 1], x_recv[j + 1])
            brecv[j + 1, x] = xpart[j + 1, x]
            newest_left_term(j + 1, pend.at[j + 1])
            wait(brecv.at[j + 1, pl.ds(0, nx - 1)], x_recv[j + 1], "x_%d" % (j + 1))
            acc[...] = pend[j + 1] - jnp.sum(brecv[j + 1], axis=0)
            finish(j + 1)

    start_last(CB - 1)
    exchange(CB - 2)
    last_product(CB - 3)
    exchange(CB - 1)
    last_product(CB - 2)
    last_product(CB - 1)

    for n in range(PAIRS):

        @pl.when(core == (nq - 1 - n) % 2)
        def _(n=n):
            wait(lhs.at[n], b3_pass[n])

    for c in range(2):
        wait(urecv.at[pl.ds(0, ns - 1), chunks[c]], c1_send[c])
        wait(ux.at[blocks[c], pl.ds(0, nx - 1)], c2_send[c])
        wait(qside.at[blocks[c], pl.ds(0, nx - 1)], q2_send[c])
        wait(crecv.at[blocks[c], pl.ds(0, nz - 1)], c3_send[c])
    for j in range(CB):
        wait(yx.at[j, pl.ds(0, nz - 1)], z_send[j])
        wait(wrecv.at[j, pl.ds(0, nx - 1)], v_send[j])
        wait(wbuf.at[j, :, pl.ds(0, (ns - 1) * ew)], w_send[j])
        if j > 0:
            wait(brecv.at[j, pl.ds(0, nx - 1)], x_send[j])
        for k in range(1, RB):

            @pl.when(i == k)
            def _(k=k):
                wait(at.at[0, pl.ds(0, fw * k * ns)], col_send[j])

    for k in range(1, RB):

        @pl.when(k > i)
        def _(k=k):
            wait(at.at[k, pl.ds(0, bs - fw)], a4_send[k - 1])

        @pl.when(jnp.logical_and(i == k, q == holder))
        def _(k=k):
            wait(at.at[pl.ds(0, k * ns * cww // (2 * ew))], a2_send)

    @pl.when(has_coupling)
    def _():
        wait(hrecv.at[pl.ds(0, ns - 1)], a1_send)
        wait(gpart.at[pl.ds(0, bs - fw)], a3_send)

        @pl.when(core == holder % 2)
        def _():
            wait(pk, a2_pass)

    def end_pair(r):
        wait(bx.at[r, pl.ds(0, (nx - 1) * fw)], b1_send[r])
        wait(qx.at[r, pl.ds(0, (nx - 1) * fw)], q1_send[r])
        wait(ql.at[r, pl.ds(0, bs - fw)], l1_send[r])
        wait(trecv.at[r, pl.ds(0, nz - 1)], b2_send[r])
        wait(at.at[0, pl.ds(0, (nq // 2 - 1) * nx * fw)], b3_send[r])

    @pl.when(top)
    def _():
        end_pair(0)
        end_pair(1)

    pl.when(late_pair)(functools.partial(end_pair, 0))


def shards(np_, nq, right_side, coupling, row_bases, row_values, column_bases, column_values, column_coupling):
    ns = nq // RB
    fw, ew = right_side.shape[1], right_side.shape[2]
    cww = coupling.shape[1]
    bs = row_bases.shape[1]
    nx = bs // ew
    nz = np_ // nx
    nw = bs // cww
    vmem = pl.BlockSpec(memory_space=pltpu.VMEM)
    scratch = (
        (ns, CB * fw, ew),
        (ns, CB * fw, ew),
        (CB, nx, fw, ew),
        (CB, fw, ew),
        (CB, nx, fw, ew),
        (CB, nz, fw, ew),
        (CB, nz, fw, ew),
        (ns, cww, ew),
        (ns, cww, ew),
        (cww, bs),
        (bs, ew),
        (RB - 1, nw, fw, ew),
        (RB - 1, fw, ew),
        (RB, bs, ew),
        (2, nx * fw, bs),
        (2, nx * fw, bs),
        (2, bs, ew),
        (2, nx, nz, fw, ew),
        (2, nz, nx, fw, ew),
        (2, nx, fw, ew),
        (PAIRS, nx, fw, ew),
        (CB, fw, ew),
        (CB, nz, fw, ew),
        (CB, nx, fw, ew),
        (CB, nx, fw, ew),
        (CB, nx, fw, ew),
        (CB, nx, fw, ew),
        (CB, fw, ew),
        (CB, fw, bs),
        (RB - 1, CB, fw, bs),
        (CB, fw, ew),
        (nx * fw, ew),
        (CB, fw, ew),
        (fw, ew),
    )
    return pl.pallas_call(
        functools.partial(kernel, np_, nq),
        out_shape=jax.ShapeDtypeStruct((CB, fw, ew), F32),
        in_specs=[vmem] * 7,
        out_specs=vmem,
        scratch_shapes=[pltpu.VMEM(shape, F32) for shape in scratch]
        + [pltpu.SemaphoreType.DMA((160,))],
        compiler_params=pltpu.CompilerParams(collective_id=0, has_side_effects=True),
    )(
        right_side,
        coupling.T,
        row_bases,
        row_values,
        column_bases,
        column_values,
        column_coupling,
    )


def solution(mesh):
    placed = (
        P(None, "pcol", "prow"),
        P("prow", "pcol"),
        P("prow", None),
        P(),
        P(None, "pcol", None),
        P(),
        P(None, "pcol", None),
    )
    body = functools.partial(shards, mesh.shape["pcol"], mesh.shape["prow"])
    return jax.shard_map(
        body, mesh=mesh, in_specs=placed, out_specs=P(None, "pcol", "prow"), check_vma=False
    )
```

```python
import functools

import jax
import jax.numpy as jnp
from jax import lax
from jax.experimental import pallas as pl
from jax.experimental.pallas import tpu as pltpu
from jax.sharding import PartitionSpec as P

RB = 4
CB = 6
PAIRS = CB * (CB - 1) // 2
FIRST = 2
MESH = pl.DeviceIdType.MESH
F32 = jnp.float32
BF16 = jnp.bfloat16
ROW_BY_COL = ((1,), (0,))
COL_BY_COL = ((0,), (0,))
ROW_BY_ROW = ((1,), (1,))


def halves(value):
    high = value.astype(BF16)
    low = (value - high.astype(F32)).astype(BF16)
    return high, low


def dot_of(left, right, dims):
    return lax.dot_general(left, right, (dims, ((), ())), preferred_element_type=F32)


def dot_split(left, right, dims):
    (left_high, left_low), (right_high, right_low) = left, right
    small = dot_of(left_low, right_high, dims) + dot_of(left_high, right_low, dims)
    return dot_of(left_high, right_high, dims) + small


def dot3(left, right, dims=ROW_BY_COL):
    return dot_split(halves(left), halves(right), dims)


def kernel(np_, nq, *refs):
    (rhs, coupling, bases, row_values, colbases, col_values, colcoup, out, *rest) = refs
    (upart, urecv, ux, uown, qside, vpart, crecv) = rest[:7]
    (hpart, hrecv, pk, gpart, grecv, apiece, at) = rest[7:14]
    (bx, qx, ql, tpart, trecv, tpiece, lhs) = rest[14:21]
    (yown, yx, xpart, brecv, wpart, wrecv, wown, wbuf) = rest[21:29]
    (ycol, pend, psum, den, acc, sems) = rest[29:]
    fw, ew = rhs.shape[1], rhs.shape[2]
    cww = coupling.shape[0]
    bs = fw * np_
    ns = nq // RB
    nx = bs // ew
    nz = np_ // nx
    nw = bs // cww
    per_row = ew // cww
    q = lax.axis_index("prow")
    p = lax.axis_index("pcol")
    i, s = q // ns, q % ns
    z, x = p // nx, p % nx
    core = q % 2
    partner = q + 1 - 2 * core
    k_own, w_own = p // nw, p % nw
    has_coupling = k_own > i
    top = i == RB - 1
    holder = p // per_row
    late_pair = jnp.logical_and(q > ns, q < nq - ns)

    used = [0]

    def new_sem(count=1):
        at_sem = used[0]
        used[0] += count
        return [sems.at[at_sem + n] for n in range(count)]

    z_send, z_recv, x_send, x_recv = new_sem(CB), new_sem(CB), new_sem(CB), new_sem(CB)
    v_send, v_recv = new_sem(CB), new_sem(CB)
    w_send, w_recv, col_send = new_sem(CB), new_sem(CB), new_sem(CB)
    col_recv = [new_sem(CB) for _ in range(RB - 1)]
    c1_send, c1_recv, c2_send, c2_recv = new_sem(2), new_sem(2), new_sem(2), new_sem(2)
    c3_send, c3_recv, q2_send, q2_recv = new_sem(2), new_sem(2), new_sem(2), new_sem(2)
    a1_send, a1_recv, a2_send, a2_recv, a2_pass, a3_send = new_sem(6)
    a3_recv, a4_send, a4_recv = new_sem(RB - 1), new_sem(RB - 1), new_sem(RB - 1)
    a5_send, a5_recv = new_sem(RB - 1), new_sem(RB - 1)
    b1_send, b1_recv, q1_send, q1_recv = new_sem(2), new_sem(2), new_sem(2), new_sem(2)
    l1_send, l1_recv, b2_send, b2_recv = new_sem(2), new_sem(2), new_sem(2), new_sem(2)
    b3_send = new_sem(2)
    b3_pass = new_sem(PAIRS)
    b3_base = used[0]
    b3_recv = new_sem(PAIRS)

    def send(src, dst, send_sem, recv_sem, q_to, p_to):
        pltpu.make_async_remote_copy(
            src_ref=src,
            dst_ref=dst,
            send_sem=send_sem,
            recv_sem=recv_sem,
            device_id=(q_to, p_to),
            device_id_type=MESH,
        ).start()

    def keep(src, dst, recv_sem):
        pltpu.make_async_copy(src, dst, recv_sem).start()

    def send_or_keep(here, src, dst, send_sem, recv_sem, q_to, p_to):
        @pl.when(here)
        def _():
            keep(src, dst, recv_sem)

        @pl.when(jnp.logical_not(here))
        def _():
            send(src, dst, send_sem, recv_sem, q_to, p_to)

    def wait(ref, sem, name="w"):
        pltpu.make_async_copy(ref, ref, sem).wait()

    def rows_of(n, size):
        return pl.ds(pl.multiple_of(n * size, size), size)

    def to_columns(body):
        for start, stop in ((np_ // 2, np_), (1, np_ // 2)):

            @pl.loop(start, stop)
            def _(d):
                body(lax.rem(p + d, np_))

    def pair_of(n):
        j_own = 1
        for first in range(2, CB):
            j_own = j_own + (n >= first * (first - 1) // 2).astype(jnp.int32)
        return n - j_own * (j_own - 1) // 2, j_own

    own_pair = (nq - 1 - q, nq + ns - 1 - q)

    barrier = pltpu.get_barrier_semaphore()

    def greet(to):
        pl.semaphore_signal(barrier, inc=1, device_id=(q, to), device_id_type=MESH)

    to_columns(greet)

    @pl.loop(1, nq)
    def _(d):
        pl.semaphore_signal(
            barrier, inc=1, device_id=(lax.rem(q + d, nq), p), device_id_type=MESH
        )

    bases_split = halves(bases[...])
    inner = dot_split(halves(coupling[...]), bases_split, ROW_BY_COL)
    stacked = rhs[...].reshape(CB * fw, ew)
    first = dot_split(halves(stacked), bases_split, ROW_BY_COL)
    for n in range(ns):
        upart[n] = first[:, n * ew : (n + 1) * ew]
        hpart[n] = inner[:, n * ew : (n + 1) * ew]
    own_lanes = rows_of(s, ew)
    values = row_values[:, own_lanes]
    own_value = lax.broadcasted_iota(jnp.int32, values.shape, 0) == i
    eigen = jnp.sum(jnp.where(own_value, values, 0.0), axis=0, keepdims=True)
    lanes = lax.broadcasted_iota(jnp.int32, (fw, ew), 1)
    chosen = lanes == z * fw + lax.broadcasted_iota(jnp.int32, (fw, ew), 0)
    for j in range(CB):
        shifts = col_values[pl.ds(j, 1), rows_of(x, ew)]
        shift = jnp.sum(jnp.where(chosen, shifts, 0.0), axis=1, keepdims=True)
        den[j] = shift + eigen

    pl.semaphore_wait(barrier, np_ + nq - 2)

    chunks = (pl.ds(0, FIRST * fw), pl.ds(FIRST * fw, (CB - FIRST) * fw))
    blocks = (pl.ds(0, FIRST), pl.ds(FIRST, CB - FIRST))

    def send_c1(c):
        @pl.loop(0, ns)
        def _(t):
            src, dst = upart.at[t, chunks[c]], urecv.at[s, chunks[c]]
            send_or_keep(t == s, src, dst, c1_send[c], c1_recv[c], i * ns + t, p)

    def send_q2(c):
        @pl.loop(0, nx)
        def _(t):
            src, dst = colbases.at[blocks[c], :, rows_of(t, ew)], qside.at[blocks[c], x]
            send_or_keep(t == x, src, dst, q2_send[c], q2_recv[c], q, z * nx + t)

    def send_c2(c):
        wait(urecv.at[:, chunks[c]], c1_recv[c], "c1_%d" % c)
        count = (FIRST, CB - FIRST)[c]
        summed = jnp.sum(urecv[:, chunks[c]], axis=0)
        uown[blocks[c]] = summed.reshape(count, fw, ew)

        @pl.loop(0, nx)
        def _(t):
            src, dst = uown.at[blocks[c]], ux.at[blocks[c], x]
            send_or_keep(t == x, src, dst, c2_send[c], c2_recv[c], q, z * nx + t)

    def send_c3(c):
        wait(ux.at[blocks[c]], c2_recv[c], "c2_%d" % c)
        wait(qside.at[blocks[c]], q2_recv[c], "q2_%d" % c)
        for j in (range(FIRST), range(FIRST, CB))[c]:
            left = qside[j].reshape(nx * fw, ew)
            right = ux[j].reshape(nx * fw, ew)
            vpart[j] = dot3(left, right, COL_BY_COL).reshape(nz, fw, ew)

        @pl.loop(0, nz)
        def _(t):
            src, dst = vpart.at[blocks[c], t], crecv.at[blocks[c], z]
            send_or_keep(t == z, src, dst, c3_send[c], c3_recv[c], q, t * nx + x)

    def send_b1(r, n):
        l_own, j_own = pair_of(n)

        @pl.loop(0, nx)
        def _(t):
            src_b = colcoup.at[j_own, :, rows_of(l_own, bs)]
            src_q = colbases.at[j_own]
            dst_b, dst_q = bx.at[r, rows_of(x, fw)], qx.at[r, rows_of(x, fw)]
            to = z * nx + t
            send_or_keep(t == x, src_b, dst_b, b1_send[r], b1_recv[r], q, to)
            send_or_keep(t == x, src_q, dst_q, q1_send[r], q1_recv[r], q, to)

        dst = ql.at[r, rows_of(p, fw)]
        keep(colbases.at[l_own, :, rows_of(x, ew)], dst, l1_recv[r])

        def one(to):
            src = colbases.at[l_own, :, rows_of(lax.rem(to, nx), ew)]
            send(src, dst, l1_send[r], l1_recv[r], q, to)

        to_columns(one)

    def send_b2(r):
        wait(bx.at[r], b1_recv[r], "bx%d" % r)
        wait(qx.at[r], q1_recv[r], "qx%d" % r)
        wait(ql.at[r], l1_recv[r], "ql%d" % r)
        mixed = dot3(bx[r], ql[r])
        tpart[r] = dot3(qx[r], mixed, COL_BY_COL).reshape(nx, nz, fw, ew)

        @pl.loop(0, nz)
        def _(t):
            src, dst = tpart.at[r, :, t], trecv.at[r, z]
            send_or_keep(t == z, src, dst, b2_send[r], b2_recv[r], q, t * nx + x)

    def send_b3(r, n):
        wait(trecv.at[r], b2_recv[r], "b2%d" % r)
        tpiece[r] = jnp.sum(trecv[r], axis=0)
        dst, recv_sem = lhs.at[n], sems.at[b3_base + n]

        @pl.loop(0, nq // 2)
        def _(t):
            q_to = nq - 2 - 2 * t + core
            send_or_keep(q_to == q, tpiece.at[r], dst, b3_send[r], recv_sem, q_to, p)

    @pl.when(q == holder)
    def _():
        @pl.loop(0, i * ns // 2)
        def _(t):
            src = bases.at[rows_of(lax.rem(p, per_row), cww)]
            send(src, pk, a2_send, a2_recv, i * ns - 2 - 2 * t + core, p)

    @pl.when(has_coupling)
    def _():
        @pl.loop(0, ns)
        def _(t):
            send_or_keep(t == s, hpart.at[t], hrecv.at[s], a1_send, a1_recv, i * ns + t, p)

    send_c1(0)
    send_q2(0)

    @pl.when(top)
    def _():
        send_b1(0, own_pair[0])

    send_c1(1)
    send_q2(1)

    @pl.when(has_coupling)
    def _():
        wait(hrecv, a1_recv, "a1")
        wait(pk, a2_recv, "a2")

        @pl.when(core == holder % 2)
        def _():
            send(pk, pk, a2_pass, a2_recv, partner, p)

        gpart[...] = dot3(pk[...], jnp.sum(hrecv[...], axis=0), COL_BY_COL)
        for k in range(1, RB):

            @pl.when(k_own == k)
            def _(k=k):
                dst = grecv.at[k - 1, w_own]
                keep(gpart.at[rows_of(x * nz + z, fw)], dst, a3_recv[k - 1])

                def one(to):
                    order = lax.rem(to, nx) * nz + to // nx
                    send(gpart.at[rows_of(order, fw)], dst, a3_send, a3_recv[k - 1], q, to)

                to_columns(one)

    send_c2(0)

    @pl.when(top)
    def _():
        send_b2(0)

    send_c3(0)
    send_c2(1)

    for k in range(RB - 1, 0, -1):

        @pl.when(k > i)
        def _(k=k):
            wait(grecv.at[k - 1], a3_recv[k - 1], "a3_%d" % k)
            apiece[k - 1] = jnp.sum(grecv[k - 1], axis=0)
            dst = at.at[k, rows_of(x * nz + z, fw)]
            keep(apiece.at[k - 1], dst, a4_recv[k - 1])
            for d in (4, 3, 5, 2, 6, 1, 7):
                if d < nz:
                    to = lax.rem(z + d, nz) * nx + x
                    send(apiece.at[k - 1], dst, a4_send[k - 1], a4_recv[k - 1], q, to)

    for k in range(RB - 1, 0, -1):

        @pl.when(k > i)
        def _(k=k):
            half = at.at[k, rows_of(x, nz * fw)]
            wait(half, a4_recv[k - 1], "a4_%d" % k)
            for d in (2, 1, 3):
                if d < nx:
                    to = z * nx + lax.rem(x + d, nx)
                    send(half, half, a5_send[k - 1], a5_recv[k - 1], q, to)

    send_c3(1)

    @pl.when(top)
    def _():
        send_b1(1, own_pair[1])

    @pl.when(late_pair)
    def _():
        send_b1(0, own_pair[1])

    def finish(j):
        yown[j] = acc[...] / den[j]
        for d in (4, 3, 5, 2, 6, 1, 7):
            if d < nz:
                to = lax.rem(z + d, nz) * nx + x
                send(yown.at[j], yx.at[j, z], z_send[j], z_recv[j], q, to)
        for k in range(1, RB):

            @pl.when(i == k)
            def _(k=k):
                @pl.loop(0, k * ns)
                def _(t):
                    send(
                        yown.at[j],
                        ycol.at[k - 1, j, :, own_lanes],
                        col_send[j],
                        col_recv[k - 1][j],
                        k * ns - 1 - t,
                        p,
                    )

        yx[j, z] = yown[j]

    def left_term(j, k, total):
        if j == 0:
            wait(at.at[k, pl.ds(0, (nx - 1) * nz * fw)], a5_recv[k - 1], "a5_%d" % k)
        wait(ycol.at[k - 1, j], col_recv[k - 1][j], "col_%d_%d" % (k, j))
        total[...] -= dot3(ycol[k - 1, j], at[k])

    def older_left_terms(j, total):
        for k in range(RB - 1, 1, -1):
            pl.when(k > i + 1)(functools.partial(left_term, j, k, total))

    def newest_left_term(j, total):
        for k in range(1, RB):
            pl.when(k == i + 1)(functools.partial(left_term, j, k, total))

    def scatter_x(part, arrived, send_sem, recv_sem):
        for d in (2, 1, 3):
            if d < nx:
                to = lax.rem(x + d, nx)
                send(part.at[to], arrived.at[x], send_sem, recv_sem, q, z * nx + to)

    def whole_of(ref, j):
        return ref[j].reshape(nz * fw, ew)

    def start_last(j):
        wpart[j] = dot3(qside[j].reshape(nx * fw, ew), whole_of(yx, j)).reshape(nx, fw, ew)
        scatter_x(wpart.at[j], wrecv.at[j], v_send[j], v_recv[j])
        wrecv[j, x] = wpart[j, x]

    def exchange(j):
        wait(wrecv.at[j, pl.ds(0, nx - 1)], v_recv[j], "v_%d" % j)
        wown[j] = jnp.sum(wrecv[j], axis=0)

        @pl.loop(1, ns)
        def _(d):
            send(
                wown.at[j],
                wbuf.at[j, :, own_lanes],
                w_send[j],
                w_recv[j],
                i * ns + lax.rem(s + d, ns),
                p,
            )

        wbuf[j, :, own_lanes] = wown[j]

    def last_product(j):
        wait(wbuf.at[j, :, pl.ds(0, (ns - 1) * ew)], w_recv[j], "wx_%d" % j)
        out[j] = dot3(wbuf[j], bases[...], ROW_BY_ROW)

    def pair_at(l, j):
        return j * (j - 1) // 2 + l

    def pass_pairs(j):
        for l in range(j):
            n = pair_at(l, j)

            @pl.when(core == (nq - 1 - n) % 2)
            def _(n=n):
                wait(lhs.at[n], b3_recv[n], "b3_%d" % n)
                send(lhs.at[n], lhs.at[n], b3_pass[n], b3_recv[n], partner, p)

        for l in range(j):
            n = pair_at(l, j)

            @pl.when(core != (nq - 1 - n) % 2)
            def _(n=n):
                wait(lhs.at[n], b3_recv[n], "b3_%d" % n)

    def right_term(l, j):
        return dot3(lhs[pair_at(l, j)].reshape(nx * fw, ew), whole_of(yx, l))

    wait(crecv.at[blocks[0]], c3_recv[0], "c3_0")
    acc[...] = jnp.sum(crecv[0], axis=0)
    older_left_terms(0, acc)
    newest_left_term(0, acc)
    finish(0)

    @pl.when(top)
    def _():
        send_b3(0, own_pair[0])

    for j in range(1, FIRST):
        pend[j] = jnp.sum(crecv[j], axis=0)

    for j in range(CB):
        last = j + 1 == CB
        if j == 1:
            pl.when(top)(functools.partial(send_b2, 1))
            pl.when(late_pair)(functools.partial(send_b2, 0))
            wait(crecv.at[blocks[1]], c3_recv[1], "c3_1")
            for later in range(FIRST, CB):
                pend[later] = jnp.sum(crecv[later], axis=0)
        if j == 2:
            pl.when(top)(functools.partial(send_b3, 1, own_pair[1]))
        if not last:
            pass_pairs(j + 1)
            psum[...] = jnp.zeros_like(psum)
            for l in range(j):
                psum[...] += right_term(l, j + 1)
            older_left_terms(j + 1, pend.at[j + 1])
        if j >= 1:
            start_last(j - 1)
        if j >= 2:
            exchange(j - 2)
        if j >= 3:
            last_product(j - 3)
        if last:
            exchange(j - 1)
        if j == 2:
            pl.when(late_pair)(functools.partial(send_b3, 0, own_pair[1]))

        wait(yx.at[j, pl.ds(0, nz - 1)], z_recv[j], "z_%d" % j)
        if not last:
            xpart[j + 1] = (psum[...] + right_term(j, j + 1)).reshape(nx, fw, ew)
            scatter_x(xpart.at[j + 1], brecv.at[j + 1], x_send[j + 1], x_recv[j + 1])
            brecv[j + 1, x] = xpart[j + 1, x]
            newest_left_term(j + 1, pend.at[j + 1])
            wait(brecv.at[j + 1, pl.ds(0, nx - 1)], x_recv[j + 1], "x_%d" % (j + 1))
            acc[...] = pend[j + 1] - jnp.sum(brecv[j + 1], axis=0)
            finish(j + 1)

    start_last(CB - 1)
    last_product(CB - 3)
    last_product(CB - 2)
    exchange(CB - 1)
    last_product(CB - 1)

    for n in range(PAIRS):

        @pl.when(core == (nq - 1 - n) % 2)
        def _(n=n):
            wait(lhs.at[n], b3_pass[n])

    for c in range(2):
        wait(urecv.at[pl.ds(0, ns - 1), chunks[c]], c1_send[c])
        wait(ux.at[blocks[c], pl.ds(0, nx - 1)], c2_send[c])
        wait(qside.at[blocks[c], pl.ds(0, nx - 1)], q2_send[c])
        wait(crecv.at[blocks[c], pl.ds(0, nz - 1)], c3_send[c])
    for j in range(CB):
        wait(yx.at[j, pl.ds(0, nz - 1)], z_send[j])
        wait(wrecv.at[j, pl.ds(0, nx - 1)], v_send[j])
        wait(wbuf.at[j, :, pl.ds(0, (ns - 1) * ew)], w_send[j])
        if j > 0:
            wait(brecv.at[j, pl.ds(0, nx - 1)], x_send[j])
        for k in range(1, RB):

            @pl.when(i == k)
            def _(k=k):
                wait(at.at[0, pl.ds(0, fw * k * ns)], col_send[j])

    for k in range(1, RB):

        @pl.when(k > i)
        def _(k=k):
            wait(at.at[k, pl.ds(0, (nz - 1) * fw)], a4_send[k - 1])
            wait(at.at[k, pl.ds(0, (nx - 1) * nz * fw)], a5_send[k - 1])

        @pl.when(jnp.logical_and(i == k, q == holder))
        def _(k=k):
            wait(at.at[pl.ds(0, k * ns * cww // (2 * ew))], a2_send)

    @pl.when(has_coupling)
    def _():
        wait(hrecv.at[pl.ds(0, ns - 1)], a1_send)
        wait(gpart.at[pl.ds(0, bs - fw)], a3_send)

        @pl.when(core == holder % 2)
        def _():
            wait(pk, a2_pass)

    def end_pair(r):
        wait(bx.at[r, pl.ds(0, (nx - 1) * fw)], b1_send[r])
        wait(qx.at[r, pl.ds(0, (nx - 1) * fw)], q1_send[r])
        wait(ql.at[r, pl.ds(0, bs - fw)], l1_send[r])
        wait(trecv.at[r, pl.ds(0, nz - 1)], b2_send[r])
        wait(at.at[0, pl.ds(0, (nq // 2 - 1) * nx * fw)], b3_send[r])

    @pl.when(top)
    def _():
        end_pair(0)
        end_pair(1)

    pl.when(late_pair)(functools.partial(end_pair, 0))


def shards(np_, nq, right_side, coupling, row_bases, row_values, column_bases, column_values, column_coupling):
    ns = nq // RB
    fw, ew = right_side.shape[1], right_side.shape[2]
    cww = coupling.shape[1]
    bs = row_bases.shape[1]
    nx = bs // ew
    nz = np_ // nx
    nw = bs // cww
    vmem = pl.BlockSpec(memory_space=pltpu.VMEM)
    scratch = (
        (ns, CB * fw, ew),
        (ns, CB * fw, ew),
        (CB, nx, fw, ew),
        (CB, fw, ew),
        (CB, nx, fw, ew),
        (CB, nz, fw, ew),
        (CB, nz, fw, ew),
        (ns, cww, ew),
        (ns, cww, ew),
        (cww, bs),
        (bs, ew),
        (RB - 1, nw, fw, ew),
        (RB - 1, fw, ew),
        (RB, bs, ew),
        (2, nx * fw, bs),
        (2, nx * fw, bs),
        (2, bs, ew),
        (2, nx, nz, fw, ew),
        (2, nz, nx, fw, ew),
        (2, nx, fw, ew),
        (PAIRS, nx, fw, ew),
        (CB, fw, ew),
        (CB, nz, fw, ew),
        (CB, nx, fw, ew),
        (CB, nx, fw, ew),
        (CB, nx, fw, ew),
        (CB, nx, fw, ew),
        (CB, fw, ew),
        (CB, fw, bs),
        (RB - 1, CB, fw, bs),
        (CB, fw, ew),
        (nx * fw, ew),
        (CB, fw, ew),
        (fw, ew),
    )
    return pl.pallas_call(
        functools.partial(kernel, np_, nq),
        out_shape=jax.ShapeDtypeStruct((CB, fw, ew), F32),
        in_specs=[vmem] * 7,
        out_specs=vmem,
        scratch_shapes=[pltpu.VMEM(shape, F32) for shape in scratch]
        + [pltpu.SemaphoreType.DMA((160,))],
        compiler_params=pltpu.CompilerParams(collective_id=0, has_side_effects=True),
    )(
        right_side,
        coupling.T,
        row_bases,
        row_values,
        column_bases,
        column_values,
        column_coupling,
    )


def solution(mesh):
    placed = (
        P(None, "pcol", "prow"),
        P("prow", "pcol"),
        P("prow", None),
        P(),
        P(None, "pcol", None),
        P(),
        P(None, "pcol", None),
    )
    body = functools.partial(shards, mesh.shape["pcol"], mesh.shape["prow"])
    return jax.shard_map(
        body, mesh=mesh, in_specs=placed, out_specs=P(None, "pcol", "prow"), check_vma=False
    )
```

```python
import functools

import jax
import jax.numpy as jnp
from jax import lax
from jax.experimental import pallas as pl
from jax.experimental.pallas import tpu as pltpu
from jax.sharding import PartitionSpec as P

RB = 4
CB = 6
PAIRS = CB * (CB - 1) // 2
FIRST = 2
MESH = pl.DeviceIdType.MESH
F32 = jnp.float32
BF16 = jnp.bfloat16
ROW_BY_COL = ((1,), (0,))
COL_BY_COL = ((0,), (0,))
ROW_BY_ROW = ((1,), (1,))


def halves(value):
    high = value.astype(BF16)
    low = (value - high.astype(F32)).astype(BF16)
    return high, low


def dot_of(left, right, dims):
    return lax.dot_general(left, right, (dims, ((), ())), preferred_element_type=F32)


def dot_split(left, right, dims):
    (left_high, left_low), (right_high, right_low) = left, right
    small = dot_of(left_low, right_high, dims) + dot_of(left_high, right_low, dims)
    return dot_of(left_high, right_high, dims) + small


def dot3(left, right, dims=ROW_BY_COL):
    return dot_split(halves(left), halves(right), dims)


def kernel(np_, nq, *refs):
    (rhs, coupling, bases, row_values, colbases, col_values, colcoup, out, *rest) = refs
    (upart, urecv, ux, uown, qside, vpart, crecv) = rest[:7]
    (hpart, hrecv, pk, gpart, grecv, apiece, at) = rest[7:14]
    (bx, qx, ql, tpart, trecv, tpiece, lhs) = rest[14:21]
    (yown, yx, xpart, brecv, wpart, wrecv) = rest[21:27]
    (ycol, pend, psum, den, acc, sems) = rest[27:]
    fw, ew = rhs.shape[1], rhs.shape[2]
    cww = coupling.shape[0]
    bs = fw * np_
    ns = nq // RB
    nx = bs // ew
    nz = np_ // nx
    nw = bs // cww
    per_row = ew // cww
    q = lax.axis_index("prow")
    p = lax.axis_index("pcol")
    i, s = q // ns, q % ns
    z, x = p // nx, p % nx
    core = q % 2
    partner = q + 1 - 2 * core
    k_own, w_own = p // nw, p % nw
    has_coupling = k_own > i
    top = i == RB - 1
    holder = p // per_row
    late_pair = jnp.logical_and(q > ns, q < nq - ns)

    used = [0]

    def new_sem(count=1):
        at_sem = used[0]
        used[0] += count
        return [sems.at[at_sem + n] for n in range(count)]

    z_send, z_recv, x_send, x_recv = new_sem(CB), new_sem(CB), new_sem(CB), new_sem(CB)
    w_send, w_recv, col_send = new_sem(CB), new_sem(CB), new_sem(CB)
    col_recv = [new_sem(CB) for _ in range(RB - 1)]
    c1_send, c1_recv, c2_send, c2_recv = new_sem(2), new_sem(2), new_sem(2), new_sem(2)
    c3_send, c3_recv, q2_send, q2_recv = new_sem(2), new_sem(2), new_sem(2), new_sem(2)
    a1_send, a1_recv, a2_send, a2_recv, a2_pass, a3_send = new_sem(6)
    a3_recv, a4_send, a4_recv = new_sem(RB - 1), new_sem(RB - 1), new_sem(RB - 1)
    a5_send, a5_recv = new_sem(RB - 1), new_sem(RB - 1)
    b1_send, b1_recv, q1_send, q1_recv = new_sem(2), new_sem(2), new_sem(2), new_sem(2)
    l1_send, l1_recv, b2_send, b2_recv = new_sem(2), new_sem(2), new_sem(2), new_sem(2)
    b3_send = new_sem(2)
    b3_pass = new_sem(PAIRS)
    b3_base = used[0]
    b3_recv = new_sem(PAIRS)

    def send(src, dst, send_sem, recv_sem, q_to, p_to):
        pltpu.make_async_remote_copy(
            src_ref=src,
            dst_ref=dst,
            send_sem=send_sem,
            recv_sem=recv_sem,
            device_id=(q_to, p_to),
            device_id_type=MESH,
        ).start()

    def keep(src, dst, recv_sem):
        pltpu.make_async_copy(src, dst, recv_sem).start()

    def send_or_keep(here, src, dst, send_sem, recv_sem, q_to, p_to):
        @pl.when(here)
        def _():
            keep(src, dst, recv_sem)

        @pl.when(jnp.logical_not(here))
        def _():
            send(src, dst, send_sem, recv_sem, q_to, p_to)

    def wait(ref, sem, name="w"):
        pltpu.make_async_copy(ref, ref, sem).wait()

    def rows_of(n, size):
        return pl.ds(pl.multiple_of(n * size, size), size)

    def to_columns(body):
        for start, stop in ((np_ // 2, np_), (1, np_ // 2)):

            @pl.loop(start, stop)
            def _(d):
                body(lax.rem(p + d, np_))

    def pair_of(n):
        j_own = 1
        for first in range(2, CB):
            j_own = j_own + (n >= first * (first - 1) // 2).astype(jnp.int32)
        return n - j_own * (j_own - 1) // 2, j_own

    own_pair = (nq - 1 - q, nq + ns - 1 - q)

    barrier = pltpu.get_barrier_semaphore()

    def greet(to):
        pl.semaphore_signal(barrier, inc=1, device_id=(q, to), device_id_type=MESH)

    to_columns(greet)

    @pl.loop(1, nq)
    def _(d):
        pl.semaphore_signal(
            barrier, inc=1, device_id=(lax.rem(q + d, nq), p), device_id_type=MESH
        )

    @pl.loop(1, ns)
    def _(d):
        q_to = i * ns + lax.rem(s + d, ns)
        for x_off in range(1, nx):
            to = z * nx + lax.rem(x + x_off, nx)
            pl.semaphore_signal(barrier, inc=1, device_id=(q_to, to), device_id_type=MESH)

    bases_split = halves(bases[...])
    inner = dot_split(halves(coupling[...]), bases_split, ROW_BY_COL)
    stacked = rhs[...].reshape(CB * fw, ew)
    first = dot_split(halves(stacked), bases_split, ROW_BY_COL)
    for n in range(ns):
        upart[n] = first[:, n * ew : (n + 1) * ew]
        hpart[n] = inner[:, n * ew : (n + 1) * ew]
    own_lanes = rows_of(s, ew)
    values = row_values[:, own_lanes]
    own_value = lax.broadcasted_iota(jnp.int32, values.shape, 0) == i
    eigen = jnp.sum(jnp.where(own_value, values, 0.0), axis=0, keepdims=True)
    lanes = lax.broadcasted_iota(jnp.int32, (fw, ew), 1)
    chosen = lanes == z * fw + lax.broadcasted_iota(jnp.int32, (fw, ew), 0)
    for j in range(CB):
        shifts = col_values[pl.ds(j, 1), rows_of(x, ew)]
        shift = jnp.sum(jnp.where(chosen, shifts, 0.0), axis=1, keepdims=True)
        den[j] = shift + eigen

    pl.semaphore_wait(barrier, np_ + nq - 2 + (ns - 1) * (nx - 1))

    chunks = (pl.ds(0, FIRST * fw), pl.ds(FIRST * fw, (CB - FIRST) * fw))
    blocks = (pl.ds(0, FIRST), pl.ds(FIRST, CB - FIRST))

    def send_c1(c):
        @pl.loop(0, ns)
        def _(t):
            src, dst = upart.at[t, chunks[c]], urecv.at[s, chunks[c]]
            send_or_keep(t == s, src, dst, c1_send[c], c1_recv[c], i * ns + t, p)

    def send_q2(c):
        @pl.loop(0, nx)
        def _(t):
            src, dst = colbases.at[blocks[c], :, rows_of(t, ew)], qside.at[blocks[c], x]
            send_or_keep(t == x, src, dst, q2_send[c], q2_recv[c], q, z * nx + t)

    def send_c2(c):
        wait(urecv.at[:, chunks[c]], c1_recv[c], "c1_%d" % c)
        count = (FIRST, CB - FIRST)[c]
        summed = jnp.sum(urecv[:, chunks[c]], axis=0)
        uown[blocks[c]] = summed.reshape(count, fw, ew)

        @pl.loop(0, nx)
        def _(t):
            src, dst = uown.at[blocks[c]], ux.at[blocks[c], x]
            send_or_keep(t == x, src, dst, c2_send[c], c2_recv[c], q, z * nx + t)

    def send_c3(c):
        wait(ux.at[blocks[c]], c2_recv[c], "c2_%d" % c)
        wait(qside.at[blocks[c]], q2_recv[c], "q2_%d" % c)
        for j in (range(FIRST), range(FIRST, CB))[c]:
            left = qside[j].reshape(nx * fw, ew)
            right = ux[j].reshape(nx * fw, ew)
            vpart[j] = dot3(left, right, COL_BY_COL).reshape(nz, fw, ew)

        @pl.loop(0, nz)
        def _(t):
            src, dst = vpart.at[blocks[c], t], crecv.at[blocks[c], z]
            send_or_keep(t == z, src, dst, c3_send[c], c3_recv[c], q, t * nx + x)

    def send_b1(r, n):
        l_own, j_own = pair_of(n)

        @pl.loop(0, nx)
        def _(t):
            src_b = colcoup.at[j_own, :, rows_of(l_own, bs)]
            src_q = colbases.at[j_own]
            dst_b, dst_q = bx.at[r, rows_of(x, fw)], qx.at[r, rows_of(x, fw)]
            to = z * nx + t
            send_or_keep(t == x, src_b, dst_b, b1_send[r], b1_recv[r], q, to)
            send_or_keep(t == x, src_q, dst_q, q1_send[r], q1_recv[r], q, to)

        dst = ql.at[r, rows_of(p, fw)]
        keep(colbases.at[l_own, :, rows_of(x, ew)], dst, l1_recv[r])

        def one(to):
            src = colbases.at[l_own, :, rows_of(lax.rem(to, nx), ew)]
            send(src, dst, l1_send[r], l1_recv[r], q, to)

        to_columns(one)

    def send_b2(r):
        wait(bx.at[r], b1_recv[r], "bx%d" % r)
        wait(qx.at[r], q1_recv[r], "qx%d" % r)
        wait(ql.at[r], l1_recv[r], "ql%d" % r)
        mixed = dot3(bx[r], ql[r])
        tpart[r] = dot3(qx[r], mixed, COL_BY_COL).reshape(nx, nz, fw, ew)

        @pl.loop(0, nz)
        def _(t):
            src, dst = tpart.at[r, :, t], trecv.at[r, z]
            send_or_keep(t == z, src, dst, b2_send[r], b2_recv[r], q, t * nx + x)

    def send_b3(r, n):
        wait(trecv.at[r], b2_recv[r], "b2%d" % r)
        tpiece[r] = jnp.sum(trecv[r], axis=0)
        dst, recv_sem = lhs.at[n], sems.at[b3_base + n]

        @pl.loop(0, nq // 2)
        def _(t):
            q_to = nq - 2 - 2 * t + core
            send_or_keep(q_to == q, tpiece.at[r], dst, b3_send[r], recv_sem, q_to, p)

    @pl.when(q == holder)
    def _():
        @pl.loop(0, i * ns // 2)
        def _(t):
            src = bases.at[rows_of(lax.rem(p, per_row), cww)]
            send(src, pk, a2_send, a2_recv, i * ns - 2 - 2 * t + core, p)

    @pl.when(has_coupling)
    def _():
        @pl.loop(0, ns)
        def _(t):
            send_or_keep(t == s, hpart.at[t], hrecv.at[s], a1_send, a1_recv, i * ns + t, p)

    send_c1(0)
    send_q2(0)

    @pl.when(top)
    def _():
        send_b1(0, own_pair[0])

    send_c1(1)
    send_q2(1)

    @pl.when(has_coupling)
    def _():
        wait(hrecv, a1_recv, "a1")
        wait(pk, a2_recv, "a2")

        @pl.when(core == holder % 2)
        def _():
            send(pk, pk, a2_pass, a2_recv, partner, p)

        gpart[...] = dot3(pk[...], jnp.sum(hrecv[...], axis=0), COL_BY_COL)
        for k in range(1, RB):

            @pl.when(k_own == k)
            def _(k=k):
                dst = grecv.at[k - 1, w_own]
                keep(gpart.at[rows_of(x * nz + z, fw)], dst, a3_recv[k - 1])

                def one(to):
                    order = lax.rem(to, nx) * nz + to // nx
                    send(gpart.at[rows_of(order, fw)], dst, a3_send, a3_recv[k - 1], q, to)

                to_columns(one)

    send_c2(0)
    send_c3(0)

    @pl.when(top)
    def _():
        send_b2(0)

    send_c2(1)

    for k in range(RB - 1, 0, -1):

        @pl.when(k > i)
        def _(k=k):
            wait(grecv.at[k - 1], a3_recv[k - 1], "a3_%d" % k)
            apiece[k - 1] = jnp.sum(grecv[k - 1], axis=0)
            dst = at.at[k, rows_of(x * nz + z, fw)]
            keep(apiece.at[k - 1], dst, a4_recv[k - 1])
            for d in (4, 3, 5, 2, 6, 1, 7):
                if d < nz:
                    to = lax.rem(z + d, nz) * nx + x
                    send(apiece.at[k - 1], dst, a4_send[k - 1], a4_recv[k - 1], q, to)

    for k in range(RB - 1, 0, -1):

        @pl.when(k > i)
        def _(k=k):
            half = at.at[k, rows_of(x, nz * fw)]
            wait(half, a4_recv[k - 1], "a4_%d" % k)
            for d in (2, 1, 3):
                if d < nx:
                    to = z * nx + lax.rem(x + d, nx)
                    send(half, half, a5_send[k - 1], a5_recv[k - 1], q, to)

    def finish(j):
        yown[j] = acc[...] / den[j]
        for d in (4, 3, 5, 2, 6, 1, 7):
            if d < nz:
                to = lax.rem(z + d, nz) * nx + x
                send(yown.at[j], yx.at[j, z], z_send[j], z_recv[j], q, to)
        for k in range(1, RB):

            @pl.when(i == k)
            def _(k=k):
                @pl.loop(0, k * ns)
                def _(t):
                    send(
                        yown.at[j],
                        ycol.at[k - 1, j, :, own_lanes],
                        col_send[j],
                        col_recv[k - 1][j],
                        k * ns - 1 - t,
                        p,
                    )

        yx[j, z] = yown[j]

    def left_term(j, k, total):
        if j == 0:
            wait(at.at[k, pl.ds(0, (nx - 1) * nz * fw)], a5_recv[k - 1], "a5_%d" % k)
        wait(ycol.at[k - 1, j], col_recv[k - 1][j], "col_%d_%d" % (k, j))
        total[...] -= dot3(ycol[k - 1, j], at[k])

    def older_left_terms(j, total):
        for k in range(RB - 1, 1, -1):
            pl.when(k > i + 1)(functools.partial(left_term, j, k, total))

    def newest_left_term(j, total):
        for k in range(1, RB):
            pl.when(k == i + 1)(functools.partial(left_term, j, k, total))

    def scatter_x(part, arrived, send_sem, recv_sem):
        for d in (2, 1, 3):
            if d < nx:
                to = lax.rem(x + d, nx)
                send(part.at[to], arrived.at[x], send_sem, recv_sem, q, z * nx + to)

    def whole_of(ref, j):
        return ref[j].reshape(nz * fw, ew)

    def exchange(j):
        wpart[j] = dot3(qside[j].reshape(nx * fw, ew), whole_of(yx, j)).reshape(nx, fw, ew)
        dst = wrecv.at[j, x, :, own_lanes]

        @pl.loop(1, ns)
        def _(d):
            q_to = i * ns + lax.rem(s + d, ns)
            for x_to in range(nx):
                send(wpart.at[j, x_to], dst, w_send[j], w_recv[j], q_to, z * nx + x_to)

        for d in (2, 1, 3):
            if d < nx:
                to = lax.rem(x + d, nx)
                send(wpart.at[j, to], dst, w_send[j], w_recv[j], q, z * nx + to)
        keep(wpart.at[j, x], dst, w_recv[j])

    def last_product(j):
        wait(wrecv.at[j], w_recv[j], "wx_%d" % j)
        out[j] = dot3(jnp.sum(wrecv[j], axis=0), bases[...], ROW_BY_ROW)

    def pair_at(l, j):
        return j * (j - 1) // 2 + l

    def pass_pairs(j):
        for l in range(j):
            n = pair_at(l, j)

            @pl.when(core == (nq - 1 - n) % 2)
            def _(n=n):
                wait(lhs.at[n], b3_recv[n], "b3_%d" % n)
                send(lhs.at[n], lhs.at[n], b3_pass[n], b3_recv[n], partner, p)

        for l in range(j):
            n = pair_at(l, j)

            @pl.when(core != (nq - 1 - n) % 2)
            def _(n=n):
                wait(lhs.at[n], b3_recv[n], "b3_%d" % n)

    def right_term(l, j):
        return dot3(lhs[pair_at(l, j)].reshape(nx * fw, ew), whole_of(yx, l))

    def start_rows():
        wait(crecv.at[blocks[0]], c3_recv[0], "c3_0")
        acc[...] = jnp.sum(crecv[0], axis=0)

    @pl.when(top)
    def _():
        start_rows()
        finish(0)

    send_c3(1)

    @pl.when(top)
    def _():
        send_b3(0, own_pair[0])
        send_b1(1, own_pair[1])

    @pl.when(late_pair)
    def _():
        send_b1(0, own_pair[1])

    @pl.when(jnp.logical_not(top))
    def _():
        start_rows()
        older_left_terms(0, acc)
        newest_left_term(0, acc)
        finish(0)

    for j in range(1, FIRST):
        pend[j] = jnp.sum(crecv[j], axis=0)

    for j in range(CB):
        last = j + 1 == CB
        if j == 1:
            pl.when(top)(functools.partial(send_b2, 1))
            pl.when(late_pair)(functools.partial(send_b2, 0))
            wait(crecv.at[blocks[1]], c3_recv[1], "c3_1")
            for later in range(FIRST, CB):
                pend[later] = jnp.sum(crecv[later], axis=0)
        if j == 2:
            pl.when(top)(functools.partial(send_b3, 1, own_pair[1]))
        if not last:
            pass_pairs(j + 1)
            psum[...] = jnp.zeros_like(psum)
            for l in range(j):
                psum[...] += right_term(l, j + 1)
            older_left_terms(j + 1, pend.at[j + 1])
        if j >= 1:
            exchange(j - 1)
        if j >= 2:
            last_product(j - 2)
        if j == 2:
            pl.when(late_pair)(functools.partial(send_b3, 0, own_pair[1]))

        wait(yx.at[j, pl.ds(0, nz - 1)], z_recv[j], "z_%d" % j)
        if not last:
            xpart[j + 1] = (psum[...] + right_term(j, j + 1)).reshape(nx, fw, ew)
            scatter_x(xpart.at[j + 1], brecv.at[j + 1], x_send[j + 1], x_recv[j + 1])
            brecv[j + 1, x] = xpart[j + 1, x]
            newest_left_term(j + 1, pend.at[j + 1])
            wait(brecv.at[j + 1, pl.ds(0, nx - 1)], x_recv[j + 1], "x_%d" % (j + 1))
            acc[...] = pend[j + 1] - jnp.sum(brecv[j + 1], axis=0)
            finish(j + 1)

    exchange(CB - 1)
    last_product(CB - 2)
    last_product(CB - 1)

    for n in range(PAIRS):

        @pl.when(core == (nq - 1 - n) % 2)
        def _(n=n):
            wait(lhs.at[n], b3_pass[n])

    for c in range(2):
        wait(urecv.at[pl.ds(0, ns - 1), chunks[c]], c1_send[c])
        wait(ux.at[blocks[c], pl.ds(0, nx - 1)], c2_send[c])
        wait(qside.at[blocks[c], pl.ds(0, nx - 1)], q2_send[c])
        wait(crecv.at[blocks[c], pl.ds(0, nz - 1)], c3_send[c])
    for j in range(CB):
        wait(yx.at[j, pl.ds(0, nz - 1)], z_send[j])
        wait(at.at[0, pl.ds(0, (nx * ns - 1) * fw)], w_send[j])
        if j > 0:
            wait(brecv.at[j, pl.ds(0, nx - 1)], x_send[j])
        for k in range(1, RB):

            @pl.when(i == k)
            def _(k=k):
                wait(at.at[0, pl.ds(0, fw * k * ns)], col_send[j])

    for k in range(1, RB):

        @pl.when(k > i)
        def _(k=k):
            wait(at.at[k, pl.ds(0, (nz - 1) * fw)], a4_send[k - 1])
            wait(at.at[k, pl.ds(0, (nx - 1) * nz * fw)], a5_send[k - 1])

        @pl.when(jnp.logical_and(i == k, q == holder))
        def _(k=k):
            wait(at.at[pl.ds(0, k * ns * cww // (2 * ew))], a2_send)

    @pl.when(has_coupling)
    def _():
        wait(hrecv.at[pl.ds(0, ns - 1)], a1_send)
        wait(gpart.at[pl.ds(0, bs - fw)], a3_send)

        @pl.when(core == holder % 2)
        def _():
            wait(pk, a2_pass)

    def end_pair(r):
        wait(bx.at[r, pl.ds(0, (nx - 1) * fw)], b1_send[r])
        wait(qx.at[r, pl.ds(0, (nx - 1) * fw)], q1_send[r])
        wait(ql.at[r, pl.ds(0, bs - fw)], l1_send[r])
        wait(trecv.at[r, pl.ds(0, nz - 1)], b2_send[r])
        wait(at.at[0, pl.ds(0, (nq // 2 - 1) * nx * fw)], b3_send[r])

    @pl.when(top)
    def _():
        end_pair(0)
        end_pair(1)

    pl.when(late_pair)(functools.partial(end_pair, 0))


def shards(np_, nq, right_side, coupling, row_bases, row_values, column_bases, column_values, column_coupling):
    ns = nq // RB
    fw, ew = right_side.shape[1], right_side.shape[2]
    cww = coupling.shape[1]
    bs = row_bases.shape[1]
    nx = bs // ew
    nz = np_ // nx
    nw = bs // cww
    vmem = pl.BlockSpec(memory_space=pltpu.VMEM)
    scratch = (
        (ns, CB * fw, ew),
        (ns, CB * fw, ew),
        (CB, nx, fw, ew),
        (CB, fw, ew),
        (CB, nx, fw, ew),
        (CB, nz, fw, ew),
        (CB, nz, fw, ew),
        (ns, cww, ew),
        (ns, cww, ew),
        (cww, bs),
        (bs, ew),
        (RB - 1, nw, fw, ew),
        (RB - 1, fw, ew),
        (RB, bs, ew),
        (2, nx * fw, bs),
        (2, nx * fw, bs),
        (2, bs, ew),
        (2, nx, nz, fw, ew),
        (2, nz, nx, fw, ew),
        (2, nx, fw, ew),
        (PAIRS, nx, fw, ew),
        (CB, fw, ew),
        (CB, nz, fw, ew),
        (CB, nx, fw, ew),
        (CB, nx, fw, ew),
        (CB, nx, fw, ew),
        (CB, nx, fw, bs),
        (RB - 1, CB, fw, bs),
        (CB, fw, ew),
        (nx * fw, ew),
        (CB, fw, ew),
        (fw, ew),
    )
    return pl.pallas_call(
        functools.partial(kernel, np_, nq),
        out_shape=jax.ShapeDtypeStruct((CB, fw, ew), F32),
        in_specs=[vmem] * 7,
        out_specs=vmem,
        scratch_shapes=[pltpu.VMEM(shape, F32) for shape in scratch]
        + [pltpu.SemaphoreType.DMA((160,))],
        compiler_params=pltpu.CompilerParams(collective_id=0, has_side_effects=True),
    )(
        right_side,
        coupling.T,
        row_bases,
        row_values,
        column_bases,
        column_values,
        column_coupling,
    )


def solution(mesh):
    placed = (
        P(None, "pcol", "prow"),
        P("prow", "pcol"),
        P("prow", None),
        P(),
        P(None, "pcol", None),
        P(),
        P(None, "pcol", None),
    )
    body = functools.partial(shards, mesh.shape["pcol"], mesh.shape["prow"])
    return jax.shard_map(
        body, mesh=mesh, in_specs=placed, out_specs=P(None, "pcol", "prow"), check_vma=False
    )
```

```python
import functools

import jax
import jax.numpy as jnp
from jax import lax
from jax.experimental import pallas as pl
from jax.experimental.pallas import tpu as pltpu
from jax.sharding import PartitionSpec as P

RB = 4
CB = 6
PAIRS = CB * (CB - 1) // 2
FIRST = 2
MESH = pl.DeviceIdType.MESH
F32 = jnp.float32
BF16 = jnp.bfloat16
ROW_BY_COL = ((1,), (0,))
COL_BY_COL = ((0,), (0,))
ROW_BY_ROW = ((1,), (1,))


def halves(value):
    high = value.astype(BF16)
    low = (value - high.astype(F32)).astype(BF16)
    return high, low


def dot_of(left, right, dims):
    return lax.dot_general(left, right, (dims, ((), ())), preferred_element_type=F32)


def dot_split(left, right, dims):
    (left_high, left_low), (right_high, right_low) = left, right
    small = dot_of(left_low, right_high, dims) + dot_of(left_high, right_low, dims)
    return dot_of(left_high, right_high, dims) + small


def dot3(left, right, dims=ROW_BY_COL):
    return dot_split(halves(left), halves(right), dims)


def kernel(np_, nq, *refs):
    (rhs, coupling, bases, row_values, colbases, col_values, colcoup, out, *rest) = refs
    (upart, urecv, ux, uown, qside, vpart, crecv) = rest[:7]
    (hpart, hrecv, pk, gpart, grecv, apiece, at) = rest[7:14]
    (bx, qx, ql, tpart, trecv, tpiece, lhs) = rest[14:21]
    (yown, yx, xpart, brecv, wpart, wrecv) = rest[21:27]
    (ycol, pend, psum, den, acc, sems) = rest[27:]
    fw, ew = rhs.shape[1], rhs.shape[2]
    cww = coupling.shape[0]
    bs = fw * np_
    ns = nq // RB
    nx = bs // ew
    nz = np_ // nx
    nw = bs // cww
    per_row = ew // cww
    q = lax.axis_index("prow")
    p = lax.axis_index("pcol")
    i, s = q // ns, q % ns
    z, x = p // nx, p % nx
    core = q % 2
    partner = q + 1 - 2 * core
    k_own, w_own = p // nw, p % nw
    has_coupling = k_own > i
    top = i == RB - 1
    holder = p // per_row
    late_pair = jnp.logical_and(q > ns, q < nq - ns)

    used = [0]

    def new_sem(count=1):
        at_sem = used[0]
        used[0] += count
        return [sems.at[at_sem + n] for n in range(count)]

    z_send, z_recv, x_send, x_recv = new_sem(CB), new_sem(CB), new_sem(CB), new_sem(CB)
    w_send, w_recv, col_send = new_sem(CB), new_sem(CB), new_sem(CB)
    col_recv = [new_sem(CB) for _ in range(RB - 1)]
    c1_send, c1_recv, c2_send, c2_recv = new_sem(2), new_sem(2), new_sem(2), new_sem(2)
    c3_send, c3_recv, q2_send, q2_recv = new_sem(2), new_sem(2), new_sem(2), new_sem(2)
    a1_send, a1_recv, a2_send, a2_recv, a2_pass, a3_send = new_sem(6)
    a3_recv, a4_send, a4_recv = new_sem(RB - 1), new_sem(RB - 1), new_sem(RB - 1)
    a5_send, a5_recv = new_sem(RB - 1), new_sem(RB - 1)
    b1_send, b1_recv, q1_send, q1_recv = new_sem(2), new_sem(2), new_sem(2), new_sem(2)
    l1_send, l1_recv, b2_send, b2_recv = new_sem(2), new_sem(2), new_sem(2), new_sem(2)
    b3_send = new_sem(2)
    b3_pass = new_sem(PAIRS)
    b3_base = used[0]
    b3_recv = new_sem(PAIRS)

    def send(src, dst, send_sem, recv_sem, q_to, p_to):
        pltpu.make_async_remote_copy(
            src_ref=src,
            dst_ref=dst,
            send_sem=send_sem,
            recv_sem=recv_sem,
            device_id=(q_to, p_to),
            device_id_type=MESH,
        ).start()

    def keep(src, dst, recv_sem):
        pltpu.make_async_copy(src, dst, recv_sem).start()

    def send_or_keep(here, src, dst, send_sem, recv_sem, q_to, p_to):
        @pl.when(here)
        def _():
            keep(src, dst, recv_sem)

        @pl.when(jnp.logical_not(here))
        def _():
            send(src, dst, send_sem, recv_sem, q_to, p_to)

    def wait(ref, sem, name="w"):
        pltpu.make_async_copy(ref, ref, sem).wait()

    def rows_of(n, size):
        return pl.ds(pl.multiple_of(n * size, size), size)

    def to_columns(body):
        for start, stop in ((np_ // 2, np_), (1, np_ // 2)):

            @pl.loop(start, stop)
            def _(d):
                body(lax.rem(p + d, np_))

    def pair_of(n):
        j_own = 1
        for first in range(2, CB):
            j_own = j_own + (n >= first * (first - 1) // 2).astype(jnp.int32)
        return n - j_own * (j_own - 1) // 2, j_own

    own_pair = (nq - 1 - q, nq + ns - 1 - q)

    barrier = pltpu.get_barrier_semaphore()

    def greet(to):
        pl.semaphore_signal(barrier, inc=1, device_id=(q, to), device_id_type=MESH)

    to_columns(greet)

    @pl.loop(1, nq)
    def _(d):
        pl.semaphore_signal(
            barrier, inc=1, device_id=(lax.rem(q + d, nq), p), device_id_type=MESH
        )

    @pl.loop(1, ns)
    def _(d):
        q_to = i * ns + lax.rem(s + d, ns)
        for x_off in range(1, nx):
            to = z * nx + lax.rem(x + x_off, nx)
            pl.semaphore_signal(barrier, inc=1, device_id=(q_to, to), device_id_type=MESH)

    bases_split = halves(bases[...])
    inner = dot_split(halves(coupling[...]), bases_split, ROW_BY_COL)
    stacked = rhs[...].reshape(CB * fw, ew)
    first = dot_split(halves(stacked), bases_split, ROW_BY_COL)
    for n in range(ns):
        upart[n] = first[:, n * ew : (n + 1) * ew]
        hpart[n] = inner[:, n * ew : (n + 1) * ew]
    own_lanes = rows_of(s, ew)
    values = row_values[:, own_lanes]
    own_value = lax.broadcasted_iota(jnp.int32, values.shape, 0) == i
    eigen = jnp.sum(jnp.where(own_value, values, 0.0), axis=0, keepdims=True)
    lanes = lax.broadcasted_iota(jnp.int32, (fw, ew), 1)
    chosen = lanes == z * fw + lax.broadcasted_iota(jnp.int32, (fw, ew), 0)
    for j in range(CB):
        shifts = col_values[pl.ds(j, 1), rows_of(x, ew)]
        shift = jnp.sum(jnp.where(chosen, shifts, 0.0), axis=1, keepdims=True)
        den[j] = shift + eigen

    pl.semaphore_wait(barrier, np_ + nq - 2 + (ns - 1) * (nx - 1))

    chunks = (pl.ds(0, FIRST * fw), pl.ds(FIRST * fw, (CB - FIRST) * fw))
    blocks = (pl.ds(0, FIRST), pl.ds(FIRST, CB - FIRST))

    def send_c1(c):
        @pl.loop(0, ns)
        def _(t):
            src, dst = upart.at[t, chunks[c]], urecv.at[s, chunks[c]]
            send_or_keep(t == s, src, dst, c1_send[c], c1_recv[c], i * ns + t, p)

    def send_q2(c):
        @pl.loop(0, nx)
        def _(t):
            src, dst = colbases.at[blocks[c], :, rows_of(t, ew)], qside.at[blocks[c], x]
            send_or_keep(t == x, src, dst, q2_send[c], q2_recv[c], q, z * nx + t)

    def send_c2(c):
        wait(urecv.at[:, chunks[c]], c1_recv[c], "c1_%d" % c)
        count = (FIRST, CB - FIRST)[c]
        summed = jnp.sum(urecv[:, chunks[c]], axis=0)
        uown[blocks[c]] = summed.reshape(count, fw, ew)

        @pl.loop(0, nx)
        def _(t):
            src, dst = uown.at[blocks[c]], ux.at[blocks[c], x]
            send_or_keep(t == x, src, dst, c2_send[c], c2_recv[c], q, z * nx + t)

    def send_c3(c):
        wait(ux.at[blocks[c]], c2_recv[c], "c2_%d" % c)
        wait(qside.at[blocks[c]], q2_recv[c], "q2_%d" % c)
        for j in (range(FIRST), range(FIRST, CB))[c]:
            left = qside[j].reshape(nx * fw, ew)
            right = ux[j].reshape(nx * fw, ew)
            vpart[j] = dot3(left, right, COL_BY_COL).reshape(nz, fw, ew)

        @pl.loop(0, nz)
        def _(t):
            src, dst = vpart.at[blocks[c], t], crecv.at[blocks[c], z]
            send_or_keep(t == z, src, dst, c3_send[c], c3_recv[c], q, t * nx + x)

    def send_b1(r, n):
        l_own, j_own = pair_of(n)

        @pl.loop(0, nx)
        def _(t):
            src_b = colcoup.at[j_own, :, rows_of(l_own, bs)]
            src_q = colbases.at[j_own]
            dst_b, dst_q = bx.at[r, rows_of(x, fw)], qx.at[r, rows_of(x, fw)]
            to = z * nx + t
            send_or_keep(t == x, src_b, dst_b, b1_send[r], b1_recv[r], q, to)
            send_or_keep(t == x, src_q, dst_q, q1_send[r], q1_recv[r], q, to)

        dst = ql.at[r, rows_of(p, fw)]
        keep(colbases.at[l_own, :, rows_of(x, ew)], dst, l1_recv[r])

        def one(to):
            src = colbases.at[l_own, :, rows_of(lax.rem(to, nx), ew)]
            send(src, dst, l1_send[r], l1_recv[r], q, to)

        to_columns(one)

    def send_b2(r):
        wait(bx.at[r], b1_recv[r], "bx%d" % r)
        wait(qx.at[r], q1_recv[r], "qx%d" % r)
        wait(ql.at[r], l1_recv[r], "ql%d" % r)
        mixed = dot3(bx[r], ql[r])
        tpart[r] = dot3(qx[r], mixed, COL_BY_COL).reshape(nx, nz, fw, ew)

        @pl.loop(0, nz)
        def _(t):
            src, dst = tpart.at[r, :, t], trecv.at[r, z]
            send_or_keep(t == z, src, dst, b2_send[r], b2_recv[r], q, t * nx + x)

    def send_b3(r, n):
        wait(trecv.at[r], b2_recv[r], "b2%d" % r)
        tpiece[r] = jnp.sum(trecv[r], axis=0)
        dst, recv_sem = lhs.at[n], sems.at[b3_base + n]

        @pl.loop(0, nq // 2)
        def _(t):
            q_to = nq - 2 - 2 * t + core
            send_or_keep(q_to == q, tpiece.at[r], dst, b3_send[r], recv_sem, q_to, p)

    @pl.when(q == holder)
    def _():
        @pl.loop(0, i * ns // 2)
        def _(t):
            src = bases.at[rows_of(lax.rem(p, per_row), cww)]
            send(src, pk, a2_send, a2_recv, i * ns - 2 - 2 * t + core, p)

    @pl.when(has_coupling)
    def _():
        @pl.loop(0, ns)
        def _(t):
            send_or_keep(t == s, hpart.at[t], hrecv.at[s], a1_send, a1_recv, i * ns + t, p)

    send_c1(0)
    send_q2(0)

    @pl.when(top)
    def _():
        send_b1(0, own_pair[0])

    send_c1(1)
    send_q2(1)

    @pl.when(has_coupling)
    def _():
        wait(hrecv, a1_recv, "a1")
        wait(pk, a2_recv, "a2")

        @pl.when(core == holder % 2)
        def _():
            send(pk, pk, a2_pass, a2_recv, partner, p)

        gpart[...] = dot3(pk[...], jnp.sum(hrecv[...], axis=0), COL_BY_COL)
        for k in range(1, RB):

            @pl.when(k_own == k)
            def _(k=k):
                dst = grecv.at[k - 1, w_own]
                keep(gpart.at[rows_of(x * nz + z, fw)], dst, a3_recv[k - 1])

                def one(to):
                    order = lax.rem(to, nx) * nz + to // nx
                    send(gpart.at[rows_of(order, fw)], dst, a3_send, a3_recv[k - 1], q, to)

                to_columns(one)

    send_c2(0)
    send_c3(0)

    @pl.when(top)
    def _():
        send_b2(0)

    send_c2(1)

    for k in range(RB - 1, 0, -1):

        @pl.when(k > i)
        def _(k=k):
            wait(grecv.at[k - 1], a3_recv[k - 1], "a3_%d" % k)
            apiece[k - 1] = jnp.sum(grecv[k - 1], axis=0)
            dst = at.at[k, rows_of(x * nz + z, fw)]
            keep(apiece.at[k - 1], dst, a4_recv[k - 1])
            for d in (4, 3, 5, 2, 6, 1, 7):
                if d < nz:
                    to = lax.rem(z + d, nz) * nx + x
                    send(apiece.at[k - 1], dst, a4_send[k - 1], a4_recv[k - 1], q, to)

    for k in range(RB - 1, 0, -1):

        @pl.when(k > i)
        def _(k=k):
            half = at.at[k, rows_of(x, nz * fw)]
            wait(half, a4_recv[k - 1], "a4_%d" % k)
            for d in (2, 1, 3):
                if d < nx:
                    to = z * nx + lax.rem(x + d, nx)
                    send(half, half, a5_send[k - 1], a5_recv[k - 1], q, to)

    def finish(j):
        yown[j] = acc[...] / den[j]
        for d in (4, 3, 5, 2, 6, 1, 7):
            if d < nz:
                to = lax.rem(z + d, nz) * nx + x
                send(yown.at[j], yx.at[j, z], z_send[j], z_recv[j], q, to)
        for k in range(1, RB):

            @pl.when(i == k)
            def _(k=k):
                @pl.loop(0, k * ns)
                def _(t):
                    send(
                        yown.at[j],
                        ycol.at[k - 1, j, :, own_lanes],
                        col_send[j],
                        col_recv[k - 1][j],
                        k * ns - 1 - t,
                        p,
                    )

        yx[j, z] = yown[j]

    def left_term(j, k, total):
        if j == 0:
            wait(at.at[k, pl.ds(0, (nx - 1) * nz * fw)], a5_recv[k - 1], "a5_%d" % k)
        wait(ycol.at[k - 1, j], col_recv[k - 1][j], "col_%d_%d" % (k, j))
        total[...] -= dot3(ycol[k - 1, j], at[k])

    def older_left_terms(j, total):
        for k in range(RB - 1, 1, -1):
            pl.when(k > i + 1)(functools.partial(left_term, j, k, total))

    def newest_left_term(j, total):
        for k in range(1, RB):
            pl.when(k == i + 1)(functools.partial(left_term, j, k, total))

    def scatter_x(part, arrived, send_sem, recv_sem):
        for d in (2, 1, 3):
            if d < nx:
                to = lax.rem(x + d, nx)
                send(part.at[to], arrived.at[x], send_sem, recv_sem, q, z * nx + to)

    def whole_of(ref, j):
        return ref[j].reshape(nz * fw, ew)

    def exchange(j):
        wpart[j] = dot3(qside[j].reshape(nx * fw, ew), whole_of(yx, j)).reshape(nx, fw, ew)
        dst = wrecv.at[j, x, :, own_lanes]

        @pl.loop(1, ns)
        def _(d):
            q_to = i * ns + lax.rem(s + d, ns)
            for x_to in range(nx):
                send(wpart.at[j, x_to], dst, w_send[j], w_recv[j], q_to, z * nx + x_to)

        for d in (2, 1, 3):
            if d < nx:
                to = lax.rem(x + d, nx)
                send(wpart.at[j, to], dst, w_send[j], w_recv[j], q, z * nx + to)
        keep(wpart.at[j, x], dst, w_recv[j])

    def last_product(j):
        wait(wrecv.at[j], w_recv[j], "wx_%d" % j)
        out[j] = dot3(jnp.sum(wrecv[j], axis=0), bases[...], ROW_BY_ROW)

    def pair_at(l, j):
        return j * (j - 1) // 2 + l

    def pass_pairs(j):
        for l in range(j):
            n = pair_at(l, j)

            @pl.when(core == (nq - 1 - n) % 2)
            def _(n=n):
                wait(lhs.at[n], b3_recv[n], "b3_%d" % n)
                send(lhs.at[n], lhs.at[n], b3_pass[n], b3_recv[n], partner, p)

        for l in range(j):
            n = pair_at(l, j)

            @pl.when(core != (nq - 1 - n) % 2)
            def _(n=n):
                wait(lhs.at[n], b3_recv[n], "b3_%d" % n)

    def right_term(l, j):
        return dot3(lhs[pair_at(l, j)].reshape(nx * fw, ew), whole_of(yx, l))

    def start_rows():
        wait(crecv.at[blocks[0]], c3_recv[0], "c3_0")
        acc[...] = jnp.sum(crecv[0], axis=0)

    start_rows()
    older_left_terms(0, acc)
    newest_left_term(0, acc)
    finish(0)

    @pl.when(top)
    def _():
        send_b1(1, own_pair[1])

    send_c3(1)

    @pl.when(top)
    def _():
        send_b3(0, own_pair[0])

    @pl.when(late_pair)
    def _():
        send_b1(0, own_pair[1])

    for j in range(1, FIRST):
        pend[j] = jnp.sum(crecv[j], axis=0)

    for j in range(CB):
        last = j + 1 == CB
        if j == 1:
            pl.when(top)(functools.partial(send_b2, 1))
            pl.when(late_pair)(functools.partial(send_b2, 0))
        if j == 2:
            pl.when(top)(functools.partial(send_b3, 1, own_pair[1]))
        if not last:
            pass_pairs(j + 1)
            psum[...] = jnp.zeros_like(psum)
            for l in range(j):
                psum[...] += right_term(l, j + 1)
            if j + 1 != FIRST:
                older_left_terms(j + 1, pend.at[j + 1])
        if j >= 1:
            exchange(j - 1)
        if j >= 2:
            last_product(j - 2)
        if j == 2:
            pl.when(late_pair)(functools.partial(send_b3, 0, own_pair[1]))

        wait(yx.at[j, pl.ds(0, nz - 1)], z_recv[j], "z_%d" % j)
        if not last:
            xpart[j + 1] = (psum[...] + right_term(j, j + 1)).reshape(nx, fw, ew)
            scatter_x(xpart.at[j + 1], brecv.at[j + 1], x_send[j + 1], x_recv[j + 1])
            brecv[j + 1, x] = xpart[j + 1, x]
            if j + 1 == FIRST:
                wait(crecv.at[blocks[1]], c3_recv[1], "c3_1")
                for later in range(FIRST, CB):
                    pend[later] = jnp.sum(crecv[later], axis=0)
                older_left_terms(j + 1, pend.at[j + 1])
            newest_left_term(j + 1, pend.at[j + 1])
            wait(brecv.at[j + 1, pl.ds(0, nx - 1)], x_recv[j + 1], "x_%d" % (j + 1))
            acc[...] = pend[j + 1] - jnp.sum(brecv[j + 1], axis=0)
            finish(j + 1)

    exchange(CB - 1)
    last_product(CB - 2)
    last_product(CB - 1)

    for n in range(PAIRS):

        @pl.when(core == (nq - 1 - n) % 2)
        def _(n=n):
            wait(lhs.at[n], b3_pass[n])

    for c in range(2):
        wait(urecv.at[pl.ds(0, ns - 1), chunks[c]], c1_send[c])
        wait(ux.at[blocks[c], pl.ds(0, nx - 1)], c2_send[c])
        wait(qside.at[blocks[c], pl.ds(0, nx - 1)], q2_send[c])
        wait(crecv.at[blocks[c], pl.ds(0, nz - 1)], c3_send[c])
    for j in range(CB):
        wait(yx.at[j, pl.ds(0, nz - 1)], z_send[j])
        wait(at.at[0, pl.ds(0, (nx * ns - 1) * fw)], w_send[j])
        if j > 0:
            wait(brecv.at[j, pl.ds(0, nx - 1)], x_send[j])
        for k in range(1, RB):

            @pl.when(i == k)
            def _(k=k):
                wait(at.at[0, pl.ds(0, fw * k * ns)], col_send[j])

    for k in range(1, RB):

        @pl.when(k > i)
        def _(k=k):
            wait(at.at[k, pl.ds(0, (nz - 1) * fw)], a4_send[k - 1])
            wait(at.at[k, pl.ds(0, (nx - 1) * nz * fw)], a5_send[k - 1])

        @pl.when(jnp.logical_and(i == k, q == holder))
        def _(k=k):
            wait(at.at[pl.ds(0, k * ns * cww // (2 * ew))], a2_send)

    @pl.when(has_coupling)
    def _():
        wait(hrecv.at[pl.ds(0, ns - 1)], a1_send)
        wait(gpart.at[pl.ds(0, bs - fw)], a3_send)

        @pl.when(core == holder % 2)
        def _():
            wait(pk, a2_pass)

    def end_pair(r):
        wait(bx.at[r, pl.ds(0, (nx - 1) * fw)], b1_send[r])
        wait(qx.at[r, pl.ds(0, (nx - 1) * fw)], q1_send[r])
        wait(ql.at[r, pl.ds(0, bs - fw)], l1_send[r])
        wait(trecv.at[r, pl.ds(0, nz - 1)], b2_send[r])
        wait(at.at[0, pl.ds(0, (nq // 2 - 1) * nx * fw)], b3_send[r])

    @pl.when(top)
    def _():
        end_pair(0)
        end_pair(1)

    pl.when(late_pair)(functools.partial(end_pair, 0))


def shards(np_, nq, right_side, coupling, row_bases, row_values, column_bases, column_values, column_coupling):
    ns = nq // RB
    fw, ew = right_side.shape[1], right_side.shape[2]
    cww = coupling.shape[1]
    bs = row_bases.shape[1]
    nx = bs // ew
    nz = np_ // nx
    nw = bs // cww
    vmem = pl.BlockSpec(memory_space=pltpu.VMEM)
    scratch = (
        (ns, CB * fw, ew),
        (ns, CB * fw, ew),
        (CB, nx, fw, ew),
        (CB, fw, ew),
        (CB, nx, fw, ew),
        (CB, nz, fw, ew),
        (CB, nz, fw, ew),
        (ns, cww, ew),
        (ns, cww, ew),
        (cww, bs),
        (bs, ew),
        (RB - 1, nw, fw, ew),
        (RB - 1, fw, ew),
        (RB, bs, ew),
        (2, nx * fw, bs),
        (2, nx * fw, bs),
        (2, bs, ew),
        (2, nx, nz, fw, ew),
        (2, nz, nx, fw, ew),
        (2, nx, fw, ew),
        (PAIRS, nx, fw, ew),
        (CB, fw, ew),
        (CB, nz, fw, ew),
        (CB, nx, fw, ew),
        (CB, nx, fw, ew),
        (CB, nx, fw, ew),
        (CB, nx, fw, bs),
        (RB - 1, CB, fw, bs),
        (CB, fw, ew),
        (nx * fw, ew),
        (CB, fw, ew),
        (fw, ew),
    )
    return pl.pallas_call(
        functools.partial(kernel, np_, nq),
        out_shape=jax.ShapeDtypeStruct((CB, fw, ew), F32),
        in_specs=[vmem] * 7,
        out_specs=vmem,
        scratch_shapes=[pltpu.VMEM(shape, F32) for shape in scratch]
        + [pltpu.SemaphoreType.DMA((160,))],
        compiler_params=pltpu.CompilerParams(collective_id=0, has_side_effects=True),
    )(
        right_side,
        coupling.T,
        row_bases,
        row_values,
        column_bases,
        column_values,
        column_coupling,
    )


def solution(mesh):
    placed = (
        P(None, "pcol", "prow"),
        P("prow", "pcol"),
        P("prow", None),
        P(),
        P(None, "pcol", None),
        P(),
        P(None, "pcol", None),
    )
    body = functools.partial(shards, mesh.shape["pcol"], mesh.shape["prow"])
    return jax.shard_map(
        body, mesh=mesh, in_specs=placed, out_specs=P(None, "pcol", "prow"), check_vma=False
    )
```

```python
import functools

import jax
import jax.numpy as jnp
from jax import lax
from jax.experimental import pallas as pl
from jax.experimental.pallas import tpu as pltpu
from jax.sharding import PartitionSpec as P

RB = 4
CB = 6
PAIRS = CB * (CB - 1) // 2
FIRST = 2
MESH = pl.DeviceIdType.MESH
F32 = jnp.float32
BF16 = jnp.bfloat16
ROW_BY_COL = ((1,), (0,))
COL_BY_COL = ((0,), (0,))
ROW_BY_ROW = ((1,), (1,))


def halves(value):
    high = value.astype(BF16)
    low = (value - high.astype(F32)).astype(BF16)
    return high, low


def dot_of(left, right, dims):
    return lax.dot_general(left, right, (dims, ((), ())), preferred_element_type=F32)


def dot_split(left, right, dims):
    (left_high, left_low), (right_high, right_low) = left, right
    small = dot_of(left_low, right_high, dims) + dot_of(left_high, right_low, dims)
    return dot_of(left_high, right_high, dims) + small


def dot3(left, right, dims=ROW_BY_COL):
    return dot_split(halves(left), halves(right), dims)


def kernel(np_, nq, *refs):
    (rhs, coupling, bases, row_values, colbases, col_values, colcoup, out, *rest) = refs
    (upart, urecv, ux, uown, qside, vpart, crecv) = rest[:7]
    (hpart, hrecv, pk, gpart, grecv, apiece, at) = rest[7:14]
    (bx, qx, ql, tpart, trecv, tpiece, lhs) = rest[14:21]
    (yown, yx, xpart, brecv, wpart, wrecv) = rest[21:27]
    (ycol, pend, psum, den, acc, sems) = rest[27:]
    fw, ew = rhs.shape[1], rhs.shape[2]
    cww = coupling.shape[0]
    bs = fw * np_
    ns = nq // RB
    nx = bs // ew
    nz = np_ // nx
    nw = bs // cww
    per_row = ew // cww
    q = lax.axis_index("prow")
    p = lax.axis_index("pcol")
    i, s = q // ns, q % ns
    z, x = p // nx, p % nx
    core = q % 2
    partner = q + 1 - 2 * core
    k_own, w_own = p // nw, p % nw
    has_coupling = k_own > i
    top = i == RB - 1
    holder = p // per_row
    late_pair = jnp.logical_and(q > ns, q < nq - ns)

    used = [0]

    def new_sem(count=1):
        at_sem = used[0]
        used[0] += count
        return [sems.at[at_sem + n] for n in range(count)]

    z_send, z_recv, x_send, x_recv = new_sem(CB), new_sem(CB), new_sem(CB), new_sem(CB)
    w_send, w_recv, col_send = new_sem(CB), new_sem(CB), new_sem(CB)
    col_recv = [new_sem(CB) for _ in range(RB - 1)]
    c1_send, c1_recv, c2_send, c2_recv = new_sem(2), new_sem(2), new_sem(2), new_sem(2)
    c3_send, c3_recv, q2_send, q2_recv = new_sem(2), new_sem(2), new_sem(2), new_sem(2)
    a1_send, a1_recv, a2_send, a2_recv, a2_pass, a3_send = new_sem(6)
    a3_recv, a4_send, a4_recv = new_sem(RB - 1), new_sem(RB - 1), new_sem(RB - 1)
    a5_send, a5_recv = new_sem(RB - 1), new_sem(RB - 1)
    b1_send, b1_recv, q1_send, q1_recv = new_sem(2), new_sem(2), new_sem(2), new_sem(2)
    l1_send, l1_recv, b2_send, b2_recv = new_sem(2), new_sem(2), new_sem(2), new_sem(2)
    b3_send = new_sem(2)
    b3_pass = new_sem(PAIRS)
    b3_base = used[0]
    b3_recv = new_sem(PAIRS)

    def send(src, dst, send_sem, recv_sem, q_to, p_to):
        pltpu.make_async_remote_copy(
            src_ref=src,
            dst_ref=dst,
            send_sem=send_sem,
            recv_sem=recv_sem,
            device_id=(q_to, p_to),
            device_id_type=MESH,
        ).start()

    def keep(src, dst, recv_sem):
        pltpu.make_async_copy(src, dst, recv_sem).start()

    def send_or_keep(here, src, dst, send_sem, recv_sem, q_to, p_to):
        @pl.when(here)
        def _():
            keep(src, dst, recv_sem)

        @pl.when(jnp.logical_not(here))
        def _():
            send(src, dst, send_sem, recv_sem, q_to, p_to)

    def wait(ref, sem, name="w"):
        pltpu.make_async_copy(ref, ref, sem).wait()

    def rows_of(n, size):
        return pl.ds(pl.multiple_of(n * size, size), size)

    def to_columns(body):
        for start, stop in ((np_ // 2, np_), (1, np_ // 2)):

            @pl.loop(start, stop)
            def _(d):
                body(lax.rem(p + d, np_))

    def pair_of(n):
        j_own = 1
        for first in range(2, CB):
            j_own = j_own + (n >= first * (first - 1) // 2).astype(jnp.int32)
        return n - j_own * (j_own - 1) // 2, j_own

    own_pair = (nq - 1 - q, nq + ns - 1 - q)

    barrier = pltpu.get_barrier_semaphore()

    def greet(to):
        pl.semaphore_signal(barrier, inc=1, device_id=(q, to), device_id_type=MESH)

    to_columns(greet)

    @pl.loop(1, nq)
    def _(d):
        pl.semaphore_signal(
            barrier, inc=1, device_id=(lax.rem(q + d, nq), p), device_id_type=MESH
        )

    @pl.loop(1, ns)
    def _(d):
        q_to = i * ns + lax.rem(s + d, ns)
        for x_off in range(1, nx):
            to = z * nx + lax.rem(x + x_off, nx)
            pl.semaphore_signal(barrier, inc=1, device_id=(q_to, to), device_id_type=MESH)

    bases_split = halves(bases[...])
    inner = dot_split(halves(coupling[...]), bases_split, ROW_BY_COL)
    stacked = rhs[...].reshape(CB * fw, ew)
    first = dot_split(halves(stacked), bases_split, ROW_BY_COL)
    for n in range(ns):
        upart[n] = first[:, n * ew : (n + 1) * ew]
        hpart[n] = inner[:, n * ew : (n + 1) * ew]
    own_lanes = rows_of(s, ew)
    values = row_values[:, own_lanes]
    own_value = lax.broadcasted_iota(jnp.int32, values.shape, 0) == i
    eigen = jnp.sum(jnp.where(own_value, values, 0.0), axis=0, keepdims=True)
    lanes = lax.broadcasted_iota(jnp.int32, (fw, ew), 1)
    chosen = lanes == z * fw + lax.broadcasted_iota(jnp.int32, (fw, ew), 0)
    for j in range(CB):
        shifts = col_values[pl.ds(j, 1), rows_of(x, ew)]
        shift = jnp.sum(jnp.where(chosen, shifts, 0.0), axis=1, keepdims=True)
        den[j] = shift + eigen

    pl.semaphore_wait(barrier, np_ + nq - 2 + (ns - 1) * (nx - 1))

    chunks = (pl.ds(0, FIRST * fw), pl.ds(FIRST * fw, (CB - FIRST) * fw))
    blocks = (pl.ds(0, FIRST), pl.ds(FIRST, CB - FIRST))

    def send_c1(c):
        @pl.loop(0, ns)
        def _(t):
            src, dst = upart.at[t, chunks[c]], urecv.at[s, chunks[c]]
            send_or_keep(t == s, src, dst, c1_send[c], c1_recv[c], i * ns + t, p)

    def send_q2(c):
        @pl.loop(0, nx)
        def _(t):
            src, dst = colbases.at[blocks[c], :, rows_of(t, ew)], qside.at[blocks[c], x]
            send_or_keep(t == x, src, dst, q2_send[c], q2_recv[c], q, z * nx + t)

    def send_c2(c):
        wait(urecv.at[:, chunks[c]], c1_recv[c], "c1_%d" % c)
        count = (FIRST, CB - FIRST)[c]
        summed = jnp.sum(urecv[:, chunks[c]], axis=0)
        uown[blocks[c]] = summed.reshape(count, fw, ew)

        @pl.loop(0, nx)
        def _(t):
            src, dst = uown.at[blocks[c]], ux.at[blocks[c], x]
            send_or_keep(t == x, src, dst, c2_send[c], c2_recv[c], q, z * nx + t)

    def send_c3(c):
        wait(ux.at[blocks[c]], c2_recv[c], "c2_%d" % c)
        wait(qside.at[blocks[c]], q2_recv[c], "q2_%d" % c)
        for j in (range(FIRST), range(FIRST, CB))[c]:
            left = qside[j].reshape(nx * fw, ew)
            right = ux[j].reshape(nx * fw, ew)
            vpart[j] = dot3(left, right, COL_BY_COL).reshape(nz, fw, ew)

        @pl.loop(0, nz)
        def _(t):
            src, dst = vpart.at[blocks[c], t], crecv.at[blocks[c], z]
            send_or_keep(t == z, src, dst, c3_send[c], c3_recv[c], q, t * nx + x)

    def send_b1(r, n):
        l_own, j_own = pair_of(n)

        @pl.loop(0, nx)
        def _(t):
            src_b = colcoup.at[j_own, :, rows_of(l_own, bs)]
            src_q = colbases.at[j_own]
            dst_b, dst_q = bx.at[r, rows_of(x, fw)], qx.at[r, rows_of(x, fw)]
            to = z * nx + t
            send_or_keep(t == x, src_b, dst_b, b1_send[r], b1_recv[r], q, to)
            send_or_keep(t == x, src_q, dst_q, q1_send[r], q1_recv[r], q, to)

        dst = ql.at[r, rows_of(p, fw)]
        keep(colbases.at[l_own, :, rows_of(x, ew)], dst, l1_recv[r])

        def one(to):
            src = colbases.at[l_own, :, rows_of(lax.rem(to, nx), ew)]
            send(src, dst, l1_send[r], l1_recv[r], q, to)

        to_columns(one)

    def send_b2(r):
        wait(bx.at[r], b1_recv[r], "bx%d" % r)
        wait(qx.at[r], q1_recv[r], "qx%d" % r)
        wait(ql.at[r], l1_recv[r], "ql%d" % r)
        mixed = dot3(bx[r], ql[r])
        tpart[r] = dot3(qx[r], mixed, COL_BY_COL).reshape(nx, nz, fw, ew)

        @pl.loop(0, nz)
        def _(t):
            src, dst = tpart.at[r, :, t], trecv.at[r, z]
            send_or_keep(t == z, src, dst, b2_send[r], b2_recv[r], q, t * nx + x)

    def send_b3(r, n):
        wait(trecv.at[r], b2_recv[r], "b2%d" % r)
        tpiece[r] = jnp.sum(trecv[r], axis=0)
        dst, recv_sem = lhs.at[n], sems.at[b3_base + n]

        @pl.loop(0, nq // 2)
        def _(t):
            q_to = nq - 2 - 2 * t + core
            send_or_keep(q_to == q, tpiece.at[r], dst, b3_send[r], recv_sem, q_to, p)

    @pl.when(q == holder)
    def _():
        @pl.loop(0, i * ns // 2)
        def _(t):
            src = bases.at[rows_of(lax.rem(p, per_row), cww)]
            send(src, pk, a2_send, a2_recv, i * ns - 2 - 2 * t + core, p)

    @pl.when(has_coupling)
    def _():
        @pl.loop(0, ns)
        def _(t):
            send_or_keep(t == s, hpart.at[t], hrecv.at[s], a1_send, a1_recv, i * ns + t, p)

    send_c1(0)
    send_q2(0)

    @pl.when(top)
    def _():
        send_b1(0, own_pair[0])

    send_c1(1)
    send_q2(1)

    @pl.when(has_coupling)
    def _():
        wait(hrecv, a1_recv, "a1")
        wait(pk, a2_recv, "a2")

        @pl.when(core == holder % 2)
        def _():
            send(pk, pk, a2_pass, a2_recv, partner, p)

        gpart[...] = dot3(pk[...], jnp.sum(hrecv[...], axis=0), COL_BY_COL)
        for k in range(1, RB):

            @pl.when(k_own == k)
            def _(k=k):
                dst = grecv.at[k - 1, w_own]
                keep(gpart.at[rows_of(x * nz + z, fw)], dst, a3_recv[k - 1])

                def one(to):
                    order = lax.rem(to, nx) * nz + to // nx
                    send(gpart.at[rows_of(order, fw)], dst, a3_send, a3_recv[k - 1], q, to)

                to_columns(one)

    send_c2(0)
    send_c3(0)

    @pl.when(top)
    def _():
        send_b2(0)

    send_c2(1)

    for k in range(RB - 1, 0, -1):

        @pl.when(k > i)
        def _(k=k):
            wait(grecv.at[k - 1], a3_recv[k - 1], "a3_%d" % k)
            apiece[k - 1] = jnp.sum(grecv[k - 1], axis=0)
            dst = at.at[k, rows_of(x * nz + z, fw)]
            keep(apiece.at[k - 1], dst, a4_recv[k - 1])
            for d in (4, 3, 5, 2, 6, 1, 7):
                if d < nz:
                    to = lax.rem(z + d, nz) * nx + x
                    send(apiece.at[k - 1], dst, a4_send[k - 1], a4_recv[k - 1], q, to)

    for k in range(RB - 1, 0, -1):

        @pl.when(k > i)
        def _(k=k):
            half = at.at[k, rows_of(x, nz * fw)]
            wait(half, a4_recv[k - 1], "a4_%d" % k)
            for d in (2, 1, 3):
                if d < nx:
                    to = z * nx + lax.rem(x + d, nx)
                    send(half, half, a5_send[k - 1], a5_recv[k - 1], q, to)

    def finish(j):
        yown[j] = acc[...] / den[j]
        for d in (4, 3, 5, 2, 6, 1, 7):
            if d < nz:
                to = lax.rem(z + d, nz) * nx + x
                send(yown.at[j], yx.at[j, z], z_send[j], z_recv[j], q, to)
        for k in range(1, RB):

            @pl.when(i == k)
            def _(k=k):
                @pl.loop(0, k * ns)
                def _(t):
                    send(
                        yown.at[j],
                        ycol.at[k - 1, j, :, own_lanes],
                        col_send[j],
                        col_recv[k - 1][j],
                        k * ns - 1 - t,
                        p,
                    )

        yx[j, z] = yown[j]

    def left_term(j, k, total):
        if j == 0:
            wait(at.at[k, pl.ds(0, (nx - 1) * nz * fw)], a5_recv[k - 1], "a5_%d" % k)
        wait(ycol.at[k - 1, j], col_recv[k - 1][j], "col_%d_%d" % (k, j))
        total[...] -= dot3(ycol[k - 1, j], at[k])

    def older_left_terms(j, total):
        for k in range(RB - 1, 1, -1):
            pl.when(k > i + 1)(functools.partial(left_term, j, k, total))

    def newest_left_term(j, total):
        for k in range(1, RB):
            pl.when(k == i + 1)(functools.partial(left_term, j, k, total))

    def scatter_x(part, arrived, send_sem, recv_sem):
        for d in (2, 1, 3):
            if d < nx:
                to = lax.rem(x + d, nx)
                send(part.at[to], arrived.at[x], send_sem, recv_sem, q, z * nx + to)

    def whole_of(ref, j):
        return ref[j].reshape(nz * fw, ew)

    def exchange(j):
        wpart[j] = dot3(qside[j].reshape(nx * fw, ew), whole_of(yx, j)).reshape(nx, fw, ew)
        dst = wrecv.at[j, x, :, own_lanes]

        @pl.loop(1, ns)
        def _(d):
            q_to = i * ns + lax.rem(s + d, ns)
            for x_to in range(nx):
                send(wpart.at[j, x_to], dst, w_send[j], w_recv[j], q_to, z * nx + x_to)

        for d in (2, 1, 3):
            if d < nx:
                to = lax.rem(x + d, nx)
                send(wpart.at[j, to], dst, w_send[j], w_recv[j], q, z * nx + to)
        keep(wpart.at[j, x], dst, w_recv[j])

    def last_product(j):
        wait(wrecv.at[j], w_recv[j], "wx_%d" % j)
        out[j] = dot3(jnp.sum(wrecv[j], axis=0), bases[...], ROW_BY_ROW)

    def pair_at(l, j):
        return j * (j - 1) // 2 + l

    def pass_pairs(j):
        for l in range(j):
            n = pair_at(l, j)

            @pl.when(core == (nq - 1 - n) % 2)
            def _(n=n):
                wait(lhs.at[n], b3_recv[n], "b3_%d" % n)
                send(lhs.at[n], lhs.at[n], b3_pass[n], b3_recv[n], partner, p)

        for l in range(j):
            n = pair_at(l, j)

            @pl.when(core != (nq - 1 - n) % 2)
            def _(n=n):
                wait(lhs.at[n], b3_recv[n], "b3_%d" % n)

    def right_term(l, j):
        return dot3(lhs[pair_at(l, j)].reshape(nx * fw, ew), whole_of(yx, l))

    def start_rows():
        wait(crecv.at[blocks[0]], c3_recv[0], "c3_0")
        acc[...] = jnp.sum(crecv[0], axis=0)

    start_rows()
    older_left_terms(0, acc)
    newest_left_term(0, acc)
    finish(0)

    @pl.when(top)
    def _():
        send_b1(1, own_pair[1])

    send_c3(1)

    @pl.when(top)
    def _():
        send_b3(0, own_pair[0])

    @pl.when(late_pair)
    def _():
        send_b1(0, own_pair[1])

    for j in range(1, FIRST):
        pend[j] = jnp.sum(crecv[j], axis=0)

    for j in range(CB):
        last = j + 1 == CB
        if j == 1:
            pl.when(top)(functools.partial(send_b2, 1))
        if j == 2:
            pl.when(top)(functools.partial(send_b3, 1, own_pair[1]))
        if not last:
            pass_pairs(j + 1)
            psum[...] = jnp.zeros_like(psum)
            for l in range(j):
                psum[...] += right_term(l, j + 1)
            if j + 1 != FIRST:
                older_left_terms(j + 1, pend.at[j + 1])
        if j >= 1:
            exchange(j - 1)
        if j >= 2:
            last_product(j - 2)

        wait(yx.at[j, pl.ds(0, nz - 1)], z_recv[j], "z_%d" % j)
        if not last:
            xpart[j + 1] = (psum[...] + right_term(j, j + 1)).reshape(nx, fw, ew)
            scatter_x(xpart.at[j + 1], brecv.at[j + 1], x_send[j + 1], x_recv[j + 1])
            brecv[j + 1, x] = xpart[j + 1, x]
            if j == 1:
                pl.when(late_pair)(functools.partial(send_b2, 0))
            if j == 2:
                pl.when(late_pair)(functools.partial(send_b3, 0, own_pair[1]))
            if j + 1 == FIRST:
                wait(crecv.at[blocks[1]], c3_recv[1], "c3_1")
                for later in range(FIRST, CB):
                    pend[later] = jnp.sum(crecv[later], axis=0)
                older_left_terms(j + 1, pend.at[j + 1])
            newest_left_term(j + 1, pend.at[j + 1])
            wait(brecv.at[j + 1, pl.ds(0, nx - 1)], x_recv[j + 1], "x_%d" % (j + 1))
            acc[...] = pend[j + 1] - jnp.sum(brecv[j + 1], axis=0)
            finish(j + 1)

    exchange(CB - 1)
    last_product(CB - 2)
    last_product(CB - 1)

    for n in range(PAIRS):

        @pl.when(core == (nq - 1 - n) % 2)
        def _(n=n):
            wait(lhs.at[n], b3_pass[n])

    for c in range(2):
        wait(urecv.at[pl.ds(0, ns - 1), chunks[c]], c1_send[c])
        wait(ux.at[blocks[c], pl.ds(0, nx - 1)], c2_send[c])
        wait(qside.at[blocks[c], pl.ds(0, nx - 1)], q2_send[c])
        wait(crecv.at[blocks[c], pl.ds(0, nz - 1)], c3_send[c])
    for j in range(CB):
        wait(yx.at[j, pl.ds(0, nz - 1)], z_send[j])
        wait(at.at[0, pl.ds(0, (nx * ns - 1) * fw)], w_send[j])
        if j > 0:
            wait(brecv.at[j, pl.ds(0, nx - 1)], x_send[j])
        for k in range(1, RB):

            @pl.when(i == k)
            def _(k=k):
                wait(at.at[0, pl.ds(0, fw * k * ns)], col_send[j])

    for k in range(1, RB):

        @pl.when(k > i)
        def _(k=k):
            wait(at.at[k, pl.ds(0, (nz - 1) * fw)], a4_send[k - 1])
            wait(at.at[k, pl.ds(0, (nx - 1) * nz * fw)], a5_send[k - 1])

        @pl.when(jnp.logical_and(i == k, q == holder))
        def _(k=k):
            wait(at.at[pl.ds(0, k * ns * cww // (2 * ew))], a2_send)

    @pl.when(has_coupling)
    def _():
        wait(hrecv.at[pl.ds(0, ns - 1)], a1_send)
        wait(gpart.at[pl.ds(0, bs - fw)], a3_send)

        @pl.when(core == holder % 2)
        def _():
            wait(pk, a2_pass)

    def end_pair(r):
        wait(bx.at[r, pl.ds(0, (nx - 1) * fw)], b1_send[r])
        wait(qx.at[r, pl.ds(0, (nx - 1) * fw)], q1_send[r])
        wait(ql.at[r, pl.ds(0, bs - fw)], l1_send[r])
        wait(trecv.at[r, pl.ds(0, nz - 1)], b2_send[r])
        wait(at.at[0, pl.ds(0, (nq // 2 - 1) * nx * fw)], b3_send[r])

    @pl.when(top)
    def _():
        end_pair(0)
        end_pair(1)

    pl.when(late_pair)(functools.partial(end_pair, 0))


def shards(np_, nq, right_side, coupling, row_bases, row_values, column_bases, column_values, column_coupling):
    ns = nq // RB
    fw, ew = right_side.shape[1], right_side.shape[2]
    cww = coupling.shape[1]
    bs = row_bases.shape[1]
    nx = bs // ew
    nz = np_ // nx
    nw = bs // cww
    vmem = pl.BlockSpec(memory_space=pltpu.VMEM)
    scratch = (
        (ns, CB * fw, ew),
        (ns, CB * fw, ew),
        (CB, nx, fw, ew),
        (CB, fw, ew),
        (CB, nx, fw, ew),
        (CB, nz, fw, ew),
        (CB, nz, fw, ew),
        (ns, cww, ew),
        (ns, cww, ew),
        (cww, bs),
        (bs, ew),
        (RB - 1, nw, fw, ew),
        (RB - 1, fw, ew),
        (RB, bs, ew),
        (2, nx * fw, bs),
        (2, nx * fw, bs),
        (2, bs, ew),
        (2, nx, nz, fw, ew),
        (2, nz, nx, fw, ew),
        (2, nx, fw, ew),
        (PAIRS, nx, fw, ew),
        (CB, fw, ew),
        (CB, nz, fw, ew),
        (CB, nx, fw, ew),
        (CB, nx, fw, ew),
        (CB, nx, fw, ew),
        (CB, nx, fw, bs),
        (RB - 1, CB, fw, bs),
        (CB, fw, ew),
        (nx * fw, ew),
        (CB, fw, ew),
        (fw, ew),
    )
    return pl.pallas_call(
        functools.partial(kernel, np_, nq),
        out_shape=jax.ShapeDtypeStruct((CB, fw, ew), F32),
        in_specs=[vmem] * 7,
        out_specs=vmem,
        scratch_shapes=[pltpu.VMEM(shape, F32) for shape in scratch]
        + [pltpu.SemaphoreType.DMA((160,))],
        compiler_params=pltpu.CompilerParams(collective_id=0, has_side_effects=True),
    )(
        right_side,
        coupling.T,
        row_bases,
        row_values,
        column_bases,
        column_values,
        column_coupling,
    )


def solution(mesh):
    placed = (
        P(None, "pcol", "prow"),
        P("prow", "pcol"),
        P("prow", None),
        P(),
        P(None, "pcol", None),
        P(),
        P(None, "pcol", None),
    )
    body = functools.partial(shards, mesh.shape["pcol"], mesh.shape["prow"])
    return jax.shard_map(
        body, mesh=mesh, in_specs=placed, out_specs=P(None, "pcol", "prow"), check_vma=False
    )
```

```python
import functools

import jax
import jax.numpy as jnp
from jax import lax
from jax.experimental import pallas as pl
from jax.experimental.pallas import tpu as pltpu
from jax.sharding import PartitionSpec as P

RB = 4
CB = 6
PAIRS = CB * (CB - 1) // 2
FIRST = 2
MESH = pl.DeviceIdType.MESH
F32 = jnp.float32
BF16 = jnp.bfloat16
ROW_BY_COL = ((1,), (0,))
COL_BY_COL = ((0,), (0,))
ROW_BY_ROW = ((1,), (1,))


def halves(value):
    high = value.astype(BF16)
    low = (value - high.astype(F32)).astype(BF16)
    return high, low


def dot_of(left, right, dims):
    return lax.dot_general(left, right, (dims, ((), ())), preferred_element_type=F32)


def dot_split(left, right, dims):
    (left_high, left_low), (right_high, right_low) = left, right
    small = dot_of(left_low, right_high, dims) + dot_of(left_high, right_low, dims)
    return dot_of(left_high, right_high, dims) + small


def dot3(left, right, dims=ROW_BY_COL):
    return dot_split(halves(left), halves(right), dims)


def kernel(np_, nq, *refs):
    (rhs, coupling, bases, row_values, colbases, col_values, colcoup, out, *rest) = refs
    (upart, urecv, ux, uown, qside, vpart, crecv) = rest[:7]
    (hpart, hrecv, pk, gpart, grecv, apiece, at) = rest[7:14]
    (bx, qx, ql, tpart, trecv, tpiece, lhs) = rest[14:21]
    (yown, yx, xpart, brecv, wpart, wrecv) = rest[21:27]
    (ycol, pend, psum, den, acc, sems) = rest[27:]
    fw, ew = rhs.shape[1], rhs.shape[2]
    cww = coupling.shape[0]
    bs = fw * np_
    ns = nq // RB
    nx = bs // ew
    nz = np_ // nx
    nw = bs // cww
    per_row = ew // cww
    q = lax.axis_index("prow")
    p = lax.axis_index("pcol")
    i, s = q // ns, q % ns
    z, x = p // nx, p % nx
    core = q % 2
    partner = q + 1 - 2 * core
    k_own, w_own = p // nw, p % nw
    has_coupling = k_own > i
    top = i == RB - 1
    holder = p // per_row
    late_pair = jnp.logical_and(q > ns, q < nq - ns)

    used = [0]

    def new_sem(count=1):
        at_sem = used[0]
        used[0] += count
        return [sems.at[at_sem + n] for n in range(count)]

    z_send, z_recv, x_send, x_recv = new_sem(CB), new_sem(CB), new_sem(CB), new_sem(CB)
    w_send, w_recv, col_send = new_sem(CB), new_sem(CB), new_sem(CB)
    col_recv = [new_sem(CB) for _ in range(RB - 1)]
    c1_send, c1_recv, c2_send, c2_recv = new_sem(2), new_sem(2), new_sem(2), new_sem(2)
    c3_send, c3_recv, q2_send, q2_recv = new_sem(2), new_sem(2), new_sem(2), new_sem(2)
    a1_send, a1_recv, a2_send, a2_recv, a2_pass, a3_send = new_sem(6)
    a3_recv, a4_send, a4_recv = new_sem(RB - 1), new_sem(RB - 1), new_sem(RB - 1)
    a5_send, a5_recv = new_sem(RB - 1), new_sem(RB - 1)
    b1_send, b1_recv, q1_send, q1_recv = new_sem(2), new_sem(2), new_sem(2), new_sem(2)
    l1_send, l1_recv, b2_send, b2_recv = new_sem(2), new_sem(2), new_sem(2), new_sem(2)
    b3_send = new_sem(2)
    b3_pass = new_sem(PAIRS)
    b3_base = used[0]
    b3_recv = new_sem(PAIRS)

    def send(src, dst, send_sem, recv_sem, q_to, p_to):
        pltpu.make_async_remote_copy(
            src_ref=src,
            dst_ref=dst,
            send_sem=send_sem,
            recv_sem=recv_sem,
            device_id=(q_to, p_to),
            device_id_type=MESH,
        ).start()

    def keep(src, dst, recv_sem):
        pltpu.make_async_copy(src, dst, recv_sem).start()

    def send_or_keep(here, src, dst, send_sem, recv_sem, q_to, p_to):
        @pl.when(here)
        def _():
            keep(src, dst, recv_sem)

        @pl.when(jnp.logical_not(here))
        def _():
            send(src, dst, send_sem, recv_sem, q_to, p_to)

    def wait(ref, sem, name="w"):
        pltpu.make_async_copy(ref, ref, sem).wait()

    def rows_of(n, size):
        return pl.ds(pl.multiple_of(n * size, size), size)

    def to_columns(body):
        for start, stop in ((np_ // 2, np_), (1, np_ // 2)):

            @pl.loop(start, stop)
            def _(d):
                body(lax.rem(p + d, np_))

    def pair_of(n):
        j_own = 1
        for first in range(2, CB):
            j_own = j_own + (n >= first * (first - 1) // 2).astype(jnp.int32)
        return n - j_own * (j_own - 1) // 2, j_own

    own_pair = (nq - 1 - q, nq + ns - 1 - q)

    barrier = pltpu.get_barrier_semaphore()

    def greet(to):
        pl.semaphore_signal(barrier, inc=1, device_id=(q, to), device_id_type=MESH)

    to_columns(greet)

    @pl.loop(1, nq)
    def _(d):
        pl.semaphore_signal(
            barrier, inc=1, device_id=(lax.rem(q + d, nq), p), device_id_type=MESH
        )

    @pl.loop(1, ns)
    def _(d):
        q_to = i * ns + lax.rem(s + d, ns)
        for x_off in range(1, nx):
            to = z * nx + lax.rem(x + x_off, nx)
            pl.semaphore_signal(barrier, inc=1, device_id=(q_to, to), device_id_type=MESH)

    bases_split = halves(bases[...])
    inner = dot_split(halves(coupling[...]), bases_split, ROW_BY_COL)
    stacked = rhs[...].reshape(CB * fw, ew)
    first = dot_split(halves(stacked), bases_split, ROW_BY_COL)
    for n in range(ns):
        upart[n] = first[:, n * ew : (n + 1) * ew]
        hpart[n] = inner[:, n * ew : (n + 1) * ew]
    own_lanes = rows_of(s, ew)
    values = row_values[:, own_lanes]
    own_value = lax.broadcasted_iota(jnp.int32, values.shape, 0) == i
    eigen = jnp.sum(jnp.where(own_value, values, 0.0), axis=0, keepdims=True)
    lanes = lax.broadcasted_iota(jnp.int32, (fw, ew), 1)
    chosen = lanes == z * fw + lax.broadcasted_iota(jnp.int32, (fw, ew), 0)
    for j in range(CB):
        shifts = col_values[pl.ds(j, 1), rows_of(x, ew)]
        shift = jnp.sum(jnp.where(chosen, shifts, 0.0), axis=1, keepdims=True)
        den[j] = shift + eigen

    pl.semaphore_wait(barrier, np_ + nq - 2 + (ns - 1) * (nx - 1))

    chunks = (pl.ds(0, FIRST * fw), pl.ds(FIRST * fw, (CB - FIRST) * fw))
    blocks = (pl.ds(0, FIRST), pl.ds(FIRST, CB - FIRST))

    def send_c1(c):
        @pl.loop(0, ns)
        def _(t):
            src, dst = upart.at[t, chunks[c]], urecv.at[s, chunks[c]]
            send_or_keep(t == s, src, dst, c1_send[c], c1_recv[c], i * ns + t, p)

    def send_q2(c):
        @pl.loop(0, nx)
        def _(t):
            src, dst = colbases.at[blocks[c], :, rows_of(t, ew)], qside.at[blocks[c], x]
            send_or_keep(t == x, src, dst, q2_send[c], q2_recv[c], q, z * nx + t)

    def send_c2(c):
        wait(urecv.at[:, chunks[c]], c1_recv[c], "c1_%d" % c)
        count = (FIRST, CB - FIRST)[c]
        summed = jnp.sum(urecv[:, chunks[c]], axis=0)
        uown[blocks[c]] = summed.reshape(count, fw, ew)

        @pl.loop(0, nx)
        def _(t):
            src, dst = uown.at[blocks[c]], ux.at[blocks[c], x]
            send_or_keep(t == x, src, dst, c2_send[c], c2_recv[c], q, z * nx + t)

    def send_c3(c):
        wait(ux.at[blocks[c]], c2_recv[c], "c2_%d" % c)
        wait(qside.at[blocks[c]], q2_recv[c], "q2_%d" % c)
        for j in (range(FIRST), range(FIRST, CB))[c]:
            left = qside[j].reshape(nx * fw, ew)
            right = ux[j].reshape(nx * fw, ew)
            vpart[j] = dot3(left, right, COL_BY_COL).reshape(nz, fw, ew)

        @pl.loop(0, nz)
        def _(t):
            src, dst = vpart.at[blocks[c], t], crecv.at[blocks[c], z]
            send_or_keep(t == z, src, dst, c3_send[c], c3_recv[c], q, t * nx + x)

    def send_b1(r, n):
        l_own, j_own = pair_of(n)

        @pl.loop(0, nx)
        def _(t):
            src_b = colcoup.at[j_own, :, rows_of(l_own, bs)]
            src_q = colbases.at[j_own]
            dst_b, dst_q = bx.at[r, rows_of(x, fw)], qx.at[r, rows_of(x, fw)]
            to = z * nx + t
            send_or_keep(t == x, src_b, dst_b, b1_send[r], b1_recv[r], q, to)
            send_or_keep(t == x, src_q, dst_q, q1_send[r], q1_recv[r], q, to)

        dst = ql.at[r, rows_of(p, fw)]
        keep(colbases.at[l_own, :, rows_of(x, ew)], dst, l1_recv[r])

        def one(to):
            src = colbases.at[l_own, :, rows_of(lax.rem(to, nx), ew)]
            send(src, dst, l1_send[r], l1_recv[r], q, to)

        to_columns(one)

    def send_b2(r):
        wait(bx.at[r], b1_recv[r], "bx%d" % r)
        wait(qx.at[r], q1_recv[r], "qx%d" % r)
        wait(ql.at[r], l1_recv[r], "ql%d" % r)
        mixed = dot3(bx[r], ql[r])
        tpart[r] = dot3(qx[r], mixed, COL_BY_COL).reshape(nx, nz, fw, ew)

        @pl.loop(0, nz)
        def _(t):
            src, dst = tpart.at[r, :, t], trecv.at[r, z]
            send_or_keep(t == z, src, dst, b2_send[r], b2_recv[r], q, t * nx + x)

    def send_b3(r, n):
        wait(trecv.at[r], b2_recv[r], "b2%d" % r)
        tpiece[r] = jnp.sum(trecv[r], axis=0)
        dst, recv_sem = lhs.at[n], sems.at[b3_base + n]

        @pl.loop(0, nq // 2)
        def _(t):
            q_to = nq - 2 - 2 * t + core
            send_or_keep(q_to == q, tpiece.at[r], dst, b3_send[r], recv_sem, q_to, p)

    @pl.when(q == holder)
    def _():
        @pl.loop(0, i * ns // 2)
        def _(t):
            src = bases.at[rows_of(lax.rem(p, per_row), cww)]
            send(src, pk, a2_send, a2_recv, i * ns - 2 - 2 * t + core, p)

    @pl.when(has_coupling)
    def _():
        @pl.loop(0, ns)
        def _(t):
            send_or_keep(t == s, hpart.at[t], hrecv.at[s], a1_send, a1_recv, i * ns + t, p)

    send_c1(0)
    send_q2(0)

    @pl.when(top)
    def _():
        send_b1(0, own_pair[0])

    send_c1(1)
    send_q2(1)

    @pl.when(has_coupling)
    def _():
        wait(hrecv, a1_recv, "a1")
        wait(pk, a2_recv, "a2")

        @pl.when(core == holder % 2)
        def _():
            send(pk, pk, a2_pass, a2_recv, partner, p)

        gpart[...] = dot3(pk[...], jnp.sum(hrecv[...], axis=0), COL_BY_COL)
        for k in range(1, RB):

            @pl.when(k_own == k)
            def _(k=k):
                dst = grecv.at[k - 1, w_own]
                keep(gpart.at[rows_of(x * nz + z, fw)], dst, a3_recv[k - 1])

                def one(to):
                    order = lax.rem(to, nx) * nz + to // nx
                    send(gpart.at[rows_of(order, fw)], dst, a3_send, a3_recv[k - 1], q, to)

                to_columns(one)

    send_c2(0)
    send_c3(0)

    @pl.when(top)
    def _():
        send_b2(0)

    send_c2(1)

    for k in range(RB - 1, 0, -1):

        @pl.when(k > i)
        def _(k=k):
            wait(grecv.at[k - 1], a3_recv[k - 1], "a3_%d" % k)
            apiece[k - 1] = jnp.sum(grecv[k - 1], axis=0)
            dst = at.at[k, rows_of(x * nz + z, fw)]
            keep(apiece.at[k - 1], dst, a4_recv[k - 1])
            for d in (4, 3, 5, 2, 6, 1, 7):
                if d < nz:
                    to = lax.rem(z + d, nz) * nx + x
                    send(apiece.at[k - 1], dst, a4_send[k - 1], a4_recv[k - 1], q, to)

    for k in range(RB - 1, 0, -1):

        @pl.when(k > i)
        def _(k=k):
            half = at.at[k, rows_of(x, nz * fw)]
            wait(half, a4_recv[k - 1], "a4_%d" % k)
            for d in (2, 1, 3):
                if d < nx:
                    to = z * nx + lax.rem(x + d, nx)
                    send(half, half, a5_send[k - 1], a5_recv[k - 1], q, to)

    def finish(j):
        yown[j] = acc[...] / den[j]
        for d in (4, 3, 5, 2, 6, 1, 7):
            if d < nz:
                to = lax.rem(z + d, nz) * nx + x
                send(yown.at[j], yx.at[j, z], z_send[j], z_recv[j], q, to)
        for k in range(1, RB):

            @pl.when(i == k)
            def _(k=k):
                @pl.loop(0, k * ns)
                def _(t):
                    send(
                        yown.at[j],
                        ycol.at[k - 1, j, :, own_lanes],
                        col_send[j],
                        col_recv[k - 1][j],
                        k * ns - 1 - t,
                        p,
                    )

        yx[j, z] = yown[j]

    def left_term(j, k, total):
        if j == 0:
            wait(at.at[k, pl.ds(0, (nx - 1) * nz * fw)], a5_recv[k - 1], "a5_%d" % k)
        wait(ycol.at[k - 1, j], col_recv[k - 1][j], "col_%d_%d" % (k, j))
        total[...] -= dot3(ycol[k - 1, j], at[k])

    def older_left_terms(j, total):
        for k in range(RB - 1, 1, -1):
            pl.when(k > i + 1)(functools.partial(left_term, j, k, total))

    def newest_left_term(j, total):
        for k in range(1, RB):
            pl.when(k == i + 1)(functools.partial(left_term, j, k, total))

    def scatter_x(part, arrived, send_sem, recv_sem):
        for d in (2, 1, 3):
            if d < nx:
                to = lax.rem(x + d, nx)
                send(part.at[to], arrived.at[x], send_sem, recv_sem, q, z * nx + to)

    def whole_of(ref, j):
        return ref[j].reshape(nz * fw, ew)

    def exchange(j):
        wpart[j] = dot3(qside[j].reshape(nx * fw, ew), whole_of(yx, j)).reshape(nx, fw, ew)
        dst = wrecv.at[j, x, :, own_lanes]

        @pl.loop(1, ns)
        def _(d):
            q_to = i * ns + lax.rem(s + d, ns)
            for x_to in range(nx):
                send(wpart.at[j, x_to], dst, w_send[j], w_recv[j], q_to, z * nx + x_to)

        for d in (2, 1, 3):
            if d < nx:
                to = lax.rem(x + d, nx)
                send(wpart.at[j, to], dst, w_send[j], w_recv[j], q, z * nx + to)
        keep(wpart.at[j, x], dst, w_recv[j])

    def last_product(j):
        wait(wrecv.at[j], w_recv[j], "wx_%d" % j)
        out[j] = dot3(jnp.sum(wrecv[j], axis=0), bases[...], ROW_BY_ROW)

    def pair_at(l, j):
        return j * (j - 1) // 2 + l

    def pass_pairs(j):
        for l in range(j):
            n = pair_at(l, j)

            @pl.when(core == (nq - 1 - n) % 2)
            def _(n=n):
                wait(lhs.at[n], b3_recv[n], "b3_%d" % n)
                send(lhs.at[n], lhs.at[n], b3_pass[n], b3_recv[n], partner, p)

        for l in range(j):
            n = pair_at(l, j)

            @pl.when(core != (nq - 1 - n) % 2)
            def _(n=n):
                wait(lhs.at[n], b3_recv[n], "b3_%d" % n)

    def right_term(l, j):
        return dot3(lhs[pair_at(l, j)].reshape(nx * fw, ew), whole_of(yx, l))

    def start_rows():
        wait(crecv.at[blocks[0]], c3_recv[0], "c3_0")
        acc[...] = jnp.sum(crecv[0], axis=0)

    start_rows()
    older_left_terms(0, acc)
    newest_left_term(0, acc)
    finish(0)

    @pl.when(top)
    def _():
        send_b1(1, own_pair[1])

    @pl.when(late_pair)
    def _():
        send_b1(0, own_pair[1])

    send_c3(1)

    @pl.when(top)
    def _():
        send_b3(0, own_pair[0])

    for j in range(1, FIRST):
        pend[j] = jnp.sum(crecv[j], axis=0)

    for j in range(CB):
        last = j + 1 == CB
        if j == 1:
            pl.when(top)(functools.partial(send_b2, 1))
        if j == 2:
            pl.when(top)(functools.partial(send_b3, 1, own_pair[1]))
        if not last:
            pass_pairs(j + 1)
            psum[...] = jnp.zeros_like(psum)
            for l in range(j):
                psum[...] += right_term(l, j + 1)
            if j + 1 != FIRST:
                older_left_terms(j + 1, pend.at[j + 1])
        if j >= 1:
            exchange(j - 1)
        if j >= 2:
            last_product(j - 2)

        if j == 1:
            pl.when(late_pair)(functools.partial(send_b2, 0))
        if j == 2:
            pl.when(late_pair)(functools.partial(send_b3, 0, own_pair[1]))

        wait(yx.at[j, pl.ds(0, nz - 1)], z_recv[j], "z_%d" % j)
        if not last:
            xpart[j + 1] = (psum[...] + right_term(j, j + 1)).reshape(nx, fw, ew)
            scatter_x(xpart.at[j + 1], brecv.at[j + 1], x_send[j + 1], x_recv[j + 1])
            brecv[j + 1, x] = xpart[j + 1, x]
            if j + 1 == FIRST:
                wait(crecv.at[blocks[1]], c3_recv[1], "c3_1")
                for later in range(FIRST, CB):
                    pend[later] = jnp.sum(crecv[later], axis=0)
                older_left_terms(j + 1, pend.at[j + 1])
            newest_left_term(j + 1, pend.at[j + 1])
            wait(brecv.at[j + 1, pl.ds(0, nx - 1)], x_recv[j + 1], "x_%d" % (j + 1))
            acc[...] = pend[j + 1] - jnp.sum(brecv[j + 1], axis=0)
            finish(j + 1)

    exchange(CB - 1)
    last_product(CB - 2)
    last_product(CB - 1)

    for n in range(PAIRS):

        @pl.when(core == (nq - 1 - n) % 2)
        def _(n=n):
            wait(lhs.at[n], b3_pass[n])

    for c in range(2):
        wait(urecv.at[pl.ds(0, ns - 1), chunks[c]], c1_send[c])
        wait(ux.at[blocks[c], pl.ds(0, nx - 1)], c2_send[c])
        wait(qside.at[blocks[c], pl.ds(0, nx - 1)], q2_send[c])
        wait(crecv.at[blocks[c], pl.ds(0, nz - 1)], c3_send[c])
    for j in range(CB):
        wait(yx.at[j, pl.ds(0, nz - 1)], z_send[j])
        wait(at.at[0, pl.ds(0, (nx * ns - 1) * fw)], w_send[j])
        if j > 0:
            wait(brecv.at[j, pl.ds(0, nx - 1)], x_send[j])
        for k in range(1, RB):

            @pl.when(i == k)
            def _(k=k):
                wait(at.at[0, pl.ds(0, fw * k * ns)], col_send[j])

    for k in range(1, RB):

        @pl.when(k > i)
        def _(k=k):
            wait(at.at[k, pl.ds(0, (nz - 1) * fw)], a4_send[k - 1])
            wait(at.at[k, pl.ds(0, (nx - 1) * nz * fw)], a5_send[k - 1])

        @pl.when(jnp.logical_and(i == k, q == holder))
        def _(k=k):
            wait(at.at[pl.ds(0, k * ns * cww // (2 * ew))], a2_send)

    @pl.when(has_coupling)
    def _():
        wait(hrecv.at[pl.ds(0, ns - 1)], a1_send)
        wait(gpart.at[pl.ds(0, bs - fw)], a3_send)

        @pl.when(core == holder % 2)
        def _():
            wait(pk, a2_pass)

    def end_pair(r):
        wait(bx.at[r, pl.ds(0, (nx - 1) * fw)], b1_send[r])
        wait(qx.at[r, pl.ds(0, (nx - 1) * fw)], q1_send[r])
        wait(ql.at[r, pl.ds(0, bs - fw)], l1_send[r])
        wait(trecv.at[r, pl.ds(0, nz - 1)], b2_send[r])
        wait(at.at[0, pl.ds(0, (nq // 2 - 1) * nx * fw)], b3_send[r])

    @pl.when(top)
    def _():
        end_pair(0)
        end_pair(1)

    pl.when(late_pair)(functools.partial(end_pair, 0))


def shards(np_, nq, right_side, coupling, row_bases, row_values, column_bases, column_values, column_coupling):
    ns = nq // RB
    fw, ew = right_side.shape[1], right_side.shape[2]
    cww = coupling.shape[1]
    bs = row_bases.shape[1]
    nx = bs // ew
    nz = np_ // nx
    nw = bs // cww
    vmem = pl.BlockSpec(memory_space=pltpu.VMEM)
    scratch = (
        (ns, CB * fw, ew),
        (ns, CB * fw, ew),
        (CB, nx, fw, ew),
        (CB, fw, ew),
        (CB, nx, fw, ew),
        (CB, nz, fw, ew),
        (CB, nz, fw, ew),
        (ns, cww, ew),
        (ns, cww, ew),
        (cww, bs),
        (bs, ew),
        (RB - 1, nw, fw, ew),
        (RB - 1, fw, ew),
        (RB, bs, ew),
        (2, nx * fw, bs),
        (2, nx * fw, bs),
        (2, bs, ew),
        (2, nx, nz, fw, ew),
        (2, nz, nx, fw, ew),
        (2, nx, fw, ew),
        (PAIRS, nx, fw, ew),
        (CB, fw, ew),
        (CB, nz, fw, ew),
        (CB, nx, fw, ew),
        (CB, nx, fw, ew),
        (CB, nx, fw, ew),
        (CB, nx, fw, bs),
        (RB - 1, CB, fw, bs),
        (CB, fw, ew),
        (nx * fw, ew),
        (CB, fw, ew),
        (fw, ew),
    )
    return pl.pallas_call(
        functools.partial(kernel, np_, nq),
        out_shape=jax.ShapeDtypeStruct((CB, fw, ew), F32),
        in_specs=[vmem] * 7,
        out_specs=vmem,
        scratch_shapes=[pltpu.VMEM(shape, F32) for shape in scratch]
        + [pltpu.SemaphoreType.DMA((160,))],
        compiler_params=pltpu.CompilerParams(collective_id=0, has_side_effects=True),
    )(
        right_side,
        coupling.T,
        row_bases,
        row_values,
        column_bases,
        column_values,
        column_coupling,
    )


def solution(mesh):
    placed = (
        P(None, "pcol", "prow"),
        P("prow", "pcol"),
        P("prow", None),
        P(),
        P(None, "pcol", None),
        P(),
        P(None, "pcol", None),
    )
    body = functools.partial(shards, mesh.shape["pcol"], mesh.shape["prow"])
    return jax.shard_map(
        body, mesh=mesh, in_specs=placed, out_specs=P(None, "pcol", "prow"), check_vma=False
    )
```

```python
import functools

import jax
import jax.numpy as jnp
from jax import lax
from jax.experimental import pallas as pl
from jax.experimental.pallas import tpu as pltpu
from jax.sharding import PartitionSpec as P

RB = 4
CB = 6
PAIRS = CB * (CB - 1) // 2
FIRST = 2
MESH = pl.DeviceIdType.MESH
F32 = jnp.float32
BF16 = jnp.bfloat16
ROW_BY_COL = ((1,), (0,))
COL_BY_COL = ((0,), (0,))
ROW_BY_ROW = ((1,), (1,))


def halves(value):
    high = value.astype(BF16)
    low = (value - high.astype(F32)).astype(BF16)
    return high, low


def dot_of(left, right, dims):
    return lax.dot_general(left, right, (dims, ((), ())), preferred_element_type=F32)


def dot_split(left, right, dims):
    (left_high, left_low), (right_high, right_low) = left, right
    small = dot_of(left_low, right_high, dims) + dot_of(left_high, right_low, dims)
    return dot_of(left_high, right_high, dims) + small


def dot3(left, right, dims=ROW_BY_COL):
    return dot_split(halves(left), halves(right), dims)


def kernel(np_, nq, *refs):
    (rhs, coupling, bases, row_values, colbases, col_values, colcoup, out, *rest) = refs
    (upart, urecv, ux, uown, qside, vpart, crecv) = rest[:7]
    (hpart, hrecv, pk, gpart, grecv, apiece, at) = rest[7:14]
    (bx, qx, ql, tpart, trecv, tpiece, lhs) = rest[14:21]
    (yown, yx, xpart, brecv, wpart, wrecv) = rest[21:27]
    (ycol, pend, psum, den, acc, sems) = rest[27:]
    fw, ew = rhs.shape[1], rhs.shape[2]
    cww = coupling.shape[0]
    bs = fw * np_
    ns = nq // RB
    nx = bs // ew
    nz = np_ // nx
    nw = bs // cww
    per_row = ew // cww
    q = lax.axis_index("prow")
    p = lax.axis_index("pcol")
    i, s = q // ns, q % ns
    z, x = p // nx, p % nx
    core = q % 2
    partner = q + 1 - 2 * core
    k_own, w_own = p // nw, p % nw
    has_coupling = k_own > i
    top = i == RB - 1
    holder = p // per_row
    late_pair = jnp.logical_and(q > ns, q < nq - ns)

    used = [0]

    def new_sem(count=1):
        at_sem = used[0]
        used[0] += count
        return [sems.at[at_sem + n] for n in range(count)]

    z_send, z_recv, x_send, x_recv = new_sem(CB), new_sem(CB), new_sem(CB), new_sem(CB)
    w_send, w_recv, col_send = new_sem(CB), new_sem(CB), new_sem(CB)
    col_recv = [new_sem(CB) for _ in range(RB - 1)]
    c1_send, c1_recv, c2_send, c2_recv = new_sem(2), new_sem(2), new_sem(2), new_sem(2)
    c3_send, c3_recv, q2_send, q2_recv = new_sem(2), new_sem(2), new_sem(2), new_sem(2)
    a1_send, a1_recv, a2_send, a2_recv, a2_pass, a3_send = new_sem(6)
    a3_recv, a4_send, a4_recv = new_sem(RB - 1), new_sem(RB - 1), new_sem(RB - 1)
    a5_send, a5_recv = new_sem(RB - 1), new_sem(RB - 1)
    b1_send, b1_recv, q1_send, q1_recv = new_sem(2), new_sem(2), new_sem(2), new_sem(2)
    l1_send, l1_recv, b2_send, b2_recv = new_sem(2), new_sem(2), new_sem(2), new_sem(2)
    b3_send = new_sem(2)
    b3_pass = new_sem(PAIRS)
    b3_base = used[0]
    b3_recv = new_sem(PAIRS)

    def send(src, dst, send_sem, recv_sem, q_to, p_to):
        pltpu.make_async_remote_copy(
            src_ref=src,
            dst_ref=dst,
            send_sem=send_sem,
            recv_sem=recv_sem,
            device_id=(q_to, p_to),
            device_id_type=MESH,
        ).start()

    def keep(src, dst, recv_sem):
        pltpu.make_async_copy(src, dst, recv_sem).start()

    def send_or_keep(here, src, dst, send_sem, recv_sem, q_to, p_to):
        @pl.when(here)
        def _():
            keep(src, dst, recv_sem)

        @pl.when(jnp.logical_not(here))
        def _():
            send(src, dst, send_sem, recv_sem, q_to, p_to)

    def wait(ref, sem, name="w"):
        pltpu.make_async_copy(ref, ref, sem).wait()

    def rows_of(n, size):
        return pl.ds(pl.multiple_of(n * size, size), size)

    def to_columns(body):
        for start, stop in ((np_ // 2, np_), (1, np_ // 2)):

            @pl.loop(start, stop)
            def _(d):
                body(lax.rem(p + d, np_))

    def pair_of(n):
        j_own = 1
        for first in range(2, CB):
            j_own = j_own + (n >= first * (first - 1) // 2).astype(jnp.int32)
        return n - j_own * (j_own - 1) // 2, j_own

    own_pair = (nq - 1 - q, nq + ns - 1 - q)

    barrier = pltpu.get_barrier_semaphore()

    def greet(to):
        pl.semaphore_signal(barrier, inc=1, device_id=(q, to), device_id_type=MESH)

    to_columns(greet)

    @pl.loop(1, nq)
    def _(d):
        pl.semaphore_signal(
            barrier, inc=1, device_id=(lax.rem(q + d, nq), p), device_id_type=MESH
        )

    @pl.loop(1, ns)
    def _(d):
        q_to = i * ns + lax.rem(s + d, ns)
        for x_off in range(1, nx):
            to = z * nx + lax.rem(x + x_off, nx)
            pl.semaphore_signal(barrier, inc=1, device_id=(q_to, to), device_id_type=MESH)

    bases_split = halves(bases[...])
    inner = dot_split(halves(coupling[...]), bases_split, ROW_BY_COL)
    stacked = rhs[...].reshape(CB * fw, ew)
    first = dot_split(halves(stacked), bases_split, ROW_BY_COL)
    for n in range(ns):
        upart[n] = first[:, n * ew : (n + 1) * ew]
        hpart[n] = inner[:, n * ew : (n + 1) * ew]
    own_lanes = rows_of(s, ew)
    values = row_values[:, own_lanes]
    own_value = lax.broadcasted_iota(jnp.int32, values.shape, 0) == i
    eigen = jnp.sum(jnp.where(own_value, values, 0.0), axis=0, keepdims=True)
    lanes = lax.broadcasted_iota(jnp.int32, (fw, ew), 1)
    chosen = lanes == z * fw + lax.broadcasted_iota(jnp.int32, (fw, ew), 0)
    for j in range(CB):
        shifts = col_values[pl.ds(j, 1), rows_of(x, ew)]
        shift = jnp.sum(jnp.where(chosen, shifts, 0.0), axis=1, keepdims=True)
        den[j] = shift + eigen

    pl.semaphore_wait(barrier, np_ + nq - 2 + (ns - 1) * (nx - 1))

    chunks = (pl.ds(0, FIRST * fw), pl.ds(FIRST * fw, (CB - FIRST) * fw))
    blocks = (pl.ds(0, FIRST), pl.ds(FIRST, CB - FIRST))

    def send_c1(c):
        @pl.loop(0, ns)
        def _(t):
            src, dst = upart.at[t, chunks[c]], urecv.at[s, chunks[c]]
            send_or_keep(t == s, src, dst, c1_send[c], c1_recv[c], i * ns + t, p)

    def send_q2(c):
        @pl.loop(0, nx)
        def _(t):
            src, dst = colbases.at[blocks[c], :, rows_of(t, ew)], qside.at[blocks[c], x]
            send_or_keep(t == x, src, dst, q2_send[c], q2_recv[c], q, z * nx + t)

    def send_c2(c):
        wait(urecv.at[:, chunks[c]], c1_recv[c], "c1_%d" % c)
        count = (FIRST, CB - FIRST)[c]
        summed = jnp.sum(urecv[:, chunks[c]], axis=0)
        uown[blocks[c]] = summed.reshape(count, fw, ew)

        @pl.loop(0, nx)
        def _(t):
            src, dst = uown.at[blocks[c]], ux.at[blocks[c], x]
            send_or_keep(t == x, src, dst, c2_send[c], c2_recv[c], q, z * nx + t)

    def send_c3(c):
        wait(ux.at[blocks[c]], c2_recv[c], "c2_%d" % c)
        wait(qside.at[blocks[c]], q2_recv[c], "q2_%d" % c)
        for j in (range(FIRST), range(FIRST, CB))[c]:
            left = qside[j].reshape(nx * fw, ew)
            right = ux[j].reshape(nx * fw, ew)
            vpart[j] = dot3(left, right, COL_BY_COL).reshape(nz, fw, ew)

        @pl.loop(0, nz)
        def _(t):
            src, dst = vpart.at[blocks[c], t], crecv.at[blocks[c], z]
            send_or_keep(t == z, src, dst, c3_send[c], c3_recv[c], q, t * nx + x)

    def send_b1(r, n):
        l_own, j_own = pair_of(n)

        @pl.loop(0, nx)
        def _(t):
            src_b = colcoup.at[j_own, :, rows_of(l_own, bs)]
            src_q = colbases.at[j_own]
            dst_b, dst_q = bx.at[r, rows_of(x, fw)], qx.at[r, rows_of(x, fw)]
            to = z * nx + t
            send_or_keep(t == x, src_b, dst_b, b1_send[r], b1_recv[r], q, to)
            send_or_keep(t == x, src_q, dst_q, q1_send[r], q1_recv[r], q, to)

        dst = ql.at[r, rows_of(p, fw)]
        keep(colbases.at[l_own, :, rows_of(x, ew)], dst, l1_recv[r])

        def one(to):
            src = colbases.at[l_own, :, rows_of(lax.rem(to, nx), ew)]
            send(src, dst, l1_send[r], l1_recv[r], q, to)

        to_columns(one)

    def send_b2(r):
        wait(bx.at[r], b1_recv[r], "bx%d" % r)
        wait(qx.at[r], q1_recv[r], "qx%d" % r)
        wait(ql.at[r], l1_recv[r], "ql%d" % r)
        mixed = dot3(bx[r], ql[r])
        tpart[r] = dot3(qx[r], mixed, COL_BY_COL).reshape(nx, nz, fw, ew)

        @pl.loop(0, nz)
        def _(t):
            src, dst = tpart.at[r, :, t], trecv.at[r, z]
            send_or_keep(t == z, src, dst, b2_send[r], b2_recv[r], q, t * nx + x)

    def send_b3(r, n):
        wait(trecv.at[r], b2_recv[r], "b2%d" % r)
        tpiece[r] = jnp.sum(trecv[r], axis=0)
        dst, recv_sem = lhs.at[n], sems.at[b3_base + n]

        @pl.loop(0, nq // 2)
        def _(t):
            q_to = nq - 2 - 2 * t + core
            send_or_keep(q_to == q, tpiece.at[r], dst, b3_send[r], recv_sem, q_to, p)

    @pl.when(q == holder)
    def _():
        @pl.loop(0, i * ns // 2)
        def _(t):
            src = bases.at[rows_of(lax.rem(p, per_row), cww)]
            send(src, pk, a2_send, a2_recv, i * ns - 2 - 2 * t + core, p)

    @pl.when(has_coupling)
    def _():
        @pl.loop(0, ns)
        def _(t):
            send_or_keep(t == s, hpart.at[t], hrecv.at[s], a1_send, a1_recv, i * ns + t, p)

    send_c1(0)
    send_q2(0)

    @pl.when(top)
    def _():
        send_b1(0, own_pair[0])

    send_c1(1)
    send_q2(1)

    @pl.when(has_coupling)
    def _():
        wait(hrecv, a1_recv, "a1")
        wait(pk, a2_recv, "a2")

        @pl.when(core == holder % 2)
        def _():
            send(pk, pk, a2_pass, a2_recv, partner, p)

        gpart[...] = dot3(pk[...], jnp.sum(hrecv[...], axis=0), COL_BY_COL)
        for k in range(1, RB):

            @pl.when(k_own == k)
            def _(k=k):
                dst = grecv.at[k - 1, w_own]
                keep(gpart.at[rows_of(x * nz + z, fw)], dst, a3_recv[k - 1])

                def one(to):
                    order = lax.rem(to, nx) * nz + to // nx
                    send(gpart.at[rows_of(order, fw)], dst, a3_send, a3_recv[k - 1], q, to)

                to_columns(one)

    send_c2(0)
    send_c3(0)

    @pl.when(top)
    def _():
        send_b2(0)

    send_c2(1)

    for k in range(RB - 1, 0, -1):

        @pl.when(k > i)
        def _(k=k):
            wait(grecv.at[k - 1], a3_recv[k - 1], "a3_%d" % k)
            apiece[k - 1] = jnp.sum(grecv[k - 1], axis=0)
            dst = at.at[k, rows_of(x * nz + z, fw)]
            keep(apiece.at[k - 1], dst, a4_recv[k - 1])
            for d in (4, 3, 5, 2, 6, 1, 7):
                if d < nz:
                    to = lax.rem(z + d, nz) * nx + x
                    send(apiece.at[k - 1], dst, a4_send[k - 1], a4_recv[k - 1], q, to)

    for k in range(RB - 1, 0, -1):

        @pl.when(k > i)
        def _(k=k):
            half = at.at[k, rows_of(x, nz * fw)]
            wait(half, a4_recv[k - 1], "a4_%d" % k)
            for d in (2, 1, 3):
                if d < nx:
                    to = z * nx + lax.rem(x + d, nx)
                    send(half, half, a5_send[k - 1], a5_recv[k - 1], q, to)

    def finish(j):
        yown[j] = acc[...] / den[j]
        for d in (4, 3, 5, 2, 6, 1, 7):
            if d < nz:
                to = lax.rem(z + d, nz) * nx + x
                send(yown.at[j], yx.at[j, z], z_send[j], z_recv[j], q, to)
        for k in range(1, RB):

            @pl.when(i == k)
            def _(k=k):
                @pl.loop(0, k * ns)
                def _(t):
                    send(
                        yown.at[j],
                        ycol.at[k - 1, j, :, own_lanes],
                        col_send[j],
                        col_recv[k - 1][j],
                        k * ns - 1 - t,
                        p,
                    )

        yx[j, z] = yown[j]

    def left_term(j, k, total):
        if j == 0:
            wait(at.at[k, pl.ds(0, (nx - 1) * nz * fw)], a5_recv[k - 1], "a5_%d" % k)
        wait(ycol.at[k - 1, j], col_recv[k - 1][j], "col_%d_%d" % (k, j))
        total[...] -= dot3(ycol[k - 1, j], at[k])

    def older_left_terms(j, total):
        for k in range(RB - 1, 1, -1):
            pl.when(k > i + 1)(functools.partial(left_term, j, k, total))

    def newest_left_term(j, total):
        for k in range(1, RB):
            pl.when(k == i + 1)(functools.partial(left_term, j, k, total))

    def scatter_x(part, arrived, send_sem, recv_sem):
        for d in (2, 1, 3):
            if d < nx:
                to = lax.rem(x + d, nx)
                send(part.at[to], arrived.at[x], send_sem, recv_sem, q, z * nx + to)

    def whole_of(ref, j):
        return ref[j].reshape(nz * fw, ew)

    def exchange(j):
        wpart[j] = dot3(qside[j].reshape(nx * fw, ew), whole_of(yx, j)).reshape(nx, fw, ew)
        dst = wrecv.at[j, x, :, own_lanes]

        @pl.loop(1, ns)
        def _(d):
            q_to = i * ns + lax.rem(s + d, ns)
            for x_to in range(nx):
                send(wpart.at[j, x_to], dst, w_send[j], w_recv[j], q_to, z * nx + x_to)

        for d in (2, 1, 3):
            if d < nx:
                to = lax.rem(x + d, nx)
                send(wpart.at[j, to], dst, w_send[j], w_recv[j], q, z * nx + to)
        keep(wpart.at[j, x], dst, w_recv[j])

    def last_product(j):
        wait(wrecv.at[j], w_recv[j], "wx_%d" % j)
        out[j] = dot3(jnp.sum(wrecv[j], axis=0), bases[...], ROW_BY_ROW)

    def pair_at(l, j):
        return j * (j - 1) // 2 + l

    def pass_pairs(j):
        for l in range(j):
            n = pair_at(l, j)

            @pl.when(core == (nq - 1 - n) % 2)
            def _(n=n):
                wait(lhs.at[n], b3_recv[n], "b3_%d" % n)
                send(lhs.at[n], lhs.at[n], b3_pass[n], b3_recv[n], partner, p)

        for l in range(j):
            n = pair_at(l, j)

            @pl.when(core != (nq - 1 - n) % 2)
            def _(n=n):
                wait(lhs.at[n], b3_recv[n], "b3_%d" % n)

    def right_term(l, j):
        return dot3(lhs[pair_at(l, j)].reshape(nx * fw, ew), whole_of(yx, l))

    def start_rows():
        wait(crecv.at[blocks[0]], c3_recv[0], "c3_0")
        acc[...] = jnp.sum(crecv[0], axis=0)

    start_rows()
    older_left_terms(0, acc)
    newest_left_term(0, acc)
    finish(0)

    @pl.when(top)
    def _():
        send_b1(1, own_pair[1])

    send_c3(1)

    @pl.when(top)
    def _():
        send_b3(0, own_pair[0])

    @pl.when(late_pair)
    def _():
        send_b1(0, own_pair[1])

    for j in range(1, FIRST):
        pend[j] = jnp.sum(crecv[j], axis=0)

    for j in range(CB):
        last = j + 1 == CB
        if j == 1:
            pl.when(top)(functools.partial(send_b2, 1))
        if j == 2:
            pl.when(top)(functools.partial(send_b3, 1, own_pair[1]))
        if not last:
            pass_pairs(j + 1)
            psum[...] = jnp.zeros_like(psum)
            for l in range(j):
                psum[...] += right_term(l, j + 1)
            if j + 1 != FIRST:
                older_left_terms(j + 1, pend.at[j + 1])
        if last:
            exchange(j - 1)
        if j >= 2:
            last_product(j - 2)

        wait(yx.at[j, pl.ds(0, nz - 1)], z_recv[j], "z_%d" % j)
        if not last:
            xpart[j + 1] = (psum[...] + right_term(j, j + 1)).reshape(nx, fw, ew)
            scatter_x(xpart.at[j + 1], brecv.at[j + 1], x_send[j + 1], x_recv[j + 1])
            brecv[j + 1, x] = xpart[j + 1, x]
            if j >= 1:
                exchange(j - 1)
            if j == 1:
                pl.when(late_pair)(functools.partial(send_b2, 0))
            if j == 2:
                pl.when(late_pair)(functools.partial(send_b3, 0, own_pair[1]))
            if j + 1 == FIRST:
                wait(crecv.at[blocks[1]], c3_recv[1], "c3_1")
                for later in range(FIRST, CB):
                    pend[later] = jnp.sum(crecv[later], axis=0)
                older_left_terms(j + 1, pend.at[j + 1])
            newest_left_term(j + 1, pend.at[j + 1])
            wait(brecv.at[j + 1, pl.ds(0, nx - 1)], x_recv[j + 1], "x_%d" % (j + 1))
            acc[...] = pend[j + 1] - jnp.sum(brecv[j + 1], axis=0)
            finish(j + 1)

    exchange(CB - 1)
    last_product(CB - 2)
    last_product(CB - 1)

    for n in range(PAIRS):

        @pl.when(core == (nq - 1 - n) % 2)
        def _(n=n):
            wait(lhs.at[n], b3_pass[n])

    for c in range(2):
        wait(urecv.at[pl.ds(0, ns - 1), chunks[c]], c1_send[c])
        wait(ux.at[blocks[c], pl.ds(0, nx - 1)], c2_send[c])
        wait(qside.at[blocks[c], pl.ds(0, nx - 1)], q2_send[c])
        wait(crecv.at[blocks[c], pl.ds(0, nz - 1)], c3_send[c])
    for j in range(CB):
        wait(yx.at[j, pl.ds(0, nz - 1)], z_send[j])
        wait(at.at[0, pl.ds(0, (nx * ns - 1) * fw)], w_send[j])
        if j > 0:
            wait(brecv.at[j, pl.ds(0, nx - 1)], x_send[j])
        for k in range(1, RB):

            @pl.when(i == k)
            def _(k=k):
                wait(at.at[0, pl.ds(0, fw * k * ns)], col_send[j])

    for k in range(1, RB):

        @pl.when(k > i)
        def _(k=k):
            wait(at.at[k, pl.ds(0, (nz - 1) * fw)], a4_send[k - 1])
            wait(at.at[k, pl.ds(0, (nx - 1) * nz * fw)], a5_send[k - 1])

        @pl.when(jnp.logical_and(i == k, q == holder))
        def _(k=k):
            wait(at.at[pl.ds(0, k * ns * cww // (2 * ew))], a2_send)

    @pl.when(has_coupling)
    def _():
        wait(hrecv.at[pl.ds(0, ns - 1)], a1_send)
        wait(gpart.at[pl.ds(0, bs - fw)], a3_send)

        @pl.when(core == holder % 2)
        def _():
            wait(pk, a2_pass)

    def end_pair(r):
        wait(bx.at[r, pl.ds(0, (nx - 1) * fw)], b1_send[r])
        wait(qx.at[r, pl.ds(0, (nx - 1) * fw)], q1_send[r])
        wait(ql.at[r, pl.ds(0, bs - fw)], l1_send[r])
        wait(trecv.at[r, pl.ds(0, nz - 1)], b2_send[r])
        wait(at.at[0, pl.ds(0, (nq // 2 - 1) * nx * fw)], b3_send[r])

    @pl.when(top)
    def _():
        end_pair(0)
        end_pair(1)

    pl.when(late_pair)(functools.partial(end_pair, 0))


def shards(np_, nq, right_side, coupling, row_bases, row_values, column_bases, column_values, column_coupling):
    ns = nq // RB
    fw, ew = right_side.shape[1], right_side.shape[2]
    cww = coupling.shape[1]
    bs = row_bases.shape[1]
    nx = bs // ew
    nz = np_ // nx
    nw = bs // cww
    vmem = pl.BlockSpec(memory_space=pltpu.VMEM)
    scratch = (
        (ns, CB * fw, ew),
        (ns, CB * fw, ew),
        (CB, nx, fw, ew),
        (CB, fw, ew),
        (CB, nx, fw, ew),
        (CB, nz, fw, ew),
        (CB, nz, fw, ew),
        (ns, cww, ew),
        (ns, cww, ew),
        (cww, bs),
        (bs, ew),
        (RB - 1, nw, fw, ew),
        (RB - 1, fw, ew),
        (RB, bs, ew),
        (2, nx * fw, bs),
        (2, nx * fw, bs),
        (2, bs, ew),
        (2, nx, nz, fw, ew),
        (2, nz, nx, fw, ew),
        (2, nx, fw, ew),
        (PAIRS, nx, fw, ew),
        (CB, fw, ew),
        (CB, nz, fw, ew),
        (CB, nx, fw, ew),
        (CB, nx, fw, ew),
        (CB, nx, fw, ew),
        (CB, nx, fw, bs),
        (RB - 1, CB, fw, bs),
        (CB, fw, ew),
        (nx * fw, ew),
        (CB, fw, ew),
        (fw, ew),
    )
    return pl.pallas_call(
        functools.partial(kernel, np_, nq),
        out_shape=jax.ShapeDtypeStruct((CB, fw, ew), F32),
        in_specs=[vmem] * 7,
        out_specs=vmem,
        scratch_shapes=[pltpu.VMEM(shape, F32) for shape in scratch]
        + [pltpu.SemaphoreType.DMA((160,))],
        compiler_params=pltpu.CompilerParams(collective_id=0, has_side_effects=True),
    )(
        right_side,
        coupling.T,
        row_bases,
        row_values,
        column_bases,
        column_values,
        column_coupling,
    )


def solution(mesh):
    placed = (
        P(None, "pcol", "prow"),
        P("prow", "pcol"),
        P("prow", None),
        P(),
        P(None, "pcol", None),
        P(),
        P(None, "pcol", None),
    )
    body = functools.partial(shards, mesh.shape["pcol"], mesh.shape["prow"])
    return jax.shard_map(
        body, mesh=mesh, in_specs=placed, out_specs=P(None, "pcol", "prow"), check_vma=False
    )
```
